32 devices in a mesh: cfg: 2 (over y), space: 4 (over z), tm: 4 (over x, core).
Axes of the slice: x: 2, y: 2, z: 4, core: 2. Of those that a mesh axis runs over, the one named last changes fastest.
Arguments:
- eigenvectors: bfloat16 [8, 2, 3, 3072, 384], P(('cfg', 'tm'), None, None, 'space'), parts along dimension 0, may hold values from -6 to 6
- perambulator: bfloat16 [8, 2, 1536, 1536], P(('cfg', 'tm'), None, None, 'space'), parts along dimension 0, may hold values from -0.3125 to 0.3125
- momenta: int32 [2, 3], replicated, may hold values from -2 to 2
- ratios: int32 [2, 2], replicated, may hold values from 1 to 3
- source_slice: int32 [1], replicated, may hold values from 0 to 255
Outputs:
- meson_blocks: float32 [8, 2, 1536, 1536], P(('cfg', 'tm'), None, 'space'), parts along dimension 0
The draws below stay inside these ranges and needn't reach their ends.
There are 2 independent parts, one for each index of `cfg`. The reference program is written for one: setup_inputs(seed, part) draws one part's arguments, and reference() takes and returns one part's arrays. A program takes and returns all parts, laid end to end along the dimension named above; an argument that names none is the same for every part. Nothing has to cross between parts.
Inputs may be any that keep to these rules, and one draw needn't show every extreme that they name: `momenta`: row k is momentum k in units of 2 pi / 64. `ratios`: row k holds the numerator (column 0) and the denominator (column 1) of momentum k's coefficient.
All inputs are finite; a program needn't handle non-finite values.
Results may differ from the reference program's by a relative error of at most 0.0063.
Values may be sent and summed in bfloat16 or wider, within the bound.
A program may use at most 64 MiB of HBM per device.

```python
import math
import jax
import jax.numpy as jnp
from jax import lax

NVEC = 384
LSIDE = 64
NT = 4
SITES = 3072
ORDER = 1536


def plant(array, stream_key, low, largest):
    shape = array.shape
    place = [jax.random.randint(jax.random.fold_in(stream_key, axis), (), 0, shape[axis]) for axis in range(len(shape))]
    array = array.at[tuple(place)].set(low)
    longest = shape.index(max(shape))
    place[longest] = (place[longest] + 1) % shape[longest]
    return array.at[tuple(place)].set(largest)


def shard_levels(rng, dims, split, least, top_value):
    factor_of = 1.0
    for dim, shards_of in split:
        steps = jax.random.uniform(jax.random.fold_in(jax.random.fold_in(rng, 6), dim), (shards_of,), jnp.float32, least / len(split), top_value / len(split))
        factor_of = factor_of * jnp.repeat(jnp.exp(steps), dims[dim] // shards_of).reshape((-1,) + (1,) * (len(dims) - 1 - dim))
    return factor_of


def normal_values(key, dims, deviation, limit, cuts=(), kind=jnp.bfloat16):
    values = jax.random.normal(key, dims, jnp.float32) * deviation
    if len(cuts) > 0:
        values = shard_levels(key, dims, cuts, -0.22, 0.18) * values
    return jnp.clip(values, min=-limit, max=limit).astype(kind)


def setup_inputs(seed: int = 0, part: int = 0) -> dict:
    key_list = jax.random.split(jax.random.key(seed), 6)
    part_splits = jax.random.split(jax.random.fold_in(key_list[5], part), 6)
    return {
        "eigenvectors": normal_values(part_splits[0], (NT, 2, 3, SITES, NVEC), 1.0, 6.0, ((0, 4), (3, 4))),
        "perambulator": normal_values(part_splits[1], (NT, 2, ORDER, ORDER), NVEC ** -0.5, 0.3125, ((0, 4), (3, 4))),
        "momenta": plant(jax.random.randint(key_list[2], (2, 3), -2, 3), jax.random.fold_in(key_list[2], 1), -2, 2).astype(jnp.int32),
        "ratios": plant(jax.random.randint(key_list[3], (2, 2), 1, 4), jax.random.fold_in(key_list[3], 1), 1, 3).astype(jnp.int32),
        "source_slice": jax.random.randint(key_list[4], (1,), 0, 64 * NT).astype(jnp.int32),
    }


def site_phases(momenta, first_site, site_count):
    site_index = first_site + jnp.arange(site_count, dtype=jnp.int32)
    along_x = site_index % LSIDE
    along_y = site_index // LSIDE % LSIDE
    along_z = site_index // (LSIDE * LSIDE)
    turn_count = momenta[:, 0:1] * along_x[None, :] + momenta[:, 1:2] * along_y[None, :] + momenta[:, 2:3] * along_z[None, :]
    phase_angle = (turn_count % LSIDE).astype(jnp.float32) * (2.0 * math.pi / LSIDE)
    return (jnp.cos(phase_angle), jnp.sin(phase_angle))

def split_elementals(product, vector_count):
    lead_shape = product.shape[:-2]
    product_grid = product.reshape(lead_shape + (2, vector_count, 2, 2, vector_count))
    real_part = product_grid[..., 0, :, :, 0, :] + product_grid[..., 1, :, :, 1, :]
    imaginary = product_grid[..., 0, :, :, 1, :] - product_grid[..., 1, :, :, 0, :]
    stacked = jnp.stack([real_part, imaginary], axis=-4)
    return jnp.moveaxis(stacked, -2, -4)

def elementals(slab, cosine, sine_part):
    color_count, site_count, vector_count = (slab.shape[1], slab.shape[2], slab.shape[3])
    row_count = color_count * site_count
    real_rows = slab[0].reshape(row_count, vector_count)
    imaginary_rows = slab[1].reshape(row_count, vector_count)
    cos_rows = jnp.broadcast_to(cosine[:, None, :], (2, color_count, site_count)).reshape(2, row_count, 1)
    sin_rows = jnp.broadcast_to(sine_part[:, None, :], (2, color_count, site_count)).reshape(2, row_count, 1)
    phased_real = (cos_rows * real_rows[None] + sin_rows * imaginary_rows[None]).astype(jnp.bfloat16)
    phased_imaginary = (cos_rows * imaginary_rows[None] - sin_rows * real_rows[None]).astype(jnp.bfloat16)
    phased = jnp.concatenate([phased_real, phased_imaginary], axis=2)
    phased = jnp.transpose(phased, (1, 0, 2)).reshape(row_count, 4 * vector_count)
    plain_vectors = jnp.concatenate([real_rows, imaginary_rows], axis=1)
    product = jnp.dot(plain_vectors.T, phased, preferred_element_type=jnp.float32)
    return split_elementals(product, vector_count)

def source_block(chosen):
    real_t = chosen[0].T
    imaginary_t = chosen[1].T
    upper = jnp.concatenate([real_t, -imaginary_t], axis=1)
    lower = jnp.concatenate([imaginary_t, real_t], axis=1)
    return jnp.concatenate([upper, lower], axis=0)

def propagate(sink_matrix, tau):
    vector_count = sink_matrix.shape[1]
    spin_count = tau.shape[1] // vector_count
    column_count = tau.shape[2]
    real_part, imaginary = (sink_matrix[0], sink_matrix[1])
    upper = jnp.concatenate([real_part, -imaginary], axis=1)
    lower = jnp.concatenate([imaginary, real_part], axis=1)
    sink_big = jnp.concatenate([upper, lower], axis=0)
    stacked = jnp.transpose(tau.reshape(2, spin_count, vector_count, column_count), (0, 2, 1, 3))
    stacked = stacked.reshape(2 * vector_count, spin_count * column_count)
    product = jnp.dot(sink_big, stacked, preferred_element_type=jnp.float32)
    product = jnp.transpose(product.reshape(2, vector_count, spin_count, column_count), (0, 2, 1, 3))
    return product.reshape(2, spin_count * vector_count, column_count).astype(jnp.bfloat16)

def attach_source(propagated, source_big):
    vector_count = source_big.shape[0] // 2
    row_count = propagated.shape[1]
    spin_count = propagated.shape[2] // vector_count
    stacked = jnp.concatenate([propagated[0].reshape(row_count, spin_count, vector_count), propagated[1].reshape(row_count, spin_count, vector_count)], axis=2)
    product = jnp.dot(stacked.reshape(row_count * spin_count, 2 * vector_count), source_big, preferred_element_type=jnp.float32)
    product = jnp.transpose(product.reshape(row_count, spin_count, 2, vector_count), (2, 0, 1, 3))
    return product.reshape(2, row_count, spin_count * vector_count)

def reference(eigenvectors, perambulator, momenta, ratios, source_slice):
    cosine, sine_part = site_phases(momenta, 0, SITES)
    normalizer = 1.0 / math.sqrt(3 * SITES * NVEC)
    weights = ratios[:, 0].astype(jnp.float32) / ratios[:, 1].astype(jnp.float32) * normalizer

    def sink_of(slab):
        parts = elementals(slab, cosine, sine_part)
        return lax.optimization_barrier(jnp.sum(weights[:, None, None, None] * parts, axis=0)).astype(jnp.bfloat16)
    sink_matrices = lax.map(sink_of, eigenvectors)
    chosen_index = (source_slice[0] % NT).astype(jnp.int32)
    chosen = lax.dynamic_index_in_dim(sink_matrices, chosen_index, 0, keepdims=False)
    source_big = source_block(chosen)

    def slab_result(paired):
        sink_matrix, tau = paired
        return attach_source(propagate(sink_matrix, tau), source_big)
    return lax.map(slab_result, (sink_matrices, perambulator))
```

```python
import functools
import math

import jax
import jax.numpy as jnp
from jax import lax
from jax.experimental import pallas as pl
from jax.experimental.pallas import tpu as pltpu
from jax.sharding import PartitionSpec as P

MESH = pl.DeviceIdType.MESH

LSIDE = 64

VMEM_BYTES = 67043328


def spread(value, axis, source):
    kept = jnp.where(lax.axis_index(axis) == source, value, 0).astype(value.dtype)
    return lax.psum(kept, axis)


def site_phases(momenta, first_site, site_count):
    site_index = first_site + lax.iota(jnp.int32, site_count)
    along_x = site_index % LSIDE
    along_y = site_index // LSIDE % LSIDE
    along_z = site_index // (LSIDE * LSIDE)
    turn_count = (
        momenta[:, 0:1] * along_x[None, :]
        + momenta[:, 1:2] * along_y[None, :]
        + momenta[:, 2:3] * along_z[None, :]
    )
    phase_angle = (turn_count % LSIDE).astype(jnp.float32) * (2.0 * math.pi / LSIDE)
    return (jnp.cos(phase_angle), jnp.sin(phase_angle))


def split_elementals(product, vector_count):
    lead_shape = product.shape[:-2]
    product_grid = product.reshape(lead_shape + (2, vector_count, 2, 2, vector_count))
    real_part = product_grid[..., 0, :, :, 0, :] + product_grid[..., 1, :, :, 1, :]
    imaginary = product_grid[..., 0, :, :, 1, :] - product_grid[..., 1, :, :, 0, :]
    stacked = jnp.stack([real_part, imaginary], axis=-4)
    return jnp.moveaxis(stacked, -2, -4)


def elementals(vectors, cosine, sine_part):
    slab_count, color_count, site_count, vector_count = (
        vectors.shape[0],
        vectors.shape[2],
        vectors.shape[3],
        vectors.shape[4],
    )
    row_count = color_count * site_count
    real_rows = vectors[:, 0].reshape(slab_count, row_count, vector_count)
    imaginary_rows = vectors[:, 1].reshape(slab_count, row_count, vector_count)
    cos_rows = jnp.broadcast_to(cosine[:, None, :], (2, color_count, site_count)).reshape(
        1, 2, row_count, 1
    )
    sin_rows = jnp.broadcast_to(sine_part[:, None, :], (2, color_count, site_count)).reshape(
        1, 2, row_count, 1
    )
    phased_real = (cos_rows * real_rows[:, None] + sin_rows * imaginary_rows[:, None]).astype(
        jnp.bfloat16
    )
    phased_imaginary = (cos_rows * imaginary_rows[:, None] - sin_rows * real_rows[:, None]).astype(
        jnp.bfloat16
    )
    phased = jnp.concatenate([phased_real, phased_imaginary], axis=3)
    phased = jnp.transpose(phased, (0, 2, 1, 3)).reshape(slab_count, row_count, 4 * vector_count)
    plain_vectors = jnp.concatenate([real_rows, imaginary_rows], axis=2)
    product = lax.dot_general(
        plain_vectors, phased, (((1,), (1,)), ((0,), (0,))), preferred_element_type=jnp.float32
    )
    return split_elementals(product, vector_count)


def source_block(chosen):
    real_t = chosen[0].T
    imaginary_t = chosen[1].T
    upper = jnp.concatenate([real_t, -imaginary_t], axis=1)
    lower = jnp.concatenate([imaginary_t, real_t], axis=1)
    return jnp.concatenate([upper, lower], axis=0)


def propagate(sink_matrix, tau):
    vector_count = sink_matrix.shape[1]
    spin_count = tau.shape[1] // vector_count
    column_count = tau.shape[2]
    real_part, imaginary = (sink_matrix[0], sink_matrix[1])
    upper = jnp.concatenate([real_part, -imaginary], axis=1)
    lower = jnp.concatenate([imaginary, real_part], axis=1)
    sink_big = jnp.concatenate([upper, lower], axis=0)
    stacked = jnp.transpose(tau.reshape(2, spin_count, vector_count, column_count), (0, 2, 1, 3))
    stacked = stacked.reshape(2 * vector_count, spin_count * column_count)
    product = jnp.dot(sink_big, stacked, preferred_element_type=jnp.float32)
    product = jnp.transpose(
        product.reshape(2, vector_count, spin_count, column_count), (0, 2, 1, 3)
    )
    return product.reshape(2, spin_count * vector_count, column_count).astype(jnp.bfloat16)


def attach_source(propagated, source_big):
    vector_count = source_big.shape[0] // 2
    row_count = propagated.shape[1]
    spin_count = propagated.shape[2] // vector_count
    stacked = jnp.concatenate(
        [
            propagated[0].reshape(row_count, spin_count, vector_count),
            propagated[1].reshape(row_count, spin_count, vector_count),
        ],
        axis=2,
    )
    product = jnp.dot(
        stacked.reshape(row_count * spin_count, 2 * vector_count),
        source_big,
        preferred_element_type=jnp.float32,
    )
    product = jnp.transpose(product.reshape(row_count, spin_count, 2, vector_count), (2, 0, 1, 3))
    return product.reshape(2, row_count, spin_count * vector_count)


def general_body(eigenvectors, perambulator, momenta, ratios, source_slice):
    slab_count = eigenvectors.shape[0]
    color_count = eigenvectors.shape[2]
    site_count = eigenvectors.shape[3]
    vector_count = eigenvectors.shape[4]
    first_site = lax.axis_index("space") * site_count
    cosine, sine_part = site_phases(momenta, first_site, site_count)
    normalizer = 1.0 / math.sqrt(color_count * site_count * lax.axis_size("space") * vector_count)
    weights = (
        ratios[:, 0].astype(jnp.float32) / ratios[:, 1].astype(jnp.float32) * normalizer
    ).reshape(1, 2, 1, 1, 1)
    parts = elementals(eigenvectors, cosine, sine_part)
    partial_sums = jnp.sum(weights * parts, axis=1, keepdims=True)
    summed = lax.psum(partial_sums, "space")
    sink_matrices = summed[:, 0].astype(jnp.bfloat16)
    global_slice = source_slice[0] % (slab_count * lax.axis_size("tm"))
    local_source = lax.dynamic_index_in_dim(
        sink_matrices, global_slice % slab_count, 0, keepdims=False
    )
    chosen = spread(local_source, "tm", global_slice // slab_count)
    source_big = source_block(chosen)
    propagated = jnp.stack([propagate(sink_matrices[0], perambulator[0])])
    return jnp.stack(
        [
            attach_source(
                lax.all_to_all(propagated, "space", split_axis=2, concat_axis=3, tiled=True)[0],
                source_big,
            )
        ]
    )


def block_dot(left, right, left_dim, right_dim):
    return lax.dot_general(
        left, right, (((left_dim,), (right_dim,)), ((), ())), preferred_element_type=jnp.float32
    )


def exchange_kernel(
    momenta_ref,
    ratio_ref,
    slice_ref,
    eig_hbm,
    tau_hbm,
    res_ref,
    eig,
    acc,
    tau,
    tau_mine,
    part,
    pair_out,
    pair_in,
    cross_out,
    cross_in,
    sink,
    sink_pair,
    picked,
    far,
    sink_big,
    source_big,
    source_late,
    prop,
    prop_out,
    prop_in,
    cosines,
    sines,
    eig_sem,
    own_sem,
    tau_send,
    tau_recv,
    early_send,
    early_recv,
    pair_send,
    pair_recv,
    cross_send,
    cross_recv,
    back_send,
    back_recv,
    prop_send,
    prop_recv,
    spread_send,
    spread_recv,
    ready,
    *,
    normalizer,
):
    vector_count = eig_hbm.shape[4]
    site_count = eig_hbm.shape[3]
    chunk_count, chunk_rows = part.shape[0], part.shape[2]
    step_count, site_step = eig.shape[0], eig.shape[2]
    steps_per_color = site_count // site_step
    late_count = tau_mine.shape[2]
    early_count = vector_count - late_count
    piece_count = prop_send.shape[0]
    piece_rows = vector_count // piece_count
    me = lax.axis_index("space")
    slot = lax.axis_index("tm")
    near = me + 1 - 2 * (me % 2)
    across = me + 2 - 4 * (me // 2)
    mirror = 3 - me
    inner = ((me + 1) // 2) % 2
    core = slot % 2
    core_peer = slot + 1 - 2 * core
    chip_peer = slot + 2 - 4 * (slot // 2)

    def eig_copy(step):
        color, first = step // steps_per_color, (step % steps_per_color) * site_step
        return pltpu.make_async_copy(
            eig_hbm.at[0, :, color, pl.ds(first, site_step), :], eig.at[step], eig_sem.at[step]
        )

    for step in range(step_count):
        eig_copy(step).start()
    own_copy = pltpu.make_async_copy(
        tau_hbm.at[0, :, pl.ds(me * vector_count, vector_count), :], tau.at[me], own_sem.at[0]
    )
    late_copy = pltpu.make_async_copy(
        tau_hbm.at[
            0, :, pl.ds(across * vector_count, vector_count), pl.ds(early_count, late_count)
        ],
        tau_mine,
        own_sem.at[1],
    )

    barrier = pltpu.get_barrier_semaphore()

    def hello(peer):
        pl.semaphore_signal(barrier, inc=1, device_id=peer, device_id_type=MESH)

    hello({"space": near})
    hello({"tm": core_peer})
    hello({"tm": chip_peer})

    def hop(from_ref, to_ref, send_sem, recv_sem, peer):
        return pltpu.make_async_remote_copy(
            src_ref=from_ref,
            dst_ref=to_ref,
            send_sem=send_sem,
            recv_sem=recv_sem,
            device_id=peer,
            device_id_type=MESH,
        )

    def tau_copy(index, to, piece):
        return hop(
            tau_hbm.at[0, piece, pl.ds(to * vector_count, vector_count), :],
            tau.at[me, piece],
            tau_send.at[index, piece],
            tau_recv.at[me, piece],
            {"space": to},
        )

    near_copies = [tau_copy(0, near, piece) for piece in range(2)]
    across_copies = [tau_copy(1, across, piece) for piece in range(2)]
    mirror_copies = [tau_copy(2, mirror, piece) for piece in range(2)]
    early_copy = hop(
        tau_hbm.at[0, :, pl.ds(across * vector_count, vector_count), pl.ds(0, early_count)],
        tau.at[me, :, :, pl.ds(0, early_count)],
        early_send,
        early_recv,
        {"space": across},
    )
    prop_copies = [
        hop(
            prop_out.at[pl.ds(p * piece_rows, piece_rows), :],
            prop_in.at[pl.ds(p * piece_rows, piece_rows), :],
            prop_send.at[p],
            prop_recv.at[p],
            {"space": across},
        )
        for p in range(piece_count)
    ]

    def tell(index, peer):
        pl.semaphore_signal(
            ready.at[index], inc=1, device_id={"space": peer}, device_id_type=MESH
        )

    @pl.when(inner == 1)
    def _():
        hello({"space": mirror})
        pl.semaphore_wait(barrier, 4)
        mirror_copies[0].start()
        mirror_copies[1].start()
        near_copies[0].start()
        near_copies[1].start()
        tell(0, near)
        tell(0, mirror)
        pl.semaphore_wait(ready.at[0], 1)
        tell(1, near)
        late_copy.start()

    @pl.when(inner == 0)
    def _():
        pl.semaphore_wait(barrier, 3)
        near_copies[0].start()

    own_copy.start()

    lanes = cosines.shape[1]
    site = me * site_count + lax.broadcasted_iota(jnp.int32, (site_count, lanes), 0)
    first_lane = lax.broadcasted_iota(jnp.int32, (site_count, lanes), 1) == 0
    shift = LSIDE.bit_length() - 1
    places = (
        jnp.bitwise_and(site, LSIDE - 1),
        jnp.bitwise_and(jnp.right_shift(site, shift), LSIDE - 1),
        jnp.right_shift(site, 2 * shift),
    )
    turn = jnp.zeros_like(site)
    for axis in range(3):
        turn += jnp.where(first_lane, momenta_ref[0, axis], momenta_ref[1, axis]) * places[axis]
    angle = jnp.bitwise_and(turn, LSIDE - 1).astype(jnp.float32) * (2.0 * math.pi / LSIDE)
    cosines[...] = jnp.cos(angle)
    sines[...] = jnp.sin(angle)

    acc[...] = jnp.zeros_like(acc)

    def accumulate(step, carry):
        eig_copy(step).wait()
        rows = pl.ds(pl.multiple_of((step % steps_per_color) * site_step, site_step), site_step)
        plain_real, plain_imag = eig[step, 0], eig[step, 1]
        real = plain_real.astype(jnp.float32)
        imag = plain_imag.astype(jnp.float32)
        upper, lower = [], []
        for k in range(2):
            cosine = cosines[rows, k : k + 1]
            sine = sines[rows, k : k + 1]
            turned_real = (cosine * real + sine * imag).astype(jnp.bfloat16)
            turned_imag = (cosine * imag - sine * real).astype(jnp.bfloat16)
            upper += [turned_real, turned_imag]
            lower += [turned_imag, -turned_real]
        left = jnp.concatenate([plain_real, plain_imag], axis=0)
        right = jnp.concatenate(
            [jnp.concatenate(upper, axis=1), jnp.concatenate(lower, axis=1)], axis=0
        )
        acc[...] += block_dot(left, right, 0, 0)
        return carry

    lax.fori_loop(0, step_count, accumulate, 0)

    weights = [
        jnp.full((1, vector_count), ratio_ref[k, 0], jnp.int32).astype(jnp.float32)
        / jnp.full((1, vector_count), ratio_ref[k, 1], jnp.int32).astype(jnp.float32)
        * normalizer
        for k in range(2)
    ]

    def weighted(chunk, c):
        rows = pl.ds(chunk * chunk_rows, chunk_rows)
        return (
            weights[0] * acc[rows, c * vector_count : (c + 1) * vector_count]
            + weights[1] * acc[rows, (2 + c) * vector_count : (3 + c) * vector_count]
        )

    pair_hops = [
        hop(
            pair_out.at[q], pair_in.at[q], pair_send.at[q], pair_recv.at[q], {"space": near}
        )
        for q in range(chunk_count)
    ]
    cross_hops = [
        hop(
            cross_out.at[q], cross_in.at[q], cross_send.at[q], cross_recv.at[q], {"space": mirror}
        )
        for q in range(chunk_count)
    ]
    back_hops = [
        hop(sink.at[q], sink.at[q], back_send.at[q], back_recv.at[q], {"space": near})
        for q in range(chunk_count)
    ]

    @pl.when(inner == 0)
    def _():
        for q in range(chunk_count):
            for c in range(2):
                pair_out[q, c] = weighted(q, c).astype(jnp.bfloat16)
            pair_hops[q].start()
        near_copies[1].start()
        pl.semaphore_wait(ready.at[0], 1)
        pl.semaphore_wait(ready.at[1], 1)
        for q in range(chunk_count // 2):
            back_hops[q].wait_recv()
        for copy in across_copies + mirror_copies:
            copy.start()
        for q in range(chunk_count // 2, chunk_count):
            back_hops[q].wait_recv()

    @pl.when(inner == 1)
    def _():
        for q in range(chunk_count):
            for c in range(2):
                part[q, c] = weighted(q, c)
        for q in range(chunk_count):
            pair_hops[q].wait_recv()
            part[q] = part[q] + pair_in[q].astype(jnp.float32)
            cross_out[q] = part[q].astype(jnp.bfloat16)
            cross_hops[q].start()
        early_copy.start()
        for q in range(chunk_count):
            cross_hops[q].wait_recv()
            sink[q] = (part[q] + cross_in[q].astype(jnp.float32)).astype(jnp.bfloat16)
            back_hops[q].start()

    core_hop = hop(sink, sink_pair, spread_send.at[0], spread_recv.at[0], {"tm": core_peer})
    core_hop.start()
    for q in range(chunk_count):
        rows = pl.ds(q * chunk_rows, chunk_rows)
        low = pl.ds(vector_count + q * chunk_rows, chunk_rows)
        real, imag = sink[q, 0], sink[q, 1]
        sink_big[rows, :vector_count] = real
        sink_big[rows, vector_count:] = -imag
        sink_big[low, :vector_count] = imag
        sink_big[low, vector_count:] = real

    def carried(block):
        stacked = block.reshape(2 * vector_count, block.shape[2])
        product = block_dot(sink_big[...], stacked, 1, 0).astype(jnp.bfloat16)
        return product[:vector_count], product[vector_count:]

    def left_multiply(origin):
        real, imag = carried(tau[origin])
        prop[origin, :, :vector_count] = real
        prop[origin, :, vector_count:] = imag

    def right_multiply(origin):
        product = block_dot(prop[origin], source_big[...], 1, 1)
        res_ref[origin, 0] = product[:, :vector_count]
        res_ref[origin, 1] = product[:, vector_count:]

    def arrived(origin):
        for piece in range(2):
            hop(
                tau.at[origin, piece],
                tau.at[origin, piece],
                tau_send.at[0, piece],
                tau_recv.at[origin, piece],
                {"space": near},
            ).wait_recv()

    @pl.when(inner == 1)
    def _():
        late_copy.wait()
        real, imag = carried(tau_mine[...])
        prop_out[:, :late_count] = real
        prop_out[:, late_count:] = imag
        for copy in prop_copies:
            copy.start()

    core_hop.wait()
    chosen_slot = slice_ref[0] % lax.axis_size("tm")
    picked[...] = jnp.where(chosen_slot == slot, sink[...], sink_pair[...])
    half = pl.ds(core * (chunk_count // 2), chunk_count // 2)
    chip_hop = hop(
        picked.at[half], far.at[half], spread_send.at[1], spread_recv.at[1], {"tm": chip_peer}
    )
    chip_hop.start()

    own_copy.wait()
    left_multiply(me)
    chip_hop.wait()
    forward_hop = hop(
        far.at[half], far.at[half], spread_send.at[2], spread_recv.at[2], {"tm": core_peer}
    )
    forward_hop.start()
    arrived(near)
    left_multiply(near)
    forward_hop.wait()
    chosen = jnp.where(chosen_slot // 2 == slot // 2, picked[...], far[...])
    for q in range(chunk_count):
        rows = pl.ds(q * chunk_rows, chunk_rows)
        low = pl.ds(vector_count + q * chunk_rows, chunk_rows)
        source_big[rows, :vector_count] = chosen[q, 0]
        source_big[rows, vector_count:] = chosen[q, 1]
        source_big[low, :vector_count] = -chosen[q, 1]
        source_big[low, vector_count:] = chosen[q, 0]
    right_multiply(me)
    right_multiply(near)

    @pl.when(inner == 1)
    def _():
        for origin in (mirror, across):
            arrived(origin)
            left_multiply(origin)
            right_multiply(origin)
        for copy in mirror_copies + prop_copies:
            copy.wait_send()
        early_copy.wait_send()
        for q in range(chunk_count):
            cross_hops[q].wait_send()
            back_hops[q].wait_send()

    @pl.when(inner == 0)
    def _():
        early_copy.wait_recv()
        real, imag = carried(tau[across, :, :, :early_count])
        both = jnp.concatenate([real, imag], axis=1)
        source_early = jnp.concatenate(
            [
                source_big[:, :early_count],
                source_big[:, vector_count : vector_count + early_count],
            ],
            axis=1,
        )
        product = block_dot(both, source_early, 1, 1)
        res_ref[across, 0] = product[:, :vector_count]
        res_ref[across, 1] = product[:, vector_count:]
        source_late[:, :late_count] = source_big[:, early_count:vector_count]
        source_late[:, late_count:] = source_big[:, vector_count + early_count :]
        arrived(mirror)
        left_multiply(mirror)
        right_multiply(mirror)
        for q in range(chunk_count):
            pair_hops[q].wait_send()
        for copy in across_copies + mirror_copies:
            copy.wait_send()
        for p in range(piece_count):
            rows = pl.ds(p * piece_rows, piece_rows)
            prop_copies[p].wait_recv()
            product = block_dot(prop_in[rows, :], source_late[...], 1, 1)
            res_ref[across, 0, rows, :] += product[:, :vector_count]
            res_ref[across, 1, rows, :] += product[:, vector_count:]

    for copy in near_copies:
        copy.wait_send()


def finish_kernel(res_ref, out_hbm, sems):
    group, _, vector_count, _ = res_ref.shape
    copies = [
        pltpu.make_async_copy(
            res_ref.at[origin, c],
            out_hbm.at[0, c, :, pl.ds(origin * vector_count, vector_count)],
            sems.at[origin, c],
        )
        for origin in range(group)
        for c in range(2)
    ]
    for copy in copies:
        copy.start()
    for copy in copies:
        copy.wait()


def in_hbm(array):
    return pltpu.with_memory_space_constraint(array, pltpu.HBM)


def body(eigenvectors, perambulator, momenta, ratios, source_slice):
    color_count, site_count, vector_count = eigenvectors.shape[2:]
    group = lax.axis_size("space")
    normalizer = 1.0 / math.sqrt(color_count * site_count * group * vector_count)
    site_step = site_count // 2
    step_count = 2 * color_count
    chunk_count = 4
    piece_count = 4
    late_count = vector_count - 128
    whole = (chunk_count, 2, vector_count // chunk_count, vector_count)
    bf16, f32 = jnp.bfloat16, jnp.float32
    smem = pl.BlockSpec(memory_space=pltpu.SMEM)
    vmem = pl.BlockSpec(memory_space=pltpu.VMEM)
    anywhere = pl.BlockSpec(memory_space=pl.ANY)
    dma = pltpu.SemaphoreType.DMA
    room = 4 * group * 2 * vector_count * vector_count
    result = pl.pallas_call(
        functools.partial(exchange_kernel, normalizer=normalizer),
        out_shape=pltpu.VMEM((group, 2, vector_count, vector_count), f32),
        in_specs=[smem, smem, smem, anywhere, anywhere],
        out_specs=vmem,
        scratch_shapes=[
            pltpu.VMEM((step_count, 2, site_step, vector_count), bf16),
            pltpu.VMEM((vector_count, 4 * vector_count), f32),
            pltpu.VMEM((group, 2, vector_count, vector_count), bf16),
            pltpu.VMEM((2, vector_count, late_count), bf16),
            pltpu.VMEM(whole, f32),
            *[pltpu.VMEM(whole, bf16) for _ in range(8)],
            pltpu.VMEM((2 * vector_count, 2 * vector_count), bf16),
            pltpu.VMEM((2 * vector_count, 2 * vector_count), bf16),
            pltpu.VMEM((2 * vector_count, 2 * late_count), bf16),
            pltpu.VMEM((group, vector_count, 2 * vector_count), bf16),
            pltpu.VMEM((vector_count, 2 * late_count), bf16),
            pltpu.VMEM((vector_count, 2 * late_count), bf16),
            pltpu.VMEM((site_count, 128), f32),
            pltpu.VMEM((site_count, 128), f32),
            dma((step_count,)),
            dma((2,)),
            dma((3, 2)),
            dma((group, 2)),
            dma,
            dma,
            *[dma((chunk_count,)) for _ in range(6)],
            dma((piece_count,)),
            dma((piece_count,)),
            dma((3,)),
            dma((3,)),
            pltpu.SemaphoreType.REGULAR((2,)),
        ],
        compiler_params=pltpu.CompilerParams(
            collective_id=0,
            has_side_effects=True,
            vmem_limit_bytes=VMEM_BYTES - 3 * room,
        ),
        name="exchange",
    )(
        in_hbm(momenta),
        in_hbm(ratios),
        source_slice,
        in_hbm(eigenvectors),
        in_hbm(perambulator),
    )
    return pl.pallas_call(
        finish_kernel,
        out_shape=jax.ShapeDtypeStruct((1, 2, vector_count, group * vector_count), f32),
        in_specs=[vmem],
        out_specs=anywhere,
        scratch_shapes=[dma((group, 2))],
        compiler_params=pltpu.CompilerParams(vmem_limit_bytes=VMEM_BYTES // 2),
        name="finish",
    )(pltpu.with_memory_space_constraint(result, pltpu.VMEM))


def fits(mesh, eigenvectors, perambulator):
    space, slots = mesh.shape["space"], mesh.shape["tm"]
    vector_count = eigenvectors.shape[4]
    return (
        space == 4
        and slots == 4
        and eigenvectors.shape[0] == slots * mesh.shape["cfg"]
        and perambulator.shape[2] == space * vector_count
        and vector_count % 128 == 0
        and vector_count > 128
        and eigenvectors.shape[3] % (32 * space) == 0
    )


def solution(mesh):
    placed = (
        P(("cfg", "tm"), None, None, "space", None),
        P(("cfg", "tm"), None, None, "space"),
        P(),
        P(),
        P(),
    )

    def program(eigenvectors, perambulator, momenta, ratios, source_slice):
        chosen = body if fits(mesh, eigenvectors, perambulator) else general_body
        mapped = jax.shard_map(
            chosen,
            mesh=mesh,
            in_specs=placed,
            out_specs=P(("cfg", "tm"), None, "space", None),
            check_vma=False,
        )
        return mapped(eigenvectors, perambulator, momenta, ratios, source_slice)

    return program
```

```python
import functools
import math

import jax
import jax.numpy as jnp
from jax import lax
from jax.experimental import pallas as pl
from jax.experimental.pallas import tpu as pltpu
from jax.sharding import PartitionSpec as P

MESH = pl.DeviceIdType.MESH

LSIDE = 64

VMEM_BYTES = 67043328


def spread(value, axis, source):
    kept = jnp.where(lax.axis_index(axis) == source, value, 0).astype(value.dtype)
    return lax.psum(kept, axis)


def site_phases(momenta, first_site, site_count):
    site_index = first_site + lax.iota(jnp.int32, site_count)
    along_x = site_index % LSIDE
    along_y = site_index // LSIDE % LSIDE
    along_z = site_index // (LSIDE * LSIDE)
    turn_count = (
        momenta[:, 0:1] * along_x[None, :]
        + momenta[:, 1:2] * along_y[None, :]
        + momenta[:, 2:3] * along_z[None, :]
    )
    phase_angle = (turn_count % LSIDE).astype(jnp.float32) * (2.0 * math.pi / LSIDE)
    return (jnp.cos(phase_angle), jnp.sin(phase_angle))


def split_elementals(product, vector_count):
    lead_shape = product.shape[:-2]
    product_grid = product.reshape(lead_shape + (2, vector_count, 2, 2, vector_count))
    real_part = product_grid[..., 0, :, :, 0, :] + product_grid[..., 1, :, :, 1, :]
    imaginary = product_grid[..., 0, :, :, 1, :] - product_grid[..., 1, :, :, 0, :]
    stacked = jnp.stack([real_part, imaginary], axis=-4)
    return jnp.moveaxis(stacked, -2, -4)


def elementals(vectors, cosine, sine_part):
    slab_count, color_count, site_count, vector_count = (
        vectors.shape[0],
        vectors.shape[2],
        vectors.shape[3],
        vectors.shape[4],
    )
    row_count = color_count * site_count
    real_rows = vectors[:, 0].reshape(slab_count, row_count, vector_count)
    imaginary_rows = vectors[:, 1].reshape(slab_count, row_count, vector_count)
    cos_rows = jnp.broadcast_to(cosine[:, None, :], (2, color_count, site_count)).reshape(
        1, 2, row_count, 1
    )
    sin_rows = jnp.broadcast_to(sine_part[:, None, :], (2, color_count, site_count)).reshape(
        1, 2, row_count, 1
    )
    phased_real = (cos_rows * real_rows[:, None] + sin_rows * imaginary_rows[:, None]).astype(
        jnp.bfloat16
    )
    phased_imaginary = (cos_rows * imaginary_rows[:, None] - sin_rows * real_rows[:, None]).astype(
        jnp.bfloat16
    )
    phased = jnp.concatenate([phased_real, phased_imaginary], axis=3)
    phased = jnp.transpose(phased, (0, 2, 1, 3)).reshape(slab_count, row_count, 4 * vector_count)
    plain_vectors = jnp.concatenate([real_rows, imaginary_rows], axis=2)
    product = lax.dot_general(
        plain_vectors, phased, (((1,), (1,)), ((0,), (0,))), preferred_element_type=jnp.float32
    )
    return split_elementals(product, vector_count)


def source_block(chosen):
    real_t = chosen[0].T
    imaginary_t = chosen[1].T
    upper = jnp.concatenate([real_t, -imaginary_t], axis=1)
    lower = jnp.concatenate([imaginary_t, real_t], axis=1)
    return jnp.concatenate([upper, lower], axis=0)


def propagate(sink_matrix, tau):
    vector_count = sink_matrix.shape[1]
    spin_count = tau.shape[1] // vector_count
    column_count = tau.shape[2]
    real_part, imaginary = (sink_matrix[0], sink_matrix[1])
    upper = jnp.concatenate([real_part, -imaginary], axis=1)
    lower = jnp.concatenate([imaginary, real_part], axis=1)
    sink_big = jnp.concatenate([upper, lower], axis=0)
    stacked = jnp.transpose(tau.reshape(2, spin_count, vector_count, column_count), (0, 2, 1, 3))
    stacked = stacked.reshape(2 * vector_count, spin_count * column_count)
    product = jnp.dot(sink_big, stacked, preferred_element_type=jnp.float32)
    product = jnp.transpose(
        product.reshape(2, vector_count, spin_count, column_count), (0, 2, 1, 3)
    )
    return product.reshape(2, spin_count * vector_count, column_count).astype(jnp.bfloat16)


def attach_source(propagated, source_big):
    vector_count = source_big.shape[0] // 2
    row_count = propagated.shape[1]
    spin_count = propagated.shape[2] // vector_count
    stacked = jnp.concatenate(
        [
            propagated[0].reshape(row_count, spin_count, vector_count),
            propagated[1].reshape(row_count, spin_count, vector_count),
        ],
        axis=2,
    )
    product = jnp.dot(
        stacked.reshape(row_count * spin_count, 2 * vector_count),
        source_big,
        preferred_element_type=jnp.float32,
    )
    product = jnp.transpose(product.reshape(row_count, spin_count, 2, vector_count), (2, 0, 1, 3))
    return product.reshape(2, row_count, spin_count * vector_count)


def general_body(eigenvectors, perambulator, momenta, ratios, source_slice):
    slab_count = eigenvectors.shape[0]
    color_count = eigenvectors.shape[2]
    site_count = eigenvectors.shape[3]
    vector_count = eigenvectors.shape[4]
    first_site = lax.axis_index("space") * site_count
    cosine, sine_part = site_phases(momenta, first_site, site_count)
    normalizer = 1.0 / math.sqrt(color_count * site_count * lax.axis_size("space") * vector_count)
    weights = (
        ratios[:, 0].astype(jnp.float32) / ratios[:, 1].astype(jnp.float32) * normalizer
    ).reshape(1, 2, 1, 1, 1)
    parts = elementals(eigenvectors, cosine, sine_part)
    partial_sums = jnp.sum(weights * parts, axis=1, keepdims=True)
    summed = lax.psum(partial_sums, "space")
    sink_matrices = summed[:, 0].astype(jnp.bfloat16)
    global_slice = source_slice[0] % (slab_count * lax.axis_size("tm"))
    local_source = lax.dynamic_index_in_dim(
        sink_matrices, global_slice % slab_count, 0, keepdims=False
    )
    chosen = spread(local_source, "tm", global_slice // slab_count)
    source_big = source_block(chosen)
    propagated = jnp.stack([propagate(sink_matrices[0], perambulator[0])])
    return jnp.stack(
        [
            attach_source(
                lax.all_to_all(propagated, "space", split_axis=2, concat_axis=3, tiled=True)[0],
                source_big,
            )
        ]
    )


def block_dot(left, right, left_dim, right_dim):
    return lax.dot_general(
        left, right, (((left_dim,), (right_dim,)), ((), ())), preferred_element_type=jnp.float32
    )


def exchange_kernel(
    momenta_hbm,
    ratio_hbm,
    slice_ref,
    eig_hbm,
    tau_hbm,
    res_ref,
    momenta_ref,
    ratio_ref,
    eig,
    acc,
    tau,
    tau_mine,
    part,
    pair_out,
    pair_in,
    cross_out,
    cross_in,
    sink,
    sink_pair,
    picked,
    far,
    sink_big,
    source_big,
    source_late,
    prop,
    prop_out,
    prop_in,
    cosines,
    sines,
    eig_sem,
    own_sem,
    tau_send,
    tau_recv,
    early_send,
    early_recv,
    pair_send,
    pair_recv,
    cross_send,
    cross_recv,
    back_send,
    back_recv,
    prop_send,
    prop_recv,
    spread_send,
    spread_recv,
    ready,
    *,
    normalizer,
):
    vector_count = eig_hbm.shape[4]
    site_count = eig_hbm.shape[3]
    chunk_count, chunk_rows = part.shape[0], part.shape[2]
    step_count, site_step = eig.shape[0], eig.shape[2]
    steps_per_color = site_count // site_step
    late_count = tau_mine.shape[2]
    early_count = vector_count - late_count
    piece_count = prop_send.shape[0]
    piece_rows = vector_count // piece_count
    me = lax.axis_index("space")
    slot = lax.axis_index("tm")
    near = me + 1 - 2 * (me % 2)
    across = me + 2 - 4 * (me // 2)
    mirror = 3 - me
    inner = ((me + 1) // 2) % 2
    core = slot % 2
    core_peer = slot + 1 - 2 * core
    chip_peer = slot + 2 - 4 * (slot // 2)

    def eig_copy(step):
        color, first = step // steps_per_color, (step % steps_per_color) * site_step
        return pltpu.make_async_copy(
            eig_hbm.at[0, :, color, pl.ds(first, site_step), :], eig.at[step], eig_sem.at[step]
        )

    own_copy = pltpu.make_async_copy(
        tau_hbm.at[0, :, pl.ds(me * vector_count, vector_count), :], tau.at[me], own_sem.at[0]
    )
    late_copy = pltpu.make_async_copy(
        tau_hbm.at[
            0, :, pl.ds(mirror * vector_count, vector_count), pl.ds(early_count, late_count)
        ],
        tau_mine,
        own_sem.at[1],
    )
    scalar_copies = [
        pltpu.make_async_copy(momenta_hbm, momenta_ref, own_sem.at[2]),
        pltpu.make_async_copy(ratio_hbm, ratio_ref, own_sem.at[3]),
    ]

    barrier = pltpu.get_barrier_semaphore()

    def hello(peer):
        pl.semaphore_signal(barrier, inc=1, device_id=peer, device_id_type=MESH)

    hello({"space": near})
    hello({"tm": core_peer})
    hello({"tm": chip_peer})
    for copy in scalar_copies:
        copy.start()
    for step in range(step_count):
        eig_copy(step).start()

    def hop(from_ref, to_ref, send_sem, recv_sem, peer):
        return pltpu.make_async_remote_copy(
            src_ref=from_ref,
            dst_ref=to_ref,
            send_sem=send_sem,
            recv_sem=recv_sem,
            device_id=peer,
            device_id_type=MESH,
        )

    def tau_copy(index, to, piece):
        return hop(
            tau_hbm.at[0, piece, pl.ds(to * vector_count, vector_count), :],
            tau.at[me, piece],
            tau_send.at[index, piece],
            tau_recv.at[me, piece],
            {"space": to},
        )

    near_copies = [tau_copy(0, near, piece) for piece in range(2)]
    across_copies = [tau_copy(1, across, piece) for piece in range(2)]
    mirror_copies = [tau_copy(2, mirror, piece) for piece in range(2)]
    def early_copy(piece):
        first, count = early_rows[piece]
        return hop(
            tau_hbm.at[
                0, :, pl.ds(mirror * vector_count + first, count), pl.ds(0, early_count)
            ],
            tau.at[me, :, pl.ds(first, count), pl.ds(0, early_count)],
            early_send.at[piece],
            early_recv.at[piece],
            {"space": mirror},
        )

    lead = vector_count // 3 // 32 * 32
    early_rows = [(0, lead), (lead, vector_count - lead)]
    early_copies = [early_copy(piece) for piece in range(2)]
    prop_copies = [
        hop(
            prop_out.at[pl.ds(p * piece_rows, piece_rows), :],
            prop_in.at[pl.ds(p * piece_rows, piece_rows), :],
            prop_send.at[p],
            prop_recv.at[p],
            {"space": mirror},
        )
        for p in range(piece_count)
    ]

    def tell(index, peer):
        pl.semaphore_signal(ready.at[index], inc=1, device_id=peer, device_id_type=MESH)

    def phases():
        for copy in scalar_copies:
            copy.wait()
        lanes = cosines.shape[1]
        site = me * site_count + lax.broadcasted_iota(jnp.int32, (site_count, lanes), 0)
        first_lane = lax.broadcasted_iota(jnp.int32, (site_count, lanes), 1) == 0
        shift = LSIDE.bit_length() - 1
        places = (
            jnp.bitwise_and(site, LSIDE - 1),
            jnp.bitwise_and(jnp.right_shift(site, shift), LSIDE - 1),
            jnp.right_shift(site, 2 * shift),
        )
        turn = jnp.zeros_like(site)
        for axis in range(3):
            turn += jnp.where(first_lane, momenta_ref[0, axis], momenta_ref[1, axis]) * places[axis]
        angle = jnp.bitwise_and(turn, LSIDE - 1).astype(jnp.float32) * (2.0 * math.pi / LSIDE)
        cosines[...] = jnp.cos(angle)
        sines[...] = jnp.sin(angle)

    @pl.when(inner == 1)
    def _():
        hello({"space": mirror})
        pl.semaphore_wait(barrier, 4)
        tell(0, {"space": mirror})
        early_copies[0].start()
        tell(0, {"space": near})
        near_copies[0].start()
        phases()
        pl.semaphore_wait(ready.at[0], 1)
        for copy in across_copies:
            copy.start()
        tell(1, {"space": near})
        late_copy.start()

    @pl.when(inner == 0)
    def _():
        phases()
        pl.semaphore_wait(barrier, 3)
        near_copies[0].start()

    own_copy.start()

    acc[...] = jnp.zeros_like(acc)

    def accumulate(step, carry):
        eig_copy(step).wait()
        rows = pl.ds(pl.multiple_of((step % steps_per_color) * site_step, site_step), site_step)
        plain_real, plain_imag = eig[step, 0], eig[step, 1]
        real = plain_real.astype(jnp.float32)
        imag = plain_imag.astype(jnp.float32)
        upper, lower = [], []
        for k in range(2):
            cosine = cosines[rows, k : k + 1]
            sine = sines[rows, k : k + 1]
            turned_real = (cosine * real + sine * imag).astype(jnp.bfloat16)
            turned_imag = (cosine * imag - sine * real).astype(jnp.bfloat16)
            upper += [turned_real, turned_imag]
            lower += [turned_imag, -turned_real]
        left = jnp.concatenate([plain_real, plain_imag], axis=0)
        right = jnp.concatenate(
            [jnp.concatenate(upper, axis=1), jnp.concatenate(lower, axis=1)], axis=0
        )
        acc[...] += block_dot(left, right, 0, 0)
        return carry

    lax.fori_loop(0, step_count, accumulate, 0)

    weights = [
        jnp.full((1, vector_count), ratio_ref[k, 0], jnp.int32).astype(jnp.float32)
        / jnp.full((1, vector_count), ratio_ref[k, 1], jnp.int32).astype(jnp.float32)
        * normalizer
        for k in range(2)
    ]

    def weighted(chunk, c):
        rows = pl.ds(chunk * chunk_rows, chunk_rows)
        return (
            weights[0] * acc[rows, c * vector_count : (c + 1) * vector_count]
            + weights[1] * acc[rows, (2 + c) * vector_count : (3 + c) * vector_count]
        )

    pair_hops = [
        hop(
            pair_out.at[q], pair_in.at[q], pair_send.at[q], pair_recv.at[q], {"space": near}
        )
        for q in range(chunk_count)
    ]
    cross_hops = [
        hop(
            cross_out.at[q], cross_in.at[q], cross_send.at[q], cross_recv.at[q], {"space": mirror}
        )
        for q in range(chunk_count)
    ]
    back_hops = [
        hop(sink.at[q], sink.at[q], back_send.at[q], back_recv.at[q], {"space": near})
        for q in range(chunk_count)
    ]

    @pl.when(inner == 0)
    def _():
        for q in range(chunk_count):
            for c in range(2):
                pair_out[q, c] = weighted(q, c).astype(jnp.bfloat16)
            pair_hops[q].start()
        near_copies[1].start()
        pl.semaphore_wait(ready.at[0], 1)
        pl.semaphore_wait(ready.at[1], 1)
        for q in range(chunk_count - 1):
            back_hops[q].wait_recv()
        tell(2, {"tm": core_peer})
        pl.semaphore_wait(ready.at[2], 1)
        for copy in across_copies + mirror_copies:
            copy.start()
        back_hops[chunk_count - 1].wait_recv()

    @pl.when(inner == 1)
    def _():
        for q in range(chunk_count):
            for c in range(2):
                part[q, c] = weighted(q, c)

        def forward(q):
            pair_hops[q].wait_recv()
            part[q] = part[q] + pair_in[q].astype(jnp.float32)
            cross_out[q] = part[q].astype(jnp.bfloat16)
            cross_hops[q].start()

        def settle(q):
            cross_hops[q].wait_recv()
            sink[q] = (part[q] + cross_in[q].astype(jnp.float32)).astype(jnp.bfloat16)
            back_hops[q].start()

        for q in range(chunk_count):
            forward(q)
            if q == chunk_count - 1:
                early_copies[1].start()
            if q > 0:
                settle(q - 1)
        settle(chunk_count - 1)
        near_copies[1].start()

    core_hop = hop(sink, sink_pair, spread_send.at[0], spread_recv.at[0], {"tm": core_peer})
    core_hop.start()
    for q in range(chunk_count):
        rows = pl.ds(q * chunk_rows, chunk_rows)
        low = pl.ds(vector_count + q * chunk_rows, chunk_rows)
        real, imag = sink[q, 0], sink[q, 1]
        sink_big[rows, :vector_count] = real
        sink_big[rows, vector_count:] = -imag
        sink_big[low, :vector_count] = imag
        sink_big[low, vector_count:] = real

    def carried(block):
        stacked = block.reshape(2 * vector_count, block.shape[2])
        product = block_dot(sink_big[...], stacked, 1, 0).astype(jnp.bfloat16)
        return product[:vector_count], product[vector_count:]

    def left_multiply(origin):
        real, imag = carried(tau[origin])
        prop[origin, :, :vector_count] = real
        prop[origin, :, vector_count:] = imag

    def right_multiply(origin):
        product = block_dot(prop[origin], source_big[...], 1, 1)
        res_ref[origin, 0] = product[:, :vector_count]
        res_ref[origin, 1] = product[:, vector_count:]

    def arrived(origin):
        for piece in range(2):
            hop(
                tau.at[origin, piece],
                tau.at[origin, piece],
                tau_send.at[0, piece],
                tau_recv.at[origin, piece],
                {"space": near},
            ).wait_recv()

    @pl.when(inner == 1)
    def _():
        late_copy.wait()
        real, imag = carried(tau_mine[...])
        prop_out[:, :late_count] = real
        prop_out[:, late_count:] = imag
        for copy in prop_copies:
            copy.start()

    core_hop.wait()
    chosen_slot = slice_ref[0] % lax.axis_size("tm")
    picked[...] = jnp.where(chosen_slot == slot, sink[...], sink_pair[...])
    half = pl.ds(core * (chunk_count // 2), chunk_count // 2)
    chip_hop = hop(
        picked.at[half], far.at[half], spread_send.at[1], spread_recv.at[1], {"tm": chip_peer}
    )
    chip_hop.start()

    own_copy.wait()
    left_multiply(me)

    @pl.when(inner == 1)
    def _():
        arrived(near)
        left_multiply(near)

    @pl.when(inner == 0)
    def _():
        arrived(across)
        left_multiply(across)

    chip_hop.wait()
    forward_hop = hop(
        far.at[half], far.at[half], spread_send.at[2], spread_recv.at[2], {"tm": core_peer}
    )
    forward_hop.start()
    forward_hop.wait()
    chosen = jnp.where(chosen_slot // 2 == slot // 2, picked[...], far[...])
    for q in range(chunk_count):
        rows = pl.ds(q * chunk_rows, chunk_rows)
        low = pl.ds(vector_count + q * chunk_rows, chunk_rows)
        source_big[rows, :vector_count] = chosen[q, 0]
        source_big[rows, vector_count:] = chosen[q, 1]
        source_big[low, :vector_count] = -chosen[q, 1]
        source_big[low, vector_count:] = chosen[q, 0]
    right_multiply(me)

    @pl.when(inner == 0)
    def _():
        right_multiply(across)
        for origin in (near, mirror):
            arrived(origin)
            left_multiply(origin)
            right_multiply(origin)
        for q in range(chunk_count):
            pair_hops[q].wait_send()
        for copy in across_copies + mirror_copies:
            copy.wait_send()

    @pl.when(inner == 1)
    def _():
        right_multiply(near)
        for q in range(chunk_count):
            cross_hops[q].wait_send()
            back_hops[q].wait_send()
        for copy in across_copies:
            copy.wait_send()
        arrived(across)
        left_multiply(across)
        right_multiply(across)
        for copy in early_copies:
            copy.wait_recv()
        both = jnp.concatenate(carried(tau[mirror, :, :, :early_count]), axis=1)
        source_early = jnp.concatenate(
            [
                source_big[:, :early_count],
                source_big[:, vector_count : vector_count + early_count],
            ],
            axis=1,
        )
        product = block_dot(both, source_early, 1, 1)
        res_ref[mirror, 0] = product[:, :vector_count]
        res_ref[mirror, 1] = product[:, vector_count:]
        source_late[:, :late_count] = source_big[:, early_count:vector_count]
        source_late[:, late_count:] = source_big[:, vector_count + early_count :]
        for copy in early_copies:
            copy.wait_send()
        for p in range(piece_count):
            rows = pl.ds(p * piece_rows, piece_rows)
            prop_copies[p].wait_recv()
            product = block_dot(prop_in[rows, :], source_late[...], 1, 1)
            res_ref[mirror, 0, rows, :] += product[:, :vector_count]
            res_ref[mirror, 1, rows, :] += product[:, vector_count:]
        for copy in prop_copies:
            copy.wait_send()

    for copy in near_copies:
        copy.wait_send()


def finish_kernel(res_ref, out_hbm, sems):
    group, _, vector_count, _ = res_ref.shape
    copies = [
        pltpu.make_async_copy(
            res_ref.at[origin, c],
            out_hbm.at[0, c, :, pl.ds(origin * vector_count, vector_count)],
            sems.at[origin, c],
        )
        for origin in range(group)
        for c in range(2)
    ]
    for copy in copies:
        copy.start()
    for copy in copies:
        copy.wait()


def in_hbm(array):
    return pltpu.with_memory_space_constraint(array, pltpu.HBM)


def body(eigenvectors, perambulator, momenta, ratios, source_slice):
    color_count, site_count, vector_count = eigenvectors.shape[2:]
    group = lax.axis_size("space")
    normalizer = 1.0 / math.sqrt(color_count * site_count * group * vector_count)
    site_step = site_count // 2
    step_count = 2 * color_count
    chunk_count = 4
    piece_count = 4
    late_count = 128
    whole = (chunk_count, 2, vector_count // chunk_count, vector_count)
    bf16, f32 = jnp.bfloat16, jnp.float32
    smem = pl.BlockSpec(memory_space=pltpu.SMEM)
    vmem = pl.BlockSpec(memory_space=pltpu.VMEM)
    anywhere = pl.BlockSpec(memory_space=pl.ANY)
    dma = pltpu.SemaphoreType.DMA
    room = 4 * group * 2 * vector_count * vector_count
    result = pl.pallas_call(
        functools.partial(exchange_kernel, normalizer=normalizer),
        out_shape=pltpu.VMEM((group, 2, vector_count, vector_count), f32),
        in_specs=[anywhere, anywhere, smem, anywhere, anywhere],
        out_specs=vmem,
        scratch_shapes=[
            pltpu.SMEM(momenta.shape, jnp.int32),
            pltpu.SMEM(ratios.shape, jnp.int32),
            pltpu.VMEM((step_count, 2, site_step, vector_count), bf16),
            pltpu.VMEM((vector_count, 4 * vector_count), f32),
            pltpu.VMEM((group, 2, vector_count, vector_count), bf16),
            pltpu.VMEM((2, vector_count, late_count), bf16),
            pltpu.VMEM(whole, f32),
            *[pltpu.VMEM(whole, bf16) for _ in range(8)],
            pltpu.VMEM((2 * vector_count, 2 * vector_count), bf16),
            pltpu.VMEM((2 * vector_count, 2 * vector_count), bf16),
            pltpu.VMEM((2 * vector_count, 2 * late_count), bf16),
            pltpu.VMEM((group, vector_count, 2 * vector_count), bf16),
            pltpu.VMEM((vector_count, 2 * late_count), bf16),
            pltpu.VMEM((vector_count, 2 * late_count), bf16),
            pltpu.VMEM((site_count, 128), f32),
            pltpu.VMEM((site_count, 128), f32),
            dma((step_count,)),
            dma((4,)),
            dma((3, 2)),
            dma((group, 2)),
            dma((2,)),
            dma((2,)),
            *[dma((chunk_count,)) for _ in range(6)],
            dma((piece_count,)),
            dma((piece_count,)),
            dma((3,)),
            dma((3,)),
            pltpu.SemaphoreType.REGULAR((3,)),
        ],
        compiler_params=pltpu.CompilerParams(
            collective_id=0,
            has_side_effects=True,
            vmem_limit_bytes=VMEM_BYTES - 3 * room,
        ),
        name="exchange",
    )(
        in_hbm(momenta),
        in_hbm(ratios),
        source_slice,
        in_hbm(eigenvectors),
        in_hbm(perambulator),
    )
    return pl.pallas_call(
        finish_kernel,
        out_shape=jax.ShapeDtypeStruct((1, 2, vector_count, group * vector_count), f32),
        in_specs=[vmem],
        out_specs=anywhere,
        scratch_shapes=[dma((group, 2))],
        compiler_params=pltpu.CompilerParams(vmem_limit_bytes=VMEM_BYTES // 2),
        name="finish",
    )(pltpu.with_memory_space_constraint(result, pltpu.VMEM))


def fits(mesh, eigenvectors, perambulator):
    space, slots = mesh.shape["space"], mesh.shape["tm"]
    vector_count = eigenvectors.shape[4]
    return (
        space == 4
        and slots == 4
        and eigenvectors.shape[0] == slots * mesh.shape["cfg"]
        and perambulator.shape[2] == space * vector_count
        and vector_count % 128 == 0
        and vector_count > 128
        and eigenvectors.shape[3] % (32 * space) == 0
    )


def solution(mesh):
    placed = (
        P(("cfg", "tm"), None, None, "space", None),
        P(("cfg", "tm"), None, None, "space"),
        P(),
        P(),
        P(),
    )

    def program(eigenvectors, perambulator, momenta, ratios, source_slice):
        chosen = body if fits(mesh, eigenvectors, perambulator) else general_body
        mapped = jax.shard_map(
            chosen,
            mesh=mesh,
            in_specs=placed,
            out_specs=P(("cfg", "tm"), None, "space", None),
            check_vma=False,
        )
        return mapped(eigenvectors, perambulator, momenta, ratios, source_slice)

    return program
```

```python
import functools
import math

import jax
import jax.numpy as jnp
from jax import lax
from jax.experimental import pallas as pl
from jax.experimental.pallas import tpu as pltpu
from jax.sharding import PartitionSpec as P

MESH = pl.DeviceIdType.MESH

LSIDE = 64

VMEM_BYTES = 67043328


def spread(value, axis, source):
    kept = jnp.where(lax.axis_index(axis) == source, value, 0).astype(value.dtype)
    return lax.psum(kept, axis)


def site_phases(momenta, first_site, site_count):
    site_index = first_site + lax.iota(jnp.int32, site_count)
    along_x = site_index % LSIDE
    along_y = site_index // LSIDE % LSIDE
    along_z = site_index // (LSIDE * LSIDE)
    turn_count = (
        momenta[:, 0:1] * along_x[None, :]
        + momenta[:, 1:2] * along_y[None, :]
        + momenta[:, 2:3] * along_z[None, :]
    )
    phase_angle = (turn_count % LSIDE).astype(jnp.float32) * (2.0 * math.pi / LSIDE)
    return (jnp.cos(phase_angle), jnp.sin(phase_angle))


def split_elementals(product, vector_count):
    lead_shape = product.shape[:-2]
    product_grid = product.reshape(lead_shape + (2, vector_count, 2, 2, vector_count))
    real_part = product_grid[..., 0, :, :, 0, :] + product_grid[..., 1, :, :, 1, :]
    imaginary = product_grid[..., 0, :, :, 1, :] - product_grid[..., 1, :, :, 0, :]
    stacked = jnp.stack([real_part, imaginary], axis=-4)
    return jnp.moveaxis(stacked, -2, -4)


def elementals(vectors, cosine, sine_part):
    slab_count, color_count, site_count, vector_count = (
        vectors.shape[0],
        vectors.shape[2],
        vectors.shape[3],
        vectors.shape[4],
    )
    row_count = color_count * site_count
    real_rows = vectors[:, 0].reshape(slab_count, row_count, vector_count)
    imaginary_rows = vectors[:, 1].reshape(slab_count, row_count, vector_count)
    cos_rows = jnp.broadcast_to(cosine[:, None, :], (2, color_count, site_count)).reshape(
        1, 2, row_count, 1
    )
    sin_rows = jnp.broadcast_to(sine_part[:, None, :], (2, color_count, site_count)).reshape(
        1, 2, row_count, 1
    )
    phased_real = (cos_rows * real_rows[:, None] + sin_rows * imaginary_rows[:, None]).astype(
        jnp.bfloat16
    )
    phased_imaginary = (cos_rows * imaginary_rows[:, None] - sin_rows * real_rows[:, None]).astype(
        jnp.bfloat16
    )
    phased = jnp.concatenate([phased_real, phased_imaginary], axis=3)
    phased = jnp.transpose(phased, (0, 2, 1, 3)).reshape(slab_count, row_count, 4 * vector_count)
    plain_vectors = jnp.concatenate([real_rows, imaginary_rows], axis=2)
    product = lax.dot_general(
        plain_vectors, phased, (((1,), (1,)), ((0,), (0,))), preferred_element_type=jnp.float32
    )
    return split_elementals(product, vector_count)


def source_block(chosen):
    real_t = chosen[0].T
    imaginary_t = chosen[1].T
    upper = jnp.concatenate([real_t, -imaginary_t], axis=1)
    lower = jnp.concatenate([imaginary_t, real_t], axis=1)
    return jnp.concatenate([upper, lower], axis=0)


def propagate(sink_matrix, tau):
    vector_count = sink_matrix.shape[1]
    spin_count = tau.shape[1] // vector_count
    column_count = tau.shape[2]
    real_part, imaginary = (sink_matrix[0], sink_matrix[1])
    upper = jnp.concatenate([real_part, -imaginary], axis=1)
    lower = jnp.concatenate([imaginary, real_part], axis=1)
    sink_big = jnp.concatenate([upper, lower], axis=0)
    stacked = jnp.transpose(tau.reshape(2, spin_count, vector_count, column_count), (0, 2, 1, 3))
    stacked = stacked.reshape(2 * vector_count, spin_count * column_count)
    product = jnp.dot(sink_big, stacked, preferred_element_type=jnp.float32)
    product = jnp.transpose(
        product.reshape(2, vector_count, spin_count, column_count), (0, 2, 1, 3)
    )
    return product.reshape(2, spin_count * vector_count, column_count).astype(jnp.bfloat16)


def attach_source(propagated, source_big):
    vector_count = source_big.shape[0] // 2
    row_count = propagated.shape[1]
    spin_count = propagated.shape[2] // vector_count
    stacked = jnp.concatenate(
        [
            propagated[0].reshape(row_count, spin_count, vector_count),
            propagated[1].reshape(row_count, spin_count, vector_count),
        ],
        axis=2,
    )
    product = jnp.dot(
        stacked.reshape(row_count * spin_count, 2 * vector_count),
        source_big,
        preferred_element_type=jnp.float32,
    )
    product = jnp.transpose(product.reshape(row_count, spin_count, 2, vector_count), (2, 0, 1, 3))
    return product.reshape(2, row_count, spin_count * vector_count)


def general_body(eigenvectors, perambulator, momenta, ratios, source_slice):
    slab_count = eigenvectors.shape[0]
    color_count = eigenvectors.shape[2]
    site_count = eigenvectors.shape[3]
    vector_count = eigenvectors.shape[4]
    first_site = lax.axis_index("space") * site_count
    cosine, sine_part = site_phases(momenta, first_site, site_count)
    normalizer = 1.0 / math.sqrt(color_count * site_count * lax.axis_size("space") * vector_count)
    weights = (
        ratios[:, 0].astype(jnp.float32) / ratios[:, 1].astype(jnp.float32) * normalizer
    ).reshape(1, 2, 1, 1, 1)
    parts = elementals(eigenvectors, cosine, sine_part)
    partial_sums = jnp.sum(weights * parts, axis=1, keepdims=True)
    summed = lax.psum(partial_sums, "space")
    sink_matrices = summed[:, 0].astype(jnp.bfloat16)
    global_slice = source_slice[0] % (slab_count * lax.axis_size("tm"))
    local_source = lax.dynamic_index_in_dim(
        sink_matrices, global_slice % slab_count, 0, keepdims=False
    )
    chosen = spread(local_source, "tm", global_slice // slab_count)
    source_big = source_block(chosen)
    propagated = jnp.stack([propagate(sink_matrices[0], perambulator[0])])
    return jnp.stack(
        [
            attach_source(
                lax.all_to_all(propagated, "space", split_axis=2, concat_axis=3, tiled=True)[0],
                source_big,
            )
        ]
    )


def block_dot(left, right, left_dim, right_dim):
    return lax.dot_general(
        left, right, (((left_dim,), (right_dim,)), ((), ())), preferred_element_type=jnp.float32
    )


def exchange_kernel(
    momenta_hbm,
    ratio_hbm,
    slice_ref,
    eig_hbm,
    tau_hbm,
    res_ref,
    momenta_ref,
    ratio_ref,
    eig,
    acc,
    tau,
    tau_mine,
    part,
    pair_out,
    pair_in,
    cross_out,
    cross_in,
    sink,
    sink_pair,
    picked,
    far,
    sink_big,
    source_big,
    source_late,
    prop,
    prop_out,
    prop_in,
    cosines,
    sines,
    own_sem,
    send,
    recv,
    spread_recv,
    ready,
    *,
    normalizer,
):
    vector_count = eig_hbm.shape[4]
    site_count = eig_hbm.shape[3]
    chunk_count, chunk_rows = part.shape[0], part.shape[2]
    color_count = eig.shape[1]
    site_step = site_count // 2
    steps_per_color = site_count // site_step
    step_count = color_count * steps_per_color
    late_count = tau_mine.shape[2]
    early_count = vector_count - late_count
    piece_count = 4
    piece_rows = vector_count // piece_count
    me = lax.axis_index("space")
    slot = lax.axis_index("tm")
    near = me + 1 - 2 * (me % 2)
    across = me + 2 - 4 * (me // 2)
    mirror = 3 - me
    inner = ((me + 1) // 2) % 2
    core = slot % 2
    core_peer = slot + 1 - 2 * core
    chip_peer = slot + 2 - 4 * (slot // 2)

    eig_copy = pltpu.make_async_copy(eig_hbm.at[0], eig, own_sem.at[4])
    own_copy = pltpu.make_async_copy(
        tau_hbm.at[0, :, pl.ds(me * vector_count, vector_count), :], tau.at[me], own_sem.at[0]
    )
    late_copy = pltpu.make_async_copy(
        tau_hbm.at[
            0, :, pl.ds(mirror * vector_count, vector_count), pl.ds(early_count, late_count)
        ],
        tau_mine,
        own_sem.at[1],
    )
    scalar_copies = [
        pltpu.make_async_copy(momenta_hbm, momenta_ref, own_sem.at[2]),
        pltpu.make_async_copy(ratio_hbm, ratio_ref, own_sem.at[3]),
    ]

    barrier = pltpu.get_barrier_semaphore()

    def hello(peer):
        pl.semaphore_signal(barrier, inc=1, device_id=peer, device_id_type=MESH)

    def hop(from_ref, to_ref, send_sem, recv_sem, peer):
        return pltpu.make_async_remote_copy(
            src_ref=from_ref,
            dst_ref=to_ref,
            send_sem=send_sem,
            recv_sem=recv_sem,
            device_id=peer,
            device_id_type=MESH,
        )

    def tau_copy(to, part_of, recv_index):
        return hop(
            tau_hbm.at[0, part_of, pl.ds(to * vector_count, vector_count), :],
            tau.at[me, part_of],
            send.at[0],
            recv.at[recv_index],
            {"space": to},
        )

    near_copies = [tau_copy(near, piece, piece) for piece in range(2)]
    across_raw = tau_copy(across, slice(None), 6)
    across_copies = [tau_copy(across, piece, 12 + piece) for piece in range(2)]
    mirror_copy = tau_copy(mirror, slice(None), 7)
    def early_copy(piece):
        first, count = early_rows[piece]
        return hop(
            tau_hbm.at[
                0, :, pl.ds(mirror * vector_count + first, count), pl.ds(0, early_count)
            ],
            tau.at[me, :, pl.ds(first, count), pl.ds(0, early_count)],
            send.at[1],
            recv.at[10 + piece],
            {"space": mirror},
        )

    lead = vector_count * 5 // 12 // 32 * 32
    early_rows = [(0, lead), (lead, vector_count - lead)]
    early_copies = [early_copy(piece) for piece in range(2)]
    prop_copies = [
        hop(
            prop_out.at[pl.ds(p * piece_rows, piece_rows), :],
            prop_in.at[pl.ds(p * piece_rows, piece_rows), :],
            send.at[1],
            recv.at[14 + p],
            {"space": mirror},
        )
        for p in range(piece_count)
    ]

    def tell(index, peer):
        pl.semaphore_signal(ready.at[index], inc=1, device_id=peer, device_id_type=MESH)

    def phases():
        for copy in scalar_copies:
            copy.wait()
        lanes = cosines.shape[1]
        site = me * site_count + lax.broadcasted_iota(jnp.int32, (site_count, lanes), 0)
        first_lane = lax.broadcasted_iota(jnp.int32, (site_count, lanes), 1) == 0
        shift = LSIDE.bit_length() - 1
        places = (
            jnp.bitwise_and(site, LSIDE - 1),
            jnp.bitwise_and(jnp.right_shift(site, shift), LSIDE - 1),
            jnp.right_shift(site, 2 * shift),
        )
        turn = jnp.zeros_like(site)
        for axis in range(3):
            turn += jnp.where(first_lane, momenta_ref[0, axis], momenta_ref[1, axis]) * places[axis]
        angle = jnp.bitwise_and(turn, LSIDE - 1).astype(jnp.float32) * (2.0 * math.pi / LSIDE)
        cosines[...] = jnp.cos(angle)
        sines[...] = jnp.sin(angle)

    @pl.when(inner == 1)
    def _():
        hello({"space": mirror})
        hello({"space": near})
        pl.semaphore_wait(barrier, 1)
        early_copies[0].start()
        for copy in scalar_copies:
            copy.start()
        eig_copy.start()
        phases()
        pl.semaphore_wait(ready.at[0], 1)
        tell(1, {"space": mirror})
        near_copies[0].start()
        pl.semaphore_wait(ready.at[1], 1)
        across_raw.start()
        tell(2, {"space": near})
        late_copy.start()

    @pl.when(inner == 0)
    def _():
        hello({"tm": core_peer})
        hello({"tm": chip_peer})
        for copy in scalar_copies:
            copy.start()
        eig_copy.start()
        pl.semaphore_wait(barrier, 3)
        tell(0, {"space": near})
        near_copies[0].start()
        tell(0, {"tm": core_peer})
        tell(1, {"tm": chip_peer})
        phases()
        pl.semaphore_wait(ready.at[0], 1)
        pl.semaphore_wait(ready.at[1], 1)
        tell(3, {"space": near})

    own_copy.start()

    acc[...] = jnp.zeros_like(acc)

    eig_copy.wait()

    def accumulate(step, carry):
        color = step // steps_per_color
        rows = pl.ds(pl.multiple_of((step % steps_per_color) * site_step, site_step), site_step)
        plain_real, plain_imag = eig[0, color, rows, :], eig[1, color, rows, :]
        real = plain_real.astype(jnp.float32)
        imag = plain_imag.astype(jnp.float32)
        upper, lower = [], []
        for k in range(2):
            cosine = cosines[rows, k : k + 1]
            sine = sines[rows, k : k + 1]
            turned_real = (cosine * real + sine * imag).astype(jnp.bfloat16)
            turned_imag = (cosine * imag - sine * real).astype(jnp.bfloat16)
            upper += [turned_real, turned_imag]
            lower += [turned_imag, -turned_real]
        left = jnp.concatenate([plain_real, plain_imag], axis=0)
        right = jnp.concatenate(
            [jnp.concatenate(upper, axis=1), jnp.concatenate(lower, axis=1)], axis=0
        )
        acc[...] += block_dot(left, right, 0, 0)
        return carry

    lax.fori_loop(0, step_count, accumulate, 0, unroll=True)

    weights = [
        jnp.full((1, vector_count), ratio_ref[k, 0], jnp.int32).astype(jnp.float32)
        / jnp.full((1, vector_count), ratio_ref[k, 1], jnp.int32).astype(jnp.float32)
        * normalizer
        for k in range(2)
    ]

    def weighted(chunk, c):
        rows = pl.ds(chunk * chunk_rows, chunk_rows)
        return (
            weights[0] * acc[rows, c * vector_count : (c + 1) * vector_count]
            + weights[1] * acc[rows, (2 + c) * vector_count : (3 + c) * vector_count]
        )

    pair_hops = [
        hop(
            pair_out.at[q], pair_in.at[q], send.at[0], recv.at[2 + q], {"space": near}
        )
        for q in range(chunk_count)
    ]
    cross_hops = [
        hop(
            cross_out.at[q], cross_in.at[q], send.at[0], recv.at[6 + q], {"space": mirror}
        )
        for q in range(chunk_count)
    ]
    back_hops = [
        hop(sink.at[q], sink.at[q], send.at[0], recv.at[2 + q], {"space": near})
        for q in range(chunk_count)
    ]

    @pl.when(inner == 0)
    def _():
        for q in range(chunk_count):
            for c in range(2):
                pair_out[q, c] = weighted(q, c).astype(jnp.bfloat16)
            pair_hops[q].start()
        near_copies[1].start()
        pl.semaphore_wait(ready.at[2], 1)
        for q in range(chunk_count // 2):
            back_hops[q].wait_recv()
        tell(4, {"tm": core_peer})
        pl.semaphore_wait(ready.at[4], 1)
        across_copies[0].start()
        mirror_copy.start()
        across_copies[1].start()
        for q in range(chunk_count // 2, chunk_count):
            back_hops[q].wait_recv()

    @pl.when(inner == 1)
    def _():
        for q in range(chunk_count):
            for c in range(2):
                part[q, c] = weighted(q, c)

        def forward(q):
            pair_hops[q].wait_recv()
            part[q] = part[q] + pair_in[q].astype(jnp.float32)
            cross_out[q] = part[q].astype(jnp.bfloat16)
            cross_hops[q].start()

        def settle(q):
            cross_hops[q].wait_recv()
            sink[q] = (part[q] + cross_in[q].astype(jnp.float32)).astype(jnp.bfloat16)
            back_hops[q].start()

        for q in range(chunk_count):
            forward(q)
            if q == chunk_count - 1:
                early_copies[1].start()
            if q > 1:
                settle(q - 2)
        for q in range(chunk_count - 2, chunk_count):
            settle(q)
        near_copies[1].start()
        pl.semaphore_wait(ready.at[3], 1)

    core_hop = hop(sink, sink_pair, send.at[2], spread_recv.at[0], {"tm": core_peer})
    core_hop.start()
    for q in range(chunk_count):
        rows = pl.ds(q * chunk_rows, chunk_rows)
        low = pl.ds(vector_count + q * chunk_rows, chunk_rows)
        real, imag = sink[q, 0], sink[q, 1]
        sink_big[rows, :vector_count] = real
        sink_big[rows, vector_count:] = -imag
        sink_big[low, :vector_count] = imag
        sink_big[low, vector_count:] = real

    def carried(block):
        stacked = block.reshape(2 * vector_count, block.shape[2])
        product = block_dot(sink_big[...], stacked, 1, 0).astype(jnp.bfloat16)
        return product[:vector_count], product[vector_count:]

    def left_multiply(origin):
        real, imag = carried(tau[origin])
        prop[origin, :, :vector_count] = real
        prop[origin, :, vector_count:] = imag

    def right_multiply(origin):
        product = block_dot(prop[origin], source_big[...], 1, 1)
        res_ref[origin, 0] = product[:, :vector_count]
        res_ref[origin, 1] = product[:, vector_count:]

    def arrived(copies):
        for copy in copies:
            copy.wait_recv()

    @pl.when(inner == 1)
    def _():
        late_copy.wait()
        real, imag = carried(tau_mine[...])
        prop_out[:, :late_count] = real
        prop_out[:, late_count:] = imag
        for copy in prop_copies:
            copy.start()

    core_hop.wait_recv()
    chosen_slot = slice_ref[0] % lax.axis_size("tm")
    picked[...] = jnp.where(chosen_slot == slot, sink[...], sink_pair[...])
    half = pl.ds(core * (chunk_count // 2), chunk_count // 2)
    chip_hop = hop(
        picked.at[half], far.at[half], send.at[2], spread_recv.at[1], {"tm": chip_peer}
    )
    chip_hop.start()

    own_copy.wait()
    left_multiply(me)

    @pl.when(inner == 1)
    def _():
        arrived(near_copies)
        left_multiply(near)

    @pl.when(inner == 0)
    def _():
        arrived([across_raw])
        left_multiply(across)

    chip_hop.wait_recv()
    forward_hop = hop(
        far.at[half], far.at[half], send.at[2], spread_recv.at[2], {"tm": core_peer}
    )
    forward_hop.start()
    forward_hop.wait_recv()
    chosen = jnp.where(chosen_slot // 2 == slot // 2, picked[...], far[...])
    for q in range(chunk_count):
        rows = pl.ds(q * chunk_rows, chunk_rows)
        low = pl.ds(vector_count + q * chunk_rows, chunk_rows)
        source_big[rows, :vector_count] = chosen[q, 0]
        source_big[rows, vector_count:] = chosen[q, 1]
        source_big[low, :vector_count] = -chosen[q, 1]
        source_big[low, vector_count:] = chosen[q, 0]
    right_multiply(me)

    @pl.when(inner == 0)
    def _():
        right_multiply(across)
        for origin, copies in ((near, near_copies), (mirror, [mirror_copy])):
            arrived(copies)
            left_multiply(origin)
            right_multiply(origin)

    @pl.when(inner == 1)
    def _():
        right_multiply(near)
        arrived(across_copies)
        left_multiply(across)
        right_multiply(across)
        arrived(early_copies)
        both = jnp.concatenate(carried(tau[mirror, :, :, :early_count]), axis=1)
        source_early = jnp.concatenate(
            [
                source_big[:, :early_count],
                source_big[:, vector_count : vector_count + early_count],
            ],
            axis=1,
        )
        product = block_dot(both, source_early, 1, 1)
        res_ref[mirror, 0] = product[:, :vector_count]
        res_ref[mirror, 1] = product[:, vector_count:]
        source_late[:late_count] = source_big[:, early_count:vector_count].T
        source_late[late_count:] = source_big[:, vector_count + early_count :].T

        def add_piece(p):
            rows = pl.ds(p * piece_rows, piece_rows)
            prop_copies[p].wait_recv()
            product = block_dot(prop_in[rows, :], source_late[...], 1, 0)
            res_ref[mirror, 0, rows, :] += product[:, :vector_count]
            res_ref[mirror, 1, rows, :] += product[:, vector_count:]

        for p in range(piece_count):
            add_piece(p)
        hop(sink, sink, send.at[1], recv.at[0], {"space": near}).wait_send()

    hop(tau, tau, send.at[0], recv.at[0], {"space": near}).wait_send()
    pair = pl.ds(0, 2)
    hop(tau.at[pair], tau.at[pair], send.at[2], recv.at[0], {"space": near}).wait_send()


def finish_kernel(res_ref, out_hbm, sem):
    group, _, vector_count, _ = res_ref.shape
    for origin in range(group):
        pltpu.make_async_copy(
            res_ref.at[origin],
            out_hbm.at[0, :, :, pl.ds(origin * vector_count, vector_count)],
            sem,
        ).start()
    pltpu.make_async_copy(res_ref, res_ref, sem).wait()


def in_hbm(array):
    return pltpu.with_memory_space_constraint(array, pltpu.HBM)


def body(eigenvectors, perambulator, momenta, ratios, source_slice):
    color_count, site_count, vector_count = eigenvectors.shape[2:]
    group = lax.axis_size("space")
    normalizer = 1.0 / math.sqrt(color_count * site_count * group * vector_count)
    chunk_count = 4
    late_count = 128
    whole = (chunk_count, 2, vector_count // chunk_count, vector_count)
    bf16, f32 = jnp.bfloat16, jnp.float32
    smem = pl.BlockSpec(memory_space=pltpu.SMEM)
    vmem = pl.BlockSpec(memory_space=pltpu.VMEM)
    anywhere = pl.BlockSpec(memory_space=pl.ANY)
    dma = pltpu.SemaphoreType.DMA
    room = 4 * group * 2 * vector_count * vector_count
    result = pl.pallas_call(
        functools.partial(exchange_kernel, normalizer=normalizer),
        out_shape=pltpu.VMEM((group, 2, vector_count, vector_count), f32),
        in_specs=[anywhere, anywhere, smem, anywhere, anywhere],
        out_specs=vmem,
        scratch_shapes=[
            pltpu.SMEM(momenta.shape, jnp.int32),
            pltpu.SMEM(ratios.shape, jnp.int32),
            pltpu.VMEM(eigenvectors.shape[1:], bf16),
            pltpu.VMEM((vector_count, 4 * vector_count), f32),
            pltpu.VMEM((group, 2, vector_count, vector_count), bf16),
            pltpu.VMEM((2, vector_count, late_count), bf16),
            pltpu.VMEM(whole, f32),
            *[pltpu.VMEM(whole, bf16) for _ in range(8)],
            pltpu.VMEM((2 * vector_count, 2 * vector_count), bf16),
            pltpu.VMEM((2 * vector_count, 2 * vector_count), bf16),
            pltpu.VMEM((2 * late_count, 2 * vector_count), bf16),
            pltpu.VMEM((group, vector_count, 2 * vector_count), bf16),
            pltpu.VMEM((vector_count, 2 * late_count), bf16),
            pltpu.VMEM((vector_count, 2 * late_count), bf16),
            pltpu.VMEM((site_count, 128), f32),
            pltpu.VMEM((site_count, 128), f32),
            dma((5,)),
            dma((3,)),
            dma((18,)),
            dma((3,)),
            pltpu.SemaphoreType.REGULAR((5,)),
        ],
        compiler_params=pltpu.CompilerParams(
            collective_id=0,
            has_side_effects=True,
            vmem_limit_bytes=VMEM_BYTES - 3 * room,
        ),
        name="exchange",
    )(
        in_hbm(momenta),
        in_hbm(ratios),
        source_slice,
        in_hbm(eigenvectors),
        in_hbm(perambulator),
    )
    return pl.pallas_call(
        finish_kernel,
        out_shape=jax.ShapeDtypeStruct((1, 2, vector_count, group * vector_count), f32),
        in_specs=[vmem],
        out_specs=anywhere,
        scratch_shapes=[dma],
        compiler_params=pltpu.CompilerParams(vmem_limit_bytes=VMEM_BYTES // 2),
        name="finish",
    )(pltpu.with_memory_space_constraint(result, pltpu.VMEM))


def fits(mesh, eigenvectors, perambulator):
    space, slots = mesh.shape["space"], mesh.shape["tm"]
    vector_count = eigenvectors.shape[4]
    return (
        space == 4
        and slots == 4
        and eigenvectors.shape[0] == slots * mesh.shape["cfg"]
        and perambulator.shape[2] == space * vector_count
        and vector_count % 128 == 0
        and vector_count > 128
        and eigenvectors.shape[3] % (32 * space) == 0
    )


def solution(mesh):
    placed = (
        P(("cfg", "tm"), None, None, "space", None),
        P(("cfg", "tm"), None, None, "space"),
        P(),
        P(),
        P(),
    )

    def program(eigenvectors, perambulator, momenta, ratios, source_slice):
        chosen = body if fits(mesh, eigenvectors, perambulator) else general_body
        mapped = jax.shard_map(
            chosen,
            mesh=mesh,
            in_specs=placed,
            out_specs=P(("cfg", "tm"), None, "space", None),
            check_vma=False,
        )
        return mapped(eigenvectors, perambulator, momenta, ratios, source_slice)

    return program
```

```python
import functools
import math

import jax
import jax.numpy as jnp
from jax import lax
from jax.experimental import pallas as pl
from jax.experimental.pallas import tpu as pltpu
from jax.sharding import PartitionSpec as P

MESH = pl.DeviceIdType.MESH

LSIDE = 64

VMEM_BYTES = 67043328


def spread(value, axis, source):
    kept = jnp.where(lax.axis_index(axis) == source, value, 0).astype(value.dtype)
    return lax.psum(kept, axis)


def site_phases(momenta, first_site, site_count):
    site_index = first_site + lax.iota(jnp.int32, site_count)
    along_x = site_index % LSIDE
    along_y = site_index // LSIDE % LSIDE
    along_z = site_index // (LSIDE * LSIDE)
    turn_count = (
        momenta[:, 0:1] * along_x[None, :]
        + momenta[:, 1:2] * along_y[None, :]
        + momenta[:, 2:3] * along_z[None, :]
    )
    phase_angle = (turn_count % LSIDE).astype(jnp.float32) * (2.0 * math.pi / LSIDE)
    return (jnp.cos(phase_angle), jnp.sin(phase_angle))


def split_elementals(product, vector_count):
    lead_shape = product.shape[:-2]
    product_grid = product.reshape(lead_shape + (2, vector_count, 2, 2, vector_count))
    real_part = product_grid[..., 0, :, :, 0, :] + product_grid[..., 1, :, :, 1, :]
    imaginary = product_grid[..., 0, :, :, 1, :] - product_grid[..., 1, :, :, 0, :]
    stacked = jnp.stack([real_part, imaginary], axis=-4)
    return jnp.moveaxis(stacked, -2, -4)


def elementals(vectors, cosine, sine_part):
    slab_count, color_count, site_count, vector_count = (
        vectors.shape[0],
        vectors.shape[2],
        vectors.shape[3],
        vectors.shape[4],
    )
    row_count = color_count * site_count
    real_rows = vectors[:, 0].reshape(slab_count, row_count, vector_count)
    imaginary_rows = vectors[:, 1].reshape(slab_count, row_count, vector_count)
    cos_rows = jnp.broadcast_to(cosine[:, None, :], (2, color_count, site_count)).reshape(
        1, 2, row_count, 1
    )
    sin_rows = jnp.broadcast_to(sine_part[:, None, :], (2, color_count, site_count)).reshape(
        1, 2, row_count, 1
    )
    phased_real = (cos_rows * real_rows[:, None] + sin_rows * imaginary_rows[:, None]).astype(
        jnp.bfloat16
    )
    phased_imaginary = (cos_rows * imaginary_rows[:, None] - sin_rows * real_rows[:, None]).astype(
        jnp.bfloat16
    )
    phased = jnp.concatenate([phased_real, phased_imaginary], axis=3)
    phased = jnp.transpose(phased, (0, 2, 1, 3)).reshape(slab_count, row_count, 4 * vector_count)
    plain_vectors = jnp.concatenate([real_rows, imaginary_rows], axis=2)
    product = lax.dot_general(
        plain_vectors, phased, (((1,), (1,)), ((0,), (0,))), preferred_element_type=jnp.float32
    )
    return split_elementals(product, vector_count)


def source_block(chosen):
    real_t = chosen[0].T
    imaginary_t = chosen[1].T
    upper = jnp.concatenate([real_t, -imaginary_t], axis=1)
    lower = jnp.concatenate([imaginary_t, real_t], axis=1)
    return jnp.concatenate([upper, lower], axis=0)


def propagate(sink_matrix, tau):
    vector_count = sink_matrix.shape[1]
    spin_count = tau.shape[1] // vector_count
    column_count = tau.shape[2]
    real_part, imaginary = (sink_matrix[0], sink_matrix[1])
    upper = jnp.concatenate([real_part, -imaginary], axis=1)
    lower = jnp.concatenate([imaginary, real_part], axis=1)
    sink_big = jnp.concatenate([upper, lower], axis=0)
    stacked = jnp.transpose(tau.reshape(2, spin_count, vector_count, column_count), (0, 2, 1, 3))
    stacked = stacked.reshape(2 * vector_count, spin_count * column_count)
    product = jnp.dot(sink_big, stacked, preferred_element_type=jnp.float32)
    product = jnp.transpose(
        product.reshape(2, vector_count, spin_count, column_count), (0, 2, 1, 3)
    )
    return product.reshape(2, spin_count * vector_count, column_count).astype(jnp.bfloat16)


def attach_source(propagated, source_big):
    vector_count = source_big.shape[0] // 2
    row_count = propagated.shape[1]
    spin_count = propagated.shape[2] // vector_count
    stacked = jnp.concatenate(
        [
            propagated[0].reshape(row_count, spin_count, vector_count),
            propagated[1].reshape(row_count, spin_count, vector_count),
        ],
        axis=2,
    )
    product = jnp.dot(
        stacked.reshape(row_count * spin_count, 2 * vector_count),
        source_big,
        preferred_element_type=jnp.float32,
    )
    product = jnp.transpose(product.reshape(row_count, spin_count, 2, vector_count), (2, 0, 1, 3))
    return product.reshape(2, row_count, spin_count * vector_count)


def general_body(eigenvectors, perambulator, momenta, ratios, source_slice):
    slab_count = eigenvectors.shape[0]
    color_count = eigenvectors.shape[2]
    site_count = eigenvectors.shape[3]
    vector_count = eigenvectors.shape[4]
    first_site = lax.axis_index("space") * site_count
    cosine, sine_part = site_phases(momenta, first_site, site_count)
    normalizer = 1.0 / math.sqrt(color_count * site_count * lax.axis_size("space") * vector_count)
    weights = (
        ratios[:, 0].astype(jnp.float32) / ratios[:, 1].astype(jnp.float32) * normalizer
    ).reshape(1, 2, 1, 1, 1)
    parts = elementals(eigenvectors, cosine, sine_part)
    partial_sums = jnp.sum(weights * parts, axis=1, keepdims=True)
    summed = lax.psum(partial_sums, "space")
    sink_matrices = summed[:, 0].astype(jnp.bfloat16)
    global_slice = source_slice[0] % (slab_count * lax.axis_size("tm"))
    local_source = lax.dynamic_index_in_dim(
        sink_matrices, global_slice % slab_count, 0, keepdims=False
    )
    chosen = spread(local_source, "tm", global_slice // slab_count)
    source_big = source_block(chosen)
    propagated = jnp.stack([propagate(sink_matrices[0], perambulator[0])])
    return jnp.stack(
        [
            attach_source(
                lax.all_to_all(propagated, "space", split_axis=2, concat_axis=3, tiled=True)[0],
                source_big,
            )
        ]
    )


def block_dot(left, right, left_dim, right_dim):
    return lax.dot_general(
        left, right, (((left_dim,), (right_dim,)), ((), ())), preferred_element_type=jnp.float32
    )


def exchange_kernel(
    momenta_hbm,
    ratio_hbm,
    slice_ref,
    eig_hbm,
    tau_hbm,
    res_ref,
    momenta_ref,
    ratio_ref,
    eig,
    acc,
    tau,
    tau_mine,
    part,
    pair_out,
    pair_in,
    cross_out,
    cross_in,
    sink,
    sink_pair,
    picked,
    far,
    sink_big,
    source_big,
    source_late,
    prop,
    prop_out,
    prop_in,
    cosines,
    sines,
    own_sem,
    send,
    recv,
    spread_recv,
    ready,
    *,
    normalizer,
):
    vector_count = eig_hbm.shape[4]
    site_count = eig_hbm.shape[3]
    chunk_count, chunk_rows = part.shape[0], part.shape[2]
    color_count = eig.shape[1]
    site_step = site_count // 2
    steps_per_color = site_count // site_step
    step_count = color_count * steps_per_color
    late_count = tau_mine.shape[2]
    early_count = vector_count - late_count
    last_rows = vector_count // 12 // 32 * 32
    piece_rows = (vector_count - last_rows) // 3 // 32 * 32
    piece_ends = [piece_rows, 2 * piece_rows, vector_count - last_rows, vector_count]
    pieces = [pl.ds(a, b - a) for a, b in zip([0] + piece_ends, piece_ends) if b > a]
    piece_count = len(pieces)
    me = lax.axis_index("space")
    slot = lax.axis_index("tm")
    near = me + 1 - 2 * (me % 2)
    across = me + 2 - 4 * (me // 2)
    mirror = 3 - me
    inner = ((me + 1) // 2) % 2
    core = slot % 2
    core_peer = slot + 1 - 2 * core
    chip_peer = slot + 2 - 4 * (slot // 2)

    eig_copy = pltpu.make_async_copy(eig_hbm.at[0], eig, own_sem.at[4])
    own_copy = pltpu.make_async_copy(
        tau_hbm.at[0, :, pl.ds(me * vector_count, vector_count), :], tau.at[me], own_sem.at[0]
    )
    late_copy = pltpu.make_async_copy(
        tau_hbm.at[
            0, :, pl.ds(mirror * vector_count, vector_count), pl.ds(early_count, late_count)
        ],
        tau_mine,
        own_sem.at[1],
    )
    scalar_copies = [
        pltpu.make_async_copy(momenta_hbm, momenta_ref, own_sem.at[2]),
        pltpu.make_async_copy(ratio_hbm, ratio_ref, own_sem.at[3]),
    ]

    barrier = pltpu.get_barrier_semaphore()

    def hello(peer):
        pl.semaphore_signal(barrier, inc=1, device_id=peer, device_id_type=MESH)

    def hop(from_ref, to_ref, send_sem, recv_sem, peer):
        return pltpu.make_async_remote_copy(
            src_ref=from_ref,
            dst_ref=to_ref,
            send_sem=send_sem,
            recv_sem=recv_sem,
            device_id=peer,
            device_id_type=MESH,
        )

    def tau_copy(to, part_of, recv_index):
        return hop(
            tau_hbm.at[0, part_of, pl.ds(to * vector_count, vector_count), :],
            tau.at[me, part_of],
            send.at[0],
            recv.at[recv_index],
            {"space": to},
        )

    near_copies = [tau_copy(near, piece, 0) for piece in range(2)]
    near_whole = tau_copy(near, slice(None), 0)
    across_raw = tau_copy(across, slice(None), 6)
    across_copies = [tau_copy(across, piece, 11) for piece in range(2)]
    across_whole = tau_copy(across, slice(None), 11)
    mirror_copy = tau_copy(mirror, slice(None), 1)
    def early_copy(piece):
        first, count = early_rows[piece]
        return hop(
            tau_hbm.at[
                0, :, pl.ds(mirror * vector_count + first, count), pl.ds(0, early_count)
            ],
            tau.at[me, :, pl.ds(first, count), pl.ds(0, early_count)],
            send.at[1],
            recv.at[10],
            {"space": mirror},
        )

    lead = vector_count // 2 // 32 * 32
    early_rows = [(0, lead), (lead, 32), (lead + 32, vector_count - lead - 32)]
    early_copies = [early_copy(piece) for piece in range(3)]
    prop_copies = [
        hop(
            prop_out.at[pieces[p], :],
            prop_in.at[pieces[p], :],
            send.at[1],
            recv.at[12 + p],
            {"space": mirror},
        )
        for p in range(piece_count)
    ]

    def tell(index, peer):
        pl.semaphore_signal(ready.at[index], inc=1, device_id=peer, device_id_type=MESH)

    def phases():
        for copy in scalar_copies:
            copy.wait()
        lanes = cosines.shape[1]
        site = me * site_count + lax.broadcasted_iota(jnp.int32, (site_count, lanes), 0)
        first_lane = lax.broadcasted_iota(jnp.int32, (site_count, lanes), 1) == 0
        shift = LSIDE.bit_length() - 1
        places = (
            jnp.bitwise_and(site, LSIDE - 1),
            jnp.bitwise_and(jnp.right_shift(site, shift), LSIDE - 1),
            jnp.right_shift(site, 2 * shift),
        )
        turn = jnp.zeros_like(site)
        for axis in range(3):
            turn += jnp.where(first_lane, momenta_ref[0, axis], momenta_ref[1, axis]) * places[axis]
        angle = jnp.bitwise_and(turn, LSIDE - 1).astype(jnp.float32) * (2.0 * math.pi / LSIDE)
        cosines[...] = jnp.cos(angle)
        sines[...] = jnp.sin(angle)

    @pl.when(inner == 1)
    def _():
        hello({"space": mirror})
        hello({"space": near})
        pl.semaphore_wait(barrier, 1)
        early_copies[0].start()
        for copy in scalar_copies:
            copy.start()
        eig_copy.start()
        phases()
        pl.semaphore_wait(ready.at[0], 1)
        tell(1, {"space": mirror})
        near_copies[0].start()
        pl.semaphore_wait(ready.at[1], 1)
        across_raw.start()
        tell(2, {"space": near})
        late_copy.start()

    @pl.when(inner == 0)
    def _():
        hello({"tm": core_peer})
        hello({"tm": chip_peer})
        for copy in scalar_copies:
            copy.start()
        eig_copy.start()
        pl.semaphore_wait(barrier, 3)
        tell(0, {"space": near})
        near_copies[0].start()
        tell(0, {"tm": core_peer})
        tell(1, {"tm": chip_peer})
        phases()
        pl.semaphore_wait(ready.at[0], 1)
        pl.semaphore_wait(ready.at[1], 1)
        tell(3, {"space": near})

    own_copy.start()

    acc[...] = jnp.zeros_like(acc)

    eig_copy.wait()

    def accumulate(step, carry):
        color = step // steps_per_color
        rows = pl.ds(pl.multiple_of((step % steps_per_color) * site_step, site_step), site_step)
        plain_real, plain_imag = eig[0, color, rows, :], eig[1, color, rows, :]
        real = plain_real.astype(jnp.float32)
        imag = plain_imag.astype(jnp.float32)
        upper, lower = [], []
        for k in range(2):
            cosine = cosines[rows, k : k + 1]
            sine = sines[rows, k : k + 1]
            turned_real = (cosine * real + sine * imag).astype(jnp.bfloat16)
            turned_imag = (cosine * imag - sine * real).astype(jnp.bfloat16)
            upper += [turned_real, turned_imag]
            lower += [turned_imag, -turned_real]
        left = jnp.concatenate([plain_real, plain_imag], axis=0)
        right = jnp.concatenate(
            [jnp.concatenate(upper, axis=1), jnp.concatenate(lower, axis=1)], axis=0
        )
        acc[...] += block_dot(left, right, 0, 0)
        return carry

    lax.fori_loop(0, step_count, accumulate, 0, unroll=True)

    weights = [
        jnp.full((1, vector_count), ratio_ref[k, 0], jnp.int32).astype(jnp.float32)
        / jnp.full((1, vector_count), ratio_ref[k, 1], jnp.int32).astype(jnp.float32)
        * normalizer
        for k in range(2)
    ]

    def weighted(chunk, c):
        rows = pl.ds(chunk * chunk_rows, chunk_rows)
        return (
            weights[0] * acc[rows, c * vector_count : (c + 1) * vector_count]
            + weights[1] * acc[rows, (2 + c) * vector_count : (3 + c) * vector_count]
        )

    pair_hops = [
        hop(
            pair_out.at[q], pair_in.at[q], send.at[0], recv.at[2 + q], {"space": near}
        )
        for q in range(chunk_count)
    ]
    cross_hops = [
        hop(
            cross_out.at[q], cross_in.at[q], send.at[0], recv.at[6 + q], {"space": mirror}
        )
        for q in range(chunk_count)
    ]
    back_hops = [
        hop(sink.at[q], sink.at[q], send.at[0], recv.at[2 + q], {"space": near})
        for q in range(chunk_count)
    ]

    @pl.when(inner == 0)
    def _():
        for q in range(chunk_count):
            for c in range(2):
                pair_out[q, c] = weighted(q, c).astype(jnp.bfloat16)
            pair_hops[q].start()
        near_copies[1].start()
        pl.semaphore_wait(ready.at[2], 1)
        for q in range(chunk_count // 2):
            back_hops[q].wait_recv()
        tell(4, {"tm": core_peer})
        pl.semaphore_wait(ready.at[4], 1)
        across_copies[0].start()
        mirror_copy.start()
        across_copies[1].start()
        for q in range(chunk_count // 2, chunk_count):
            back_hops[q].wait_recv()

    @pl.when(inner == 1)
    def _():
        for q in range(chunk_count):
            for c in range(2):
                part[q, c] = weighted(q, c)

        def forward(q):
            pair_hops[q].wait_recv()
            part[q] = part[q] + pair_in[q].astype(jnp.float32)
            cross_out[q] = part[q].astype(jnp.bfloat16)
            cross_hops[q].start()

        def settle(q):
            cross_hops[q].wait_recv()
            sink[q] = (part[q] + cross_in[q].astype(jnp.float32)).astype(jnp.bfloat16)
            back_hops[q].start()

        for q in range(chunk_count):
            forward(q)
            if q == chunk_count - 1:
                early_copies[1].start()
                pl.when(core == 0)(early_copies[2].start)
            if q > 1:
                settle(q - 2)
        for q in range(chunk_count - 2, chunk_count):
            settle(q)
        pl.when(core == 1)(early_copies[2].start)
        near_copies[1].start()
        pl.semaphore_wait(ready.at[3], 1)

    core_hop = hop(sink, sink_pair, send.at[2], spread_recv.at[0], {"tm": core_peer})
    core_hop.start()
    for q in range(chunk_count):
        rows = pl.ds(q * chunk_rows, chunk_rows)
        low = pl.ds(vector_count + q * chunk_rows, chunk_rows)
        real, imag = sink[q, 0], sink[q, 1]
        sink_big[rows, :vector_count] = real
        sink_big[rows, vector_count:] = -imag
        sink_big[low, :vector_count] = imag
        sink_big[low, vector_count:] = real

    def carried(block):
        stacked = block.reshape(2 * vector_count, block.shape[2])
        product = block_dot(sink_big[...], stacked, 1, 0).astype(jnp.bfloat16)
        return product[:vector_count], product[vector_count:]

    def left_multiply(origin):
        real, imag = carried(tau[origin])
        prop[origin, :, :vector_count] = real
        prop[origin, :, vector_count:] = imag

    def right_multiply(origin):
        product = block_dot(prop[origin], source_big[...], 1, 1)
        res_ref[origin, 0] = product[:, :vector_count]
        res_ref[origin, 1] = product[:, vector_count:]

    @pl.when(inner == 1)
    def _():
        late_copy.wait()
        real, imag = carried(tau_mine[...])
        prop_out[:, :late_count] = real
        prop_out[:, late_count:] = imag
        for copy in prop_copies:
            copy.start()

    core_hop.wait_recv()
    chosen_slot = slice_ref[0] % lax.axis_size("tm")
    picked[...] = jnp.where(chosen_slot == slot, sink[...], sink_pair[...])
    half = pl.ds(core * (chunk_count // 2), chunk_count // 2)
    chip_hop = hop(
        picked.at[half], far.at[half], send.at[2], spread_recv.at[1], {"tm": chip_peer}
    )
    chip_hop.start()

    own_copy.wait()
    left_multiply(me)

    @pl.when(inner == 1)
    def _():
        near_whole.wait_recv()
        left_multiply(near)

    @pl.when(inner == 0)
    def _():
        across_raw.wait_recv()
        left_multiply(across)

    chip_hop.wait_recv()
    forward_hop = hop(
        far.at[half], far.at[half], send.at[2], spread_recv.at[2], {"tm": core_peer}
    )
    forward_hop.start()
    forward_hop.wait_recv()
    chosen = jnp.where(chosen_slot // 2 == slot // 2, picked[...], far[...])
    for q in range(chunk_count):
        rows = pl.ds(q * chunk_rows, chunk_rows)
        low = pl.ds(vector_count + q * chunk_rows, chunk_rows)
        source_big[rows, :vector_count] = chosen[q, 0]
        source_big[rows, vector_count:] = chosen[q, 1]
        source_big[low, :vector_count] = -chosen[q, 1]
        source_big[low, vector_count:] = chosen[q, 0]
    right_multiply(me)

    @pl.when(inner == 0)
    def _():
        right_multiply(across)
        for origin, copy in ((near, near_whole), (mirror, mirror_copy)):
            copy.wait_recv()
            left_multiply(origin)
            right_multiply(origin)

    @pl.when(inner == 1)
    def _():
        right_multiply(near)
        across_whole.wait_recv()
        left_multiply(across)
        right_multiply(across)
        landed = tau.at[mirror, :, :, pl.ds(0, early_count)]
        hop(landed, landed, send.at[1], recv.at[10], {"space": mirror}).wait_recv()
        both = jnp.concatenate(carried(tau[mirror, :, :, :early_count]), axis=1)
        source_early = jnp.concatenate(
            [
                source_big[:, :early_count],
                source_big[:, vector_count : vector_count + early_count],
            ],
            axis=1,
        )
        product = block_dot(both, source_early, 1, 1)
        res_ref[mirror, 0] = product[:, :vector_count]
        res_ref[mirror, 1] = product[:, vector_count:]
        source_late[:late_count] = source_big[:, early_count:vector_count].T
        source_late[late_count:] = source_big[:, vector_count + early_count :].T

        def add_piece(p):
            rows = pieces[p]
            prop_copies[p].wait_recv()
            product = block_dot(prop_in[rows, :], source_late[...], 1, 0)
            res_ref[mirror, 0, rows, :] += product[:, :vector_count]
            res_ref[mirror, 1, rows, :] += product[:, vector_count:]

        for p in range(piece_count):
            add_piece(p)
        hop(sink, sink, send.at[1], recv.at[0], {"space": near}).wait_send()

    hop(tau, tau, send.at[0], recv.at[0], {"space": near}).wait_send()
    pair = pl.ds(0, 2)
    hop(tau.at[pair], tau.at[pair], send.at[2], recv.at[0], {"space": near}).wait_send()


def finish_kernel(res_ref, out_hbm, sem):
    group, _, vector_count, _ = res_ref.shape
    for origin in range(group):
        pltpu.make_async_copy(
            res_ref.at[origin],
            out_hbm.at[0, :, :, pl.ds(origin * vector_count, vector_count)],
            sem,
        ).start()
    pltpu.make_async_copy(res_ref, res_ref, sem).wait()


def in_hbm(array):
    return pltpu.with_memory_space_constraint(array, pltpu.HBM)


def body(eigenvectors, perambulator, momenta, ratios, source_slice):
    color_count, site_count, vector_count = eigenvectors.shape[2:]
    group = lax.axis_size("space")
    normalizer = 1.0 / math.sqrt(color_count * site_count * group * vector_count)
    chunk_count = 4
    late_count = 128
    whole = (chunk_count, 2, vector_count // chunk_count, vector_count)
    bf16, f32 = jnp.bfloat16, jnp.float32
    smem = pl.BlockSpec(memory_space=pltpu.SMEM)
    vmem = pl.BlockSpec(memory_space=pltpu.VMEM)
    anywhere = pl.BlockSpec(memory_space=pl.ANY)
    dma = pltpu.SemaphoreType.DMA
    room = 4 * group * 2 * vector_count * vector_count
    result = pl.pallas_call(
        functools.partial(exchange_kernel, normalizer=normalizer),
        out_shape=pltpu.VMEM((group, 2, vector_count, vector_count), f32),
        in_specs=[anywhere, anywhere, smem, anywhere, anywhere],
        out_specs=vmem,
        scratch_shapes=[
            pltpu.SMEM(momenta.shape, jnp.int32),
            pltpu.SMEM(ratios.shape, jnp.int32),
            pltpu.VMEM(eigenvectors.shape[1:], bf16),
            pltpu.VMEM((vector_count, 4 * vector_count), f32),
            pltpu.VMEM((group, 2, vector_count, vector_count), bf16),
            pltpu.VMEM((2, vector_count, late_count), bf16),
            pltpu.VMEM(whole, f32),
            *[pltpu.VMEM(whole, bf16) for _ in range(8)],
            pltpu.VMEM((2 * vector_count, 2 * vector_count), bf16),
            pltpu.VMEM((2 * vector_count, 2 * vector_count), bf16),
            pltpu.VMEM((2 * late_count, 2 * vector_count), bf16),
            pltpu.VMEM((group, vector_count, 2 * vector_count), bf16),
            pltpu.VMEM((vector_count, 2 * late_count), bf16),
            pltpu.VMEM((vector_count, 2 * late_count), bf16),
            pltpu.VMEM((site_count, 128), f32),
            pltpu.VMEM((site_count, 128), f32),
            dma((5,)),
            dma((3,)),
            dma((16,)),
            dma((3,)),
            pltpu.SemaphoreType.REGULAR((5,)),
        ],
        compiler_params=pltpu.CompilerParams(
            collective_id=0,
            has_side_effects=True,
            vmem_limit_bytes=VMEM_BYTES - 3 * room,
        ),
        name="exchange",
    )(
        in_hbm(momenta),
        in_hbm(ratios),
        source_slice,
        in_hbm(eigenvectors),
        in_hbm(perambulator),
    )
    return pl.pallas_call(
        finish_kernel,
        out_shape=jax.ShapeDtypeStruct((1, 2, vector_count, group * vector_count), f32),
        in_specs=[vmem],
        out_specs=anywhere,
        scratch_shapes=[dma],
        compiler_params=pltpu.CompilerParams(vmem_limit_bytes=VMEM_BYTES // 2),
        name="finish",
    )(pltpu.with_memory_space_constraint(result, pltpu.VMEM))


def fits(mesh, eigenvectors, perambulator):
    space, slots = mesh.shape["space"], mesh.shape["tm"]
    vector_count = eigenvectors.shape[4]
    return (
        space == 4
        and slots == 4
        and eigenvectors.shape[0] == slots * mesh.shape["cfg"]
        and perambulator.shape[2] == space * vector_count
        and vector_count % 128 == 0
        and vector_count > 128
        and eigenvectors.shape[3] % (32 * space) == 0
    )


def solution(mesh):
    placed = (
        P(("cfg", "tm"), None, None, "space", None),
        P(("cfg", "tm"), None, None, "space"),
        P(),
        P(),
        P(),
    )

    def program(eigenvectors, perambulator, momenta, ratios, source_slice):
        chosen = body if fits(mesh, eigenvectors, perambulator) else general_body
        mapped = jax.shard_map(
            chosen,
            mesh=mesh,
            in_specs=placed,
            out_specs=P(("cfg", "tm"), None, "space", None),
            check_vma=False,
        )
        return mapped(eigenvectors, perambulator, momenta, ratios, source_slice)

    return program
```

```python
import functools
import math

import jax
import jax.numpy as jnp
from jax import lax
from jax.experimental import pallas as pl
from jax.experimental.pallas import tpu as pltpu
from jax.sharding import PartitionSpec as P

MESH = pl.DeviceIdType.MESH

LSIDE = 64

VMEM_BYTES = 67043328


def spread(value, axis, source):
    kept = jnp.where(lax.axis_index(axis) == source, value, 0).astype(value.dtype)
    return lax.psum(kept, axis)


def site_phases(momenta, first_site, site_count):
    site_index = first_site + lax.iota(jnp.int32, site_count)
    along_x = site_index % LSIDE
    along_y = site_index // LSIDE % LSIDE
    along_z = site_index // (LSIDE * LSIDE)
    turn_count = (
        momenta[:, 0:1] * along_x[None, :]
        + momenta[:, 1:2] * along_y[None, :]
        + momenta[:, 2:3] * along_z[None, :]
    )
    phase_angle = (turn_count % LSIDE).astype(jnp.float32) * (2.0 * math.pi / LSIDE)
    return (jnp.cos(phase_angle), jnp.sin(phase_angle))


def split_elementals(product, vector_count):
    lead_shape = product.shape[:-2]
    product_grid = product.reshape(lead_shape + (2, vector_count, 2, 2, vector_count))
    real_part = product_grid[..., 0, :, :, 0, :] + product_grid[..., 1, :, :, 1, :]
    imaginary = product_grid[..., 0, :, :, 1, :] - product_grid[..., 1, :, :, 0, :]
    stacked = jnp.stack([real_part, imaginary], axis=-4)
    return jnp.moveaxis(stacked, -2, -4)


def elementals(vectors, cosine, sine_part):
    slab_count, color_count, site_count, vector_count = (
        vectors.shape[0],
        vectors.shape[2],
        vectors.shape[3],
        vectors.shape[4],
    )
    row_count = color_count * site_count
    real_rows = vectors[:, 0].reshape(slab_count, row_count, vector_count)
    imaginary_rows = vectors[:, 1].reshape(slab_count, row_count, vector_count)
    cos_rows = jnp.broadcast_to(cosine[:, None, :], (2, color_count, site_count)).reshape(
        1, 2, row_count, 1
    )
    sin_rows = jnp.broadcast_to(sine_part[:, None, :], (2, color_count, site_count)).reshape(
        1, 2, row_count, 1
    )
    phased_real = (cos_rows * real_rows[:, None] + sin_rows * imaginary_rows[:, None]).astype(
        jnp.bfloat16
    )
    phased_imaginary = (cos_rows * imaginary_rows[:, None] - sin_rows * real_rows[:, None]).astype(
        jnp.bfloat16
    )
    phased = jnp.concatenate([phased_real, phased_imaginary], axis=3)
    phased = jnp.transpose(phased, (0, 2, 1, 3)).reshape(slab_count, row_count, 4 * vector_count)
    plain_vectors = jnp.concatenate([real_rows, imaginary_rows], axis=2)
    product = lax.dot_general(
        plain_vectors, phased, (((1,), (1,)), ((0,), (0,))), preferred_element_type=jnp.float32
    )
    return split_elementals(product, vector_count)


def source_block(chosen):
    real_t = chosen[0].T
    imaginary_t = chosen[1].T
    upper = jnp.concatenate([real_t, -imaginary_t], axis=1)
    lower = jnp.concatenate([imaginary_t, real_t], axis=1)
    return jnp.concatenate([upper, lower], axis=0)


def propagate(sink_matrix, tau):
    vector_count = sink_matrix.shape[1]
    spin_count = tau.shape[1] // vector_count
    column_count = tau.shape[2]
    real_part, imaginary = (sink_matrix[0], sink_matrix[1])
    upper = jnp.concatenate([real_part, -imaginary], axis=1)
    lower = jnp.concatenate([imaginary, real_part], axis=1)
    sink_big = jnp.concatenate([upper, lower], axis=0)
    stacked = jnp.transpose(tau.reshape(2, spin_count, vector_count, column_count), (0, 2, 1, 3))
    stacked = stacked.reshape(2 * vector_count, spin_count * column_count)
    product = jnp.dot(sink_big, stacked, preferred_element_type=jnp.float32)
    product = jnp.transpose(
        product.reshape(2, vector_count, spin_count, column_count), (0, 2, 1, 3)
    )
    return product.reshape(2, spin_count * vector_count, column_count).astype(jnp.bfloat16)


def attach_source(propagated, source_big):
    vector_count = source_big.shape[0] // 2
    row_count = propagated.shape[1]
    spin_count = propagated.shape[2] // vector_count
    stacked = jnp.concatenate(
        [
            propagated[0].reshape(row_count, spin_count, vector_count),
            propagated[1].reshape(row_count, spin_count, vector_count),
        ],
        axis=2,
    )
    product = jnp.dot(
        stacked.reshape(row_count * spin_count, 2 * vector_count),
        source_big,
        preferred_element_type=jnp.float32,
    )
    product = jnp.transpose(product.reshape(row_count, spin_count, 2, vector_count), (2, 0, 1, 3))
    return product.reshape(2, row_count, spin_count * vector_count)


def general_body(eigenvectors, perambulator, momenta, ratios, source_slice):
    slab_count = eigenvectors.shape[0]
    color_count = eigenvectors.shape[2]
    site_count = eigenvectors.shape[3]
    vector_count = eigenvectors.shape[4]
    first_site = lax.axis_index("space") * site_count
    cosine, sine_part = site_phases(momenta, first_site, site_count)
    normalizer = 1.0 / math.sqrt(color_count * site_count * lax.axis_size("space") * vector_count)
    weights = (
        ratios[:, 0].astype(jnp.float32) / ratios[:, 1].astype(jnp.float32) * normalizer
    ).reshape(1, 2, 1, 1, 1)
    parts = elementals(eigenvectors, cosine, sine_part)
    partial_sums = jnp.sum(weights * parts, axis=1, keepdims=True)
    summed = lax.psum(partial_sums, "space")
    sink_matrices = summed[:, 0].astype(jnp.bfloat16)
    global_slice = source_slice[0] % (slab_count * lax.axis_size("tm"))
    local_source = lax.dynamic_index_in_dim(
        sink_matrices, global_slice % slab_count, 0, keepdims=False
    )
    chosen = spread(local_source, "tm", global_slice // slab_count)
    source_big = source_block(chosen)
    propagated = jnp.stack([propagate(sink_matrices[0], perambulator[0])])
    return jnp.stack(
        [
            attach_source(
                lax.all_to_all(propagated, "space", split_axis=2, concat_axis=3, tiled=True)[0],
                source_big,
            )
        ]
    )


def block_dot(left, right, left_dim, right_dim):
    return lax.dot_general(
        left, right, (((left_dim,), (right_dim,)), ((), ())), preferred_element_type=jnp.float32
    )


def exchange_kernel(
    momenta_hbm,
    ratio_hbm,
    slice_hbm,
    eig_hbm,
    tau_hbm,
    res_ref,
    prop_in,
    source_late,
    momenta_ref,
    ratio_ref,
    slice_ref,
    eig,
    acc,
    tau,
    tau_mine,
    part,
    pair_out,
    pair_in,
    cross_out,
    cross_in,
    sink,
    sink_pair,
    picked,
    far,
    sink_big,
    source_big,
    prop,
    prop_out,
    cosines,
    sines,
    own_sem,
    send,
    recv,
    spread_recv,
    ready,
    *,
    normalizer,
):
    vector_count = eig_hbm.shape[4]
    site_count = eig_hbm.shape[3]
    chunk_count, chunk_rows = part.shape[0], part.shape[2]
    color_count = eig.shape[1]
    site_step = site_count // 2
    steps_per_color = site_count // site_step
    step_count = color_count * steps_per_color
    late_count = tau_mine.shape[2]
    early_count = vector_count - late_count
    last_rows = tail_rows(vector_count)
    piece_rows = (vector_count - last_rows) // 3 // 32 * 32
    piece_ends = [piece_rows, 2 * piece_rows, vector_count - last_rows, vector_count]
    pieces = [pl.ds(a, b - a) for a, b in zip([0] + piece_ends, piece_ends) if b > a]
    piece_count = len(pieces)
    me = lax.axis_index("space")
    slot = lax.axis_index("tm")
    near = me + 1 - 2 * (me % 2)
    across = me + 2 - 4 * (me // 2)
    mirror = 3 - me
    inner = ((me + 1) // 2) % 2
    core = slot % 2
    core_peer = slot + 1 - 2 * core
    chip_peer = slot + 2 - 4 * (slot // 2)

    eig_copy = pltpu.make_async_copy(eig_hbm.at[0], eig, own_sem.at[4])
    own_copy = pltpu.make_async_copy(
        tau_hbm.at[0, :, pl.ds(me * vector_count, vector_count), :], tau.at[me], own_sem.at[0]
    )
    late_copy = pltpu.make_async_copy(
        tau_hbm.at[
            0, :, pl.ds(mirror * vector_count, vector_count), pl.ds(early_count, late_count)
        ],
        tau_mine,
        own_sem.at[1],
    )
    scalar_copies = [
        pltpu.make_async_copy(momenta_hbm, momenta_ref, own_sem.at[2]),
        pltpu.make_async_copy(ratio_hbm, ratio_ref, own_sem.at[3]),
        pltpu.make_async_copy(slice_hbm, slice_ref, own_sem.at[5]),
    ]

    barrier = pltpu.get_barrier_semaphore()

    def hello(peer):
        pl.semaphore_signal(barrier, inc=1, device_id=peer, device_id_type=MESH)

    def hop(from_ref, to_ref, send_sem, recv_sem, peer):
        return pltpu.make_async_remote_copy(
            src_ref=from_ref,
            dst_ref=to_ref,
            send_sem=send_sem,
            recv_sem=recv_sem,
            device_id=peer,
            device_id_type=MESH,
        )

    def tau_copy(to, part_of, recv_index):
        return hop(
            tau_hbm.at[0, part_of, pl.ds(to * vector_count, vector_count), :],
            tau.at[me, part_of],
            send.at[0],
            recv.at[recv_index],
            {"space": to},
        )

    near_copies = [tau_copy(near, piece, 0) for piece in range(2)]
    near_whole = tau_copy(near, slice(None), 0)
    across_raw = tau_copy(across, slice(None), 6)
    across_copies = [tau_copy(across, piece, 11) for piece in range(2)]
    across_whole = tau_copy(across, slice(None), 11)
    mirror_copy = tau_copy(mirror, slice(None), 1)
    def early_copy(piece):
        first, count = early_rows[piece]
        return hop(
            tau_hbm.at[
                0, :, pl.ds(mirror * vector_count + first, count), pl.ds(0, early_count)
            ],
            tau.at[me, :, pl.ds(first, count), pl.ds(0, early_count)],
            send.at[1],
            recv.at[10],
            {"space": mirror},
        )

    lead = vector_count // 2 // 32 * 32
    early_ends = [lead, lead + lead // 3 // 32 * 32, vector_count]
    early_rows = [(a, b - a) for a, b in zip([0] + early_ends, early_ends)]
    early_copies = [early_copy(piece) for piece in range(3)]
    prop_copies = [
        hop(
            prop_out.at[pieces[p], :],
            prop_in.at[pieces[p], :],
            send.at[1],
            recv.at[12 + p],
            {"space": mirror},
        )
        for p in range(piece_count)
    ]

    def tell(index, peer):
        pl.semaphore_signal(ready.at[index], inc=1, device_id=peer, device_id_type=MESH)

    def phases():
        for copy in scalar_copies:
            copy.wait()
        lanes = cosines.shape[1]
        site = me * site_count + lax.broadcasted_iota(jnp.int32, (site_count, lanes), 0)
        first_lane = lax.broadcasted_iota(jnp.int32, (site_count, lanes), 1) == 0
        shift = LSIDE.bit_length() - 1
        places = (
            jnp.bitwise_and(site, LSIDE - 1),
            jnp.bitwise_and(jnp.right_shift(site, shift), LSIDE - 1),
            jnp.right_shift(site, 2 * shift),
        )
        turn = jnp.zeros_like(site)
        for axis in range(3):
            turn += jnp.where(first_lane, momenta_ref[0, axis], momenta_ref[1, axis]) * places[axis]
        angle = jnp.bitwise_and(turn, LSIDE - 1).astype(jnp.float32) * (2.0 * math.pi / LSIDE)
        cosines[...] = jnp.cos(angle)
        sines[...] = jnp.sin(angle)

    @pl.when(inner == 1)
    def _():
        hello({"space": mirror})
        hello({"space": near})
        pl.semaphore_wait(barrier, 1)
        early_copies[0].start()
        for copy in scalar_copies:
            copy.start()
        eig_copy.start()
        phases()
        pl.semaphore_wait(ready.at[0], 1)
        tell(1, {"space": mirror})
        near_copies[0].start()
        pl.semaphore_wait(ready.at[1], 1)
        across_raw.start()
        tell(2, {"space": near})
        late_copy.start()

    @pl.when(inner == 0)
    def _():
        hello({"tm": core_peer})
        hello({"tm": chip_peer})
        for copy in scalar_copies:
            copy.start()
        eig_copy.start()
        pl.semaphore_wait(barrier, 3)
        tell(0, {"space": near})
        near_copies[0].start()
        tell(0, {"tm": core_peer})
        tell(1, {"tm": chip_peer})
        phases()
        pl.semaphore_wait(ready.at[0], 1)
        pl.semaphore_wait(ready.at[1], 1)
        tell(3, {"space": near})

    own_copy.start()

    acc[...] = jnp.zeros_like(acc)

    eig_copy.wait()

    def accumulate(step, carry):
        color = step // steps_per_color
        rows = pl.ds(pl.multiple_of((step % steps_per_color) * site_step, site_step), site_step)
        plain_real, plain_imag = eig[0, color, rows, :], eig[1, color, rows, :]
        real = plain_real.astype(jnp.float32)
        imag = plain_imag.astype(jnp.float32)
        upper, lower = [], []
        for k in range(2):
            cosine = cosines[rows, k : k + 1]
            sine = sines[rows, k : k + 1]
            turned_real = (cosine * real + sine * imag).astype(jnp.bfloat16)
            turned_imag = (cosine * imag - sine * real).astype(jnp.bfloat16)
            upper += [turned_real, turned_imag]
            lower += [turned_imag, -turned_real]
        left = jnp.concatenate([plain_real, plain_imag], axis=0)
        right = jnp.concatenate(
            [jnp.concatenate(upper, axis=1), jnp.concatenate(lower, axis=1)], axis=0
        )
        acc[...] += block_dot(left, right, 0, 0)
        return carry

    lax.fori_loop(0, step_count, accumulate, 0, unroll=True)

    weights = [
        jnp.full((1, vector_count), ratio_ref[k, 0], jnp.int32).astype(jnp.float32)
        / jnp.full((1, vector_count), ratio_ref[k, 1], jnp.int32).astype(jnp.float32)
        * normalizer
        for k in range(2)
    ]

    def weighted(chunk, c):
        rows = pl.ds(chunk * chunk_rows, chunk_rows)
        return (
            weights[0] * acc[rows, c * vector_count : (c + 1) * vector_count]
            + weights[1] * acc[rows, (2 + c) * vector_count : (3 + c) * vector_count]
        )

    pair_hops = [
        hop(
            pair_out.at[q], pair_in.at[q], send.at[0], recv.at[2 + q], {"space": near}
        )
        for q in range(chunk_count)
    ]
    cross_hops = [
        hop(
            cross_out.at[q], cross_in.at[q], send.at[0], recv.at[6 + q], {"space": mirror}
        )
        for q in range(chunk_count)
    ]
    back_hops = [
        hop(sink.at[q], sink.at[q], send.at[0], recv.at[2 + q], {"space": near})
        for q in range(chunk_count)
    ]

    @pl.when(inner == 0)
    def _():
        for q in range(chunk_count):
            for c in range(2):
                pair_out[q, c] = weighted(q, c).astype(jnp.bfloat16)
            pair_hops[q].start()
        near_copies[1].start()
        pl.semaphore_wait(ready.at[2], 1)
        for q in range(chunk_count // 2):
            back_hops[q].wait_recv()
        tell(4, {"tm": core_peer})
        pl.semaphore_wait(ready.at[4], 1)
        across_copies[0].start()
        mirror_copy.start()
        across_copies[1].start()
        for q in range(chunk_count // 2, chunk_count):
            back_hops[q].wait_recv()

    @pl.when(inner == 1)
    def _():
        for q in range(chunk_count):
            for c in range(2):
                part[q, c] = weighted(q, c)

        def forward(q):
            pair_hops[q].wait_recv()
            part[q] = part[q] + pair_in[q].astype(jnp.float32)
            cross_out[q] = part[q].astype(jnp.bfloat16)
            cross_hops[q].start()

        def settle(q):
            cross_hops[q].wait_recv()
            sink[q] = (part[q] + cross_in[q].astype(jnp.float32)).astype(jnp.bfloat16)
            back_hops[q].start()

        for q in range(chunk_count):
            forward(q)
            if q == chunk_count - 1:
                early_copies[1].start()
                pl.when(core == 0)(early_copies[2].start)
            if q > 1:
                settle(q - 2)
        for q in range(chunk_count - 2, chunk_count):
            settle(q)
        pl.when(core == 1)(early_copies[2].start)
        near_copies[1].start()
        pl.semaphore_wait(ready.at[3], 1)

    core_hop = hop(sink, sink_pair, send.at[2], spread_recv.at[0], {"tm": core_peer})
    core_hop.start()
    for q in range(chunk_count):
        rows = pl.ds(q * chunk_rows, chunk_rows)
        low = pl.ds(vector_count + q * chunk_rows, chunk_rows)
        real, imag = sink[q, 0], sink[q, 1]
        sink_big[rows, :vector_count] = real
        sink_big[rows, vector_count:] = -imag
        sink_big[low, :vector_count] = imag
        sink_big[low, vector_count:] = real

    def carried(block):
        stacked = block.reshape(2 * vector_count, block.shape[2])
        product = block_dot(sink_big[...], stacked, 1, 0).astype(jnp.bfloat16)
        return product[:vector_count], product[vector_count:]

    def left_multiply(origin):
        real, imag = carried(tau[origin])
        prop[origin, :, :vector_count] = real
        prop[origin, :, vector_count:] = imag

    def right_multiply(origin):
        product = block_dot(prop[origin], source_big[...], 1, 1)
        res_ref[origin, 0] = product[:, :vector_count]
        res_ref[origin, 1] = product[:, vector_count:]

    @pl.when(inner == 1)
    def _():
        late_copy.wait()
        real, imag = carried(tau_mine[...])
        prop_out[:, :late_count] = real
        prop_out[:, late_count:] = imag
        for copy in prop_copies:
            copy.start()

    core_hop.wait_recv()
    chosen_slot = slice_ref[0] % lax.axis_size("tm")
    picked[...] = jnp.where(chosen_slot == slot, sink[...], sink_pair[...])
    half = pl.ds(core * (chunk_count // 2), chunk_count // 2)
    chip_hop = hop(
        picked.at[half], far.at[half], send.at[2], spread_recv.at[1], {"tm": chip_peer}
    )
    chip_hop.start()

    own_copy.wait()
    left_multiply(me)

    @pl.when(inner == 1)
    def _():
        near_whole.wait_recv()
        left_multiply(near)

    @pl.when(inner == 0)
    def _():
        across_raw.wait_recv()
        left_multiply(across)

    chip_hop.wait_recv()
    forward_hop = hop(
        far.at[half], far.at[half], send.at[2], spread_recv.at[2], {"tm": core_peer}
    )
    forward_hop.start()
    forward_hop.wait_recv()
    chosen = jnp.where(chosen_slot // 2 == slot // 2, picked[...], far[...])
    for q in range(chunk_count):
        rows = pl.ds(q * chunk_rows, chunk_rows)
        low = pl.ds(vector_count + q * chunk_rows, chunk_rows)
        source_big[rows, :vector_count] = chosen[q, 0]
        source_big[rows, vector_count:] = chosen[q, 1]
        source_big[low, :vector_count] = -chosen[q, 1]
        source_big[low, vector_count:] = chosen[q, 0]
    right_multiply(me)

    @pl.when(inner == 0)
    def _():
        right_multiply(across)
        for origin, copy in ((near, near_whole), (mirror, mirror_copy)):
            copy.wait_recv()
            left_multiply(origin)
            right_multiply(origin)

    @pl.when(inner == 1)
    def _():
        right_multiply(near)
        across_whole.wait_recv()
        left_multiply(across)
        right_multiply(across)
        landed = tau.at[mirror, :, :, pl.ds(0, early_count)]
        hop(landed, landed, send.at[1], recv.at[10], {"space": mirror}).wait_recv()
        both = jnp.concatenate(carried(tau[mirror, :, :, :early_count]), axis=1)
        source_early = jnp.concatenate(
            [
                source_big[:, :early_count],
                source_big[:, vector_count : vector_count + early_count],
            ],
            axis=1,
        )
        product = block_dot(both, source_early, 1, 1)
        res_ref[mirror, 0] = product[:, :vector_count]
        res_ref[mirror, 1] = product[:, vector_count:]
        source_late[:late_count] = source_big[:, early_count:vector_count].T
        source_late[late_count:] = source_big[:, vector_count + early_count :].T

        def add_piece(p):
            rows = pieces[p]
            prop_copies[p].wait_recv()
            product = block_dot(prop_in[rows, :], source_late[...], 1, 0)
            res_ref[mirror, 0, rows, :] += product[:, :vector_count]
            res_ref[mirror, 1, rows, :] += product[:, vector_count:]

        for p in range(piece_count - 1):
            add_piece(p)
        prop_copies[-1].wait_recv()
        hop(sink, sink, send.at[1], recv.at[0], {"space": near}).wait_send()

    hop(tau, tau, send.at[0], recv.at[0], {"space": near}).wait_send()
    pair = pl.ds(0, 2)
    hop(tau.at[pair], tau.at[pair], send.at[2], recv.at[0], {"space": near}).wait_send()


def finish_kernel(res_ref, prop_ref, source_ref, out_hbm, last, sem):
    group, _, vector_count, _ = res_ref.shape
    last_rows = last.shape[1]
    body_rows = pl.ds(0, vector_count - last_rows)
    tail = pl.ds(vector_count - last_rows, last_rows)
    me = lax.axis_index("space")
    mirror = group - 1 - me
    inner = ((me + 1) // 2) % 2

    def put(source, origin, rows):
        columns = pl.ds(origin * vector_count, vector_count)
        pltpu.make_async_copy(source, out_hbm.at[0, :, rows, columns], sem).start()

    for origin in range(group):
        put(res_ref.at[origin, :, body_rows, :], origin, body_rows)

    @pl.when(inner == 1)
    def _():
        product = block_dot(prop_ref[tail, :], source_ref[...], 1, 0)
        last[0] = res_ref[mirror, 0, tail, :] + product[:, :vector_count]
        last[1] = res_ref[mirror, 1, tail, :] + product[:, vector_count:]

    for origin in range(group):
        late = jnp.logical_and(inner == 1, mirror == origin)
        pl.when(late)(functools.partial(put, last, origin, tail))
        pl.when(jnp.logical_not(late))(
            functools.partial(put, res_ref.at[origin, :, tail, :], origin, tail)
        )
    pltpu.make_async_copy(res_ref, res_ref, sem).wait()


def tail_rows(vector_count):
    return vector_count // 12 // 32 * 32


def in_hbm(array):
    return pltpu.with_memory_space_constraint(array, pltpu.HBM)


def both_kernels(eigenvectors, perambulator, momenta, ratios, source_slice):
    color_count, site_count, vector_count = eigenvectors.shape[2:]
    group = lax.axis_size("space")
    normalizer = 1.0 / math.sqrt(color_count * site_count * group * vector_count)
    chunk_count = 4
    late_count = 128
    whole = (chunk_count, 2, vector_count // chunk_count, vector_count)
    bf16, f32 = jnp.bfloat16, jnp.float32
    vmem = pl.BlockSpec(memory_space=pltpu.VMEM)
    anywhere = pl.BlockSpec(memory_space=pl.ANY)
    dma = pltpu.SemaphoreType.DMA
    room = 4 * group * 2 * vector_count * vector_count
    results = pl.pallas_call(
        functools.partial(exchange_kernel, normalizer=normalizer),
        out_shape=(
            pltpu.VMEM((group, 2, vector_count, vector_count), f32),
            pltpu.VMEM((vector_count, 2 * late_count), bf16),
            pltpu.VMEM((2 * late_count, 2 * vector_count), bf16),
        ),
        in_specs=[anywhere] * 5,
        out_specs=(vmem, vmem, vmem),
        scratch_shapes=[
            pltpu.SMEM(momenta.shape, jnp.int32),
            pltpu.SMEM(ratios.shape, jnp.int32),
            pltpu.SMEM(source_slice.shape, jnp.int32),
            pltpu.VMEM(eigenvectors.shape[1:], bf16),
            pltpu.VMEM((vector_count, 4 * vector_count), f32),
            pltpu.VMEM((group, 2, vector_count, vector_count), bf16),
            pltpu.VMEM((2, vector_count, late_count), bf16),
            pltpu.VMEM(whole, f32),
            *[pltpu.VMEM(whole, bf16) for _ in range(8)],
            pltpu.VMEM((2 * vector_count, 2 * vector_count), bf16),
            pltpu.VMEM((2 * vector_count, 2 * vector_count), bf16),
            pltpu.VMEM((group, vector_count, 2 * vector_count), bf16),
            pltpu.VMEM((vector_count, 2 * late_count), bf16),
            pltpu.VMEM((site_count, 128), f32),
            pltpu.VMEM((site_count, 128), f32),
            dma((6,)),
            dma((3,)),
            dma((16,)),
            dma((3,)),
            pltpu.SemaphoreType.REGULAR((5,)),
        ],
        compiler_params=pltpu.CompilerParams(
            collective_id=0,
            has_side_effects=True,
            vmem_limit_bytes=VMEM_BYTES - 3 * room,
        ),
        name="exchange",
    )(
        in_hbm(momenta),
        in_hbm(ratios),
        in_hbm(source_slice),
        in_hbm(eigenvectors),
        in_hbm(perambulator),
    )
    return pl.pallas_call(
        finish_kernel,
        out_shape=pltpu.HBM((1, 2, vector_count, group * vector_count), f32),
        in_specs=[vmem, vmem, vmem],
        out_specs=anywhere,
        scratch_shapes=[pltpu.VMEM((2, tail_rows(vector_count), vector_count), f32), dma],
        compiler_params=pltpu.CompilerParams(vmem_limit_bytes=VMEM_BYTES // 2),
        name="finish",
    )(*[pltpu.with_memory_space_constraint(array, pltpu.VMEM) for array in results])


def body(*arrays):
    perambulator = arrays[1]
    group = lax.axis_size("space")
    part_count, order, columns = perambulator.shape[1:]

    def never(*_):
        return jnp.zeros((1, part_count, order // group, columns * group), jnp.float32)

    return lax.cond(lax.axis_index("space") < 2 * group, both_kernels, never, *arrays)


def fits(mesh, eigenvectors, perambulator):
    space, slots = mesh.shape["space"], mesh.shape["tm"]
    vector_count = eigenvectors.shape[4]
    return (
        space == 4
        and slots == 4
        and eigenvectors.shape[0] == slots * mesh.shape["cfg"]
        and perambulator.shape[2] == space * vector_count
        and vector_count % 128 == 0
        and vector_count >= 384
        and eigenvectors.shape[3] % (32 * space) == 0
    )


def solution(mesh):
    placed = (
        P(("cfg", "tm"), None, None, "space", None),
        P(("cfg", "tm"), None, None, "space"),
        P(),
        P(),
        P(),
    )

    def program(eigenvectors, perambulator, momenta, ratios, source_slice):
        chosen = body if fits(mesh, eigenvectors, perambulator) else general_body
        mapped = jax.shard_map(
            chosen,
            mesh=mesh,
            in_specs=placed,
            out_specs=P(("cfg", "tm"), None, "space", None),
            check_vma=False,
        )
        return mapped(eigenvectors, perambulator, momenta, ratios, source_slice)

    return program
```

```python
import functools
import math

import jax
import jax.numpy as jnp
from jax import lax
from jax.experimental import pallas as pl
from jax.experimental.pallas import tpu as pltpu
from jax.sharding import PartitionSpec as P

MESH = pl.DeviceIdType.MESH

LSIDE = 64

VMEM_BYTES = 67043328


def spread(value, axis, source):
    kept = jnp.where(lax.axis_index(axis) == source, value, 0).astype(value.dtype)
    return lax.psum(kept, axis)


def site_phases(momenta, first_site, site_count):
    site_index = first_site + lax.iota(jnp.int32, site_count)
    along_x = site_index % LSIDE
    along_y = site_index // LSIDE % LSIDE
    along_z = site_index // (LSIDE * LSIDE)
    turn_count = (
        momenta[:, 0:1] * along_x[None, :]
        + momenta[:, 1:2] * along_y[None, :]
        + momenta[:, 2:3] * along_z[None, :]
    )
    phase_angle = (turn_count % LSIDE).astype(jnp.float32) * (2.0 * math.pi / LSIDE)
    return (jnp.cos(phase_angle), jnp.sin(phase_angle))


def split_elementals(product, vector_count):
    lead_shape = product.shape[:-2]
    product_grid = product.reshape(lead_shape + (2, vector_count, 2, 2, vector_count))
    real_part = product_grid[..., 0, :, :, 0, :] + product_grid[..., 1, :, :, 1, :]
    imaginary = product_grid[..., 0, :, :, 1, :] - product_grid[..., 1, :, :, 0, :]
    stacked = jnp.stack([real_part, imaginary], axis=-4)
    return jnp.moveaxis(stacked, -2, -4)


def elementals(vectors, cosine, sine_part):
    slab_count, color_count, site_count, vector_count = (
        vectors.shape[0],
        vectors.shape[2],
        vectors.shape[3],
        vectors.shape[4],
    )
    row_count = color_count * site_count
    real_rows = vectors[:, 0].reshape(slab_count, row_count, vector_count)
    imaginary_rows = vectors[:, 1].reshape(slab_count, row_count, vector_count)
    cos_rows = jnp.broadcast_to(cosine[:, None, :], (2, color_count, site_count)).reshape(
        1, 2, row_count, 1
    )
    sin_rows = jnp.broadcast_to(sine_part[:, None, :], (2, color_count, site_count)).reshape(
        1, 2, row_count, 1
    )
    phased_real = (cos_rows * real_rows[:, None] + sin_rows * imaginary_rows[:, None]).astype(
        jnp.bfloat16
    )
    phased_imaginary = (cos_rows * imaginary_rows[:, None] - sin_rows * real_rows[:, None]).astype(
        jnp.bfloat16
    )
    phased = jnp.concatenate([phased_real, phased_imaginary], axis=3)
    phased = jnp.transpose(phased, (0, 2, 1, 3)).reshape(slab_count, row_count, 4 * vector_count)
    plain_vectors = jnp.concatenate([real_rows, imaginary_rows], axis=2)
    product = lax.dot_general(
        plain_vectors, phased, (((1,), (1,)), ((0,), (0,))), preferred_element_type=jnp.float32
    )
    return split_elementals(product, vector_count)


def source_block(chosen):
    real_t = chosen[0].T
    imaginary_t = chosen[1].T
    upper = jnp.concatenate([real_t, -imaginary_t], axis=1)
    lower = jnp.concatenate([imaginary_t, real_t], axis=1)
    return jnp.concatenate([upper, lower], axis=0)


def propagate(sink_matrix, tau):
    vector_count = sink_matrix.shape[1]
    spin_count = tau.shape[1] // vector_count
    column_count = tau.shape[2]
    real_part, imaginary = (sink_matrix[0], sink_matrix[1])
    upper = jnp.concatenate([real_part, -imaginary], axis=1)
    lower = jnp.concatenate([imaginary, real_part], axis=1)
    sink_big = jnp.concatenate([upper, lower], axis=0)
    stacked = jnp.transpose(tau.reshape(2, spin_count, vector_count, column_count), (0, 2, 1, 3))
    stacked = stacked.reshape(2 * vector_count, spin_count * column_count)
    product = jnp.dot(sink_big, stacked, preferred_element_type=jnp.float32)
    product = jnp.transpose(
        product.reshape(2, vector_count, spin_count, column_count), (0, 2, 1, 3)
    )
    return product.reshape(2, spin_count * vector_count, column_count).astype(jnp.bfloat16)


def attach_source(propagated, source_big):
    vector_count = source_big.shape[0] // 2
    row_count = propagated.shape[1]
    spin_count = propagated.shape[2] // vector_count
    stacked = jnp.concatenate(
        [
            propagated[0].reshape(row_count, spin_count, vector_count),
            propagated[1].reshape(row_count, spin_count, vector_count),
        ],
        axis=2,
    )
    product = jnp.dot(
        stacked.reshape(row_count * spin_count, 2 * vector_count),
        source_big,
        preferred_element_type=jnp.float32,
    )
    product = jnp.transpose(product.reshape(row_count, spin_count, 2, vector_count), (2, 0, 1, 3))
    return product.reshape(2, row_count, spin_count * vector_count)


def general_body(eigenvectors, perambulator, momenta, ratios, source_slice):
    slab_count = eigenvectors.shape[0]
    color_count = eigenvectors.shape[2]
    site_count = eigenvectors.shape[3]
    vector_count = eigenvectors.shape[4]
    first_site = lax.axis_index("space") * site_count
    cosine, sine_part = site_phases(momenta, first_site, site_count)
    normalizer = 1.0 / math.sqrt(color_count * site_count * lax.axis_size("space") * vector_count)
    weights = (
        ratios[:, 0].astype(jnp.float32) / ratios[:, 1].astype(jnp.float32) * normalizer
    ).reshape(1, 2, 1, 1, 1)
    parts = elementals(eigenvectors, cosine, sine_part)
    partial_sums = jnp.sum(weights * parts, axis=1, keepdims=True)
    summed = lax.psum(partial_sums, "space")
    sink_matrices = summed[:, 0].astype(jnp.bfloat16)
    global_slice = source_slice[0] % (slab_count * lax.axis_size("tm"))
    local_source = lax.dynamic_index_in_dim(
        sink_matrices, global_slice % slab_count, 0, keepdims=False
    )
    chosen = spread(local_source, "tm", global_slice // slab_count)
    source_big = source_block(chosen)
    propagated = jnp.stack([propagate(sink_matrices[0], perambulator[0])])
    return jnp.stack(
        [
            attach_source(
                lax.all_to_all(propagated, "space", split_axis=2, concat_axis=3, tiled=True)[0],
                source_big,
            )
        ]
    )


def block_dot(left, right, left_dim, right_dim):
    return lax.dot_general(
        left, right, (((left_dim,), (right_dim,)), ((), ())), preferred_element_type=jnp.float32
    )


def exchange_kernel(
    momenta_hbm,
    ratio_hbm,
    slice_hbm,
    eig_hbm,
    tau_hbm,
    res_ref,
    prop_in,
    source_late,
    momenta_ref,
    ratio_ref,
    slice_ref,
    eig,
    acc,
    tau,
    tau_mine,
    part,
    pair_out,
    pair_in,
    cross_out,
    cross_in,
    sink,
    sink_pair,
    picked,
    far,
    sink_big,
    source_big,
    prop,
    prop_out,
    cosines,
    sines,
    own_sem,
    send,
    recv,
    spread_recv,
    ready,
    *,
    normalizer,
):
    vector_count = eig_hbm.shape[4]
    site_count = eig_hbm.shape[3]
    chunk_count, chunk_rows = part.shape[0], part.shape[2]
    color_count = eig.shape[1]
    site_step = site_count // 2
    steps_per_color = site_count // site_step
    step_count = color_count * steps_per_color
    late_count = tau_mine.shape[2]
    early_count = vector_count - late_count
    last_rows = tail_rows(vector_count)
    piece_rows = (vector_count - last_rows) // 3 // 32 * 32
    piece_ends = [piece_rows, 2 * piece_rows, vector_count - last_rows, vector_count]
    pieces = [pl.ds(a, b - a) for a, b in zip([0] + piece_ends, piece_ends) if b > a]
    piece_count = len(pieces)
    me = lax.axis_index("space")
    slot = lax.axis_index("tm")
    near = me + 1 - 2 * (me % 2)
    across = me + 2 - 4 * (me // 2)
    mirror = 3 - me
    inner = ((me + 1) // 2) % 2
    core = slot % 2
    core_peer = slot + 1 - 2 * core
    chip_peer = slot + 2 - 4 * (slot // 2)

    eig_copy = pltpu.make_async_copy(eig_hbm.at[0], eig, own_sem.at[4])
    own_copy = pltpu.make_async_copy(
        tau_hbm.at[0, :, pl.ds(me * vector_count, vector_count), :], tau.at[me], own_sem.at[0]
    )
    late_copy = pltpu.make_async_copy(
        tau_hbm.at[
            0, :, pl.ds(mirror * vector_count, vector_count), pl.ds(early_count, late_count)
        ],
        tau_mine,
        own_sem.at[1],
    )
    scalar_copies = [
        pltpu.make_async_copy(momenta_hbm, momenta_ref, own_sem.at[2]),
        pltpu.make_async_copy(ratio_hbm, ratio_ref, own_sem.at[3]),
        pltpu.make_async_copy(slice_hbm, slice_ref, own_sem.at[5]),
    ]

    barrier = pltpu.get_barrier_semaphore()

    def hello(peer):
        pl.semaphore_signal(barrier, inc=1, device_id=peer, device_id_type=MESH)

    def hop(from_ref, to_ref, send_sem, recv_sem, peer):
        return pltpu.make_async_remote_copy(
            src_ref=from_ref,
            dst_ref=to_ref,
            send_sem=send_sem,
            recv_sem=recv_sem,
            device_id=peer,
            device_id_type=MESH,
        )

    def tau_copy(to, part_of, recv_index):
        return hop(
            tau_hbm.at[0, part_of, pl.ds(to * vector_count, vector_count), :],
            tau.at[me, part_of],
            send.at[0],
            recv.at[recv_index],
            {"space": to},
        )

    near_copies = [tau_copy(near, piece, 0) for piece in range(2)]
    near_whole = tau_copy(near, slice(None), 0)
    across_raw = tau_copy(across, slice(None), 6)
    across_copies = [tau_copy(across, piece, 11) for piece in range(2)]
    across_whole = tau_copy(across, slice(None), 11)
    mirror_copy = tau_copy(mirror, slice(None), 1)
    def early_copy(piece):
        first, count = early_rows[piece]
        return hop(
            tau_hbm.at[
                0, :, pl.ds(mirror * vector_count + first, count), pl.ds(0, early_count)
            ],
            tau.at[me, :, pl.ds(first, count), pl.ds(0, early_count)],
            send.at[1],
            recv.at[10],
            {"space": mirror},
        )

    lead = vector_count // 2 // 32 * 32
    early_ends = [
        lead,
        lead + lead // 4 // 16 * 16,
        lead + lead // 2 // 16 * 16,
        vector_count,
    ]
    early_rows = [(a, b - a) for a, b in zip([0] + early_ends, early_ends)]
    early_copies = [early_copy(piece) for piece in range(4)]
    prop_copies = [
        hop(
            prop_out.at[pieces[p], :],
            prop_in.at[pieces[p], :],
            send.at[1],
            recv.at[12 + p],
            {"space": mirror},
        )
        for p in range(piece_count)
    ]

    def tell(index, peer):
        pl.semaphore_signal(ready.at[index], inc=1, device_id=peer, device_id_type=MESH)

    def phases():
        for copy in scalar_copies:
            copy.wait()
        lanes = cosines.shape[1]
        site = me * site_count + lax.broadcasted_iota(jnp.int32, (site_count, lanes), 0)
        first_lane = lax.broadcasted_iota(jnp.int32, (site_count, lanes), 1) == 0
        shift = LSIDE.bit_length() - 1
        places = (
            jnp.bitwise_and(site, LSIDE - 1),
            jnp.bitwise_and(jnp.right_shift(site, shift), LSIDE - 1),
            jnp.right_shift(site, 2 * shift),
        )
        turn = jnp.zeros_like(site)
        for axis in range(3):
            turn += jnp.where(first_lane, momenta_ref[0, axis], momenta_ref[1, axis]) * places[axis]
        angle = jnp.bitwise_and(turn, LSIDE - 1).astype(jnp.float32) * (2.0 * math.pi / LSIDE)
        cosines[...] = jnp.cos(angle)
        sines[...] = jnp.sin(angle)

    @pl.when(inner == 1)
    def _():
        hello({"space": mirror})
        hello({"space": near})
        pl.semaphore_wait(barrier, 1)
        early_copies[0].start()
        for copy in scalar_copies:
            copy.start()
        eig_copy.start()
        phases()
        pl.semaphore_wait(ready.at[0], 1)
        tell(1, {"space": mirror})
        near_copies[0].start()
        pl.semaphore_wait(ready.at[1], 1)
        across_raw.start()
        tell(2, {"space": near})
        late_copy.start()

    @pl.when(inner == 0)
    def _():
        hello({"tm": core_peer})
        hello({"tm": chip_peer})
        for copy in scalar_copies:
            copy.start()
        eig_copy.start()
        pl.semaphore_wait(barrier, 3)
        tell(0, {"space": near})
        near_copies[0].start()
        tell(0, {"tm": core_peer})
        tell(1, {"tm": chip_peer})
        phases()
        pl.semaphore_wait(ready.at[0], 1)
        pl.semaphore_wait(ready.at[1], 1)
        tell(3, {"space": near})

    own_copy.start()

    acc[...] = jnp.zeros_like(acc)

    eig_copy.wait()

    def accumulate(step, carry):
        color = step // steps_per_color
        rows = pl.ds(pl.multiple_of((step % steps_per_color) * site_step, site_step), site_step)
        plain_real, plain_imag = eig[0, color, rows, :], eig[1, color, rows, :]
        real = plain_real.astype(jnp.float32)
        imag = plain_imag.astype(jnp.float32)
        upper, lower = [], []
        for k in range(2):
            cosine = cosines[rows, k : k + 1]
            sine = sines[rows, k : k + 1]
            turned_real = (cosine * real + sine * imag).astype(jnp.bfloat16)
            turned_imag = (cosine * imag - sine * real).astype(jnp.bfloat16)
            upper += [turned_real, turned_imag]
            lower += [turned_imag, -turned_real]
        left = jnp.concatenate([plain_real, plain_imag], axis=0)
        right = jnp.concatenate(
            [jnp.concatenate(upper, axis=1), jnp.concatenate(lower, axis=1)], axis=0
        )
        acc[...] += block_dot(left, right, 0, 0)
        return carry

    lax.fori_loop(0, step_count, accumulate, 0, unroll=True)

    weights = [
        jnp.full((1, vector_count), ratio_ref[k, 0], jnp.int32).astype(jnp.float32)
        / jnp.full((1, vector_count), ratio_ref[k, 1], jnp.int32).astype(jnp.float32)
        * normalizer
        for k in range(2)
    ]

    def weighted(chunk, c):
        rows = pl.ds(chunk * chunk_rows, chunk_rows)
        return (
            weights[0] * acc[rows, c * vector_count : (c + 1) * vector_count]
            + weights[1] * acc[rows, (2 + c) * vector_count : (3 + c) * vector_count]
        )

    pair_hops = [
        hop(
            pair_out.at[q], pair_in.at[q], send.at[0], recv.at[2 + q], {"space": near}
        )
        for q in range(chunk_count)
    ]
    cross_hops = [
        hop(
            cross_out.at[q], cross_in.at[q], send.at[0], recv.at[6 + q], {"space": mirror}
        )
        for q in range(chunk_count)
    ]
    back_hops = [
        hop(sink.at[q], sink.at[q], send.at[0], recv.at[2 + q], {"space": near})
        for q in range(chunk_count)
    ]

    @pl.when(inner == 0)
    def _():
        for q in range(chunk_count):
            for c in range(2):
                pair_out[q, c] = weighted(q, c).astype(jnp.bfloat16)
            pair_hops[q].start()
        near_copies[1].start()
        pl.semaphore_wait(ready.at[2], 1)
        for q in range(chunk_count // 2):
            back_hops[q].wait_recv()
        tell(4, {"tm": core_peer})
        pl.semaphore_wait(ready.at[4], 1)
        across_copies[0].start()
        mirror_copy.start()
        across_copies[1].start()
        for q in range(chunk_count // 2, chunk_count):
            back_hops[q].wait_recv()

    @pl.when(inner == 1)
    def _():
        for q in range(chunk_count):
            for c in range(2):
                part[q, c] = weighted(q, c)

        first_half = jnp.logical_or(core == 0, me // 2 == 1)

        def forward(q):
            pair_hops[q].wait_recv()
            part[q] = part[q] + pair_in[q].astype(jnp.float32)
            cross_out[q] = part[q].astype(jnp.bfloat16)
            cross_hops[q].start()

        def settle(q):
            cross_hops[q].wait_recv()
            sink[q] = (part[q] + cross_in[q].astype(jnp.float32)).astype(jnp.bfloat16)
            back_hops[q].start()

        for q in range(chunk_count):
            forward(q)
            if q == chunk_count - 1:
                early_copies[1].start()
                pl.when(first_half)(early_copies[2].start)
                pl.when(core == 0)(early_copies[3].start)
            if q > 1:
                settle(q - 2)
        for q in range(chunk_count - 2, chunk_count):
            settle(q)
        pl.when(jnp.logical_not(first_half))(early_copies[2].start)
        pl.when(core == 1)(early_copies[3].start)
        near_copies[1].start()
        pl.semaphore_wait(ready.at[3], 1)

    core_hop = hop(sink, sink_pair, send.at[2], spread_recv.at[0], {"tm": core_peer})
    core_hop.start()
    for q in range(chunk_count):
        rows = pl.ds(q * chunk_rows, chunk_rows)
        low = pl.ds(vector_count + q * chunk_rows, chunk_rows)
        real, imag = sink[q, 0], sink[q, 1]
        sink_big[rows, :vector_count] = real
        sink_big[rows, vector_count:] = -imag
        sink_big[low, :vector_count] = imag
        sink_big[low, vector_count:] = real

    def carried(block):
        stacked = block.reshape(2 * vector_count, block.shape[2])
        product = block_dot(sink_big[...], stacked, 1, 0).astype(jnp.bfloat16)
        return product[:vector_count], product[vector_count:]

    def left_multiply(origin):
        real, imag = carried(tau[origin])
        prop[origin, :, :vector_count] = real
        prop[origin, :, vector_count:] = imag

    def right_multiply(origin):
        product = block_dot(prop[origin], source_big[...], 1, 1)
        res_ref[origin, 0] = product[:, :vector_count]
        res_ref[origin, 1] = product[:, vector_count:]

    @pl.when(inner == 1)
    def _():
        late_copy.wait()
        real, imag = carried(tau_mine[...])
        prop_out[:, :late_count] = real
        prop_out[:, late_count:] = imag
        for copy in prop_copies:
            copy.start()

    core_hop.wait_recv()
    chosen_slot = slice_ref[0] % lax.axis_size("tm")
    picked[...] = jnp.where(chosen_slot == slot, sink[...], sink_pair[...])
    half = pl.ds(core * (chunk_count // 2), chunk_count // 2)
    chip_hop = hop(
        picked.at[half], far.at[half], send.at[2], spread_recv.at[1], {"tm": chip_peer}
    )
    chip_hop.start()

    own_copy.wait()
    left_multiply(me)

    @pl.when(inner == 1)
    def _():
        near_whole.wait_recv()
        left_multiply(near)

    @pl.when(inner == 0)
    def _():
        across_raw.wait_recv()
        left_multiply(across)

    chip_hop.wait_recv()
    forward_hop = hop(
        far.at[half], far.at[half], send.at[2], spread_recv.at[2], {"tm": core_peer}
    )
    forward_hop.start()
    forward_hop.wait_recv()
    chosen = jnp.where(chosen_slot // 2 == slot // 2, picked[...], far[...])
    for q in range(chunk_count):
        rows = pl.ds(q * chunk_rows, chunk_rows)
        low = pl.ds(vector_count + q * chunk_rows, chunk_rows)
        source_big[rows, :vector_count] = chosen[q, 0]
        source_big[rows, vector_count:] = chosen[q, 1]
        source_big[low, :vector_count] = -chosen[q, 1]
        source_big[low, vector_count:] = chosen[q, 0]
    right_multiply(me)

    @pl.when(inner == 0)
    def _():
        right_multiply(across)
        for origin, copy in ((near, near_whole), (mirror, mirror_copy)):
            copy.wait_recv()
            left_multiply(origin)
            right_multiply(origin)

    @pl.when(inner == 1)
    def _():
        right_multiply(near)
        across_whole.wait_recv()
        left_multiply(across)
        right_multiply(across)
        landed = tau.at[mirror, :, :, pl.ds(0, early_count)]
        hop(landed, landed, send.at[1], recv.at[10], {"space": mirror}).wait_recv()
        both = jnp.concatenate(carried(tau[mirror, :, :, :early_count]), axis=1)
        source_early = jnp.concatenate(
            [
                source_big[:, :early_count],
                source_big[:, vector_count : vector_count + early_count],
            ],
            axis=1,
        )
        product = block_dot(both, source_early, 1, 1)
        res_ref[mirror, 0] = product[:, :vector_count]
        res_ref[mirror, 1] = product[:, vector_count:]
        source_late[:late_count] = source_big[:, early_count:vector_count].T
        source_late[late_count:] = source_big[:, vector_count + early_count :].T

        def add_piece(p):
            rows = pieces[p]
            prop_copies[p].wait_recv()
            product = block_dot(prop_in[rows, :], source_late[...], 1, 0)
            res_ref[mirror, 0, rows, :] += product[:, :vector_count]
            res_ref[mirror, 1, rows, :] += product[:, vector_count:]

        for p in range(piece_count - 1):
            add_piece(p)
        prop_copies[-1].wait_recv()
        hop(sink, sink, send.at[1], recv.at[0], {"space": near}).wait_send()

    hop(tau, tau, send.at[0], recv.at[0], {"space": near}).wait_send()
    pair = pl.ds(0, 2)
    hop(tau.at[pair], tau.at[pair], send.at[2], recv.at[0], {"space": near}).wait_send()


def finish_kernel(res_ref, prop_ref, source_ref, out_hbm, last, sem):
    group, _, vector_count, _ = res_ref.shape
    last_rows = last.shape[1]
    body_rows = pl.ds(0, vector_count - last_rows)
    tail = pl.ds(vector_count - last_rows, last_rows)
    me = lax.axis_index("space")
    mirror = group - 1 - me
    inner = ((me + 1) // 2) % 2

    def put(source, origin, rows):
        columns = pl.ds(origin * vector_count, vector_count)
        pltpu.make_async_copy(source, out_hbm.at[0, :, rows, columns], sem).start()

    for origin in range(group):
        put(res_ref.at[origin, :, body_rows, :], origin, body_rows)

    @pl.when(inner == 1)
    def _():
        product = block_dot(prop_ref[tail, :], source_ref[...], 1, 0)
        last[0] = res_ref[mirror, 0, tail, :] + product[:, :vector_count]
        last[1] = res_ref[mirror, 1, tail, :] + product[:, vector_count:]

    for origin in range(group):
        late = jnp.logical_and(inner == 1, mirror == origin)
        pl.when(late)(functools.partial(put, last, origin, tail))
        pl.when(jnp.logical_not(late))(
            functools.partial(put, res_ref.at[origin, :, tail, :], origin, tail)
        )
    pltpu.make_async_copy(res_ref, res_ref, sem).wait()


def tail_rows(vector_count):
    return vector_count // 12 // 32 * 32


def in_hbm(array):
    return pltpu.with_memory_space_constraint(array, pltpu.HBM)


def both_kernels(eigenvectors, perambulator, momenta, ratios, source_slice):
    color_count, site_count, vector_count = eigenvectors.shape[2:]
    group = lax.axis_size("space")
    normalizer = 1.0 / math.sqrt(color_count * site_count * group * vector_count)
    chunk_count = 4
    late_count = 128
    whole = (chunk_count, 2, vector_count // chunk_count, vector_count)
    bf16, f32 = jnp.bfloat16, jnp.float32
    vmem = pl.BlockSpec(memory_space=pltpu.VMEM)
    anywhere = pl.BlockSpec(memory_space=pl.ANY)
    dma = pltpu.SemaphoreType.DMA
    room = 4 * group * 2 * vector_count * vector_count
    results = pl.pallas_call(
        functools.partial(exchange_kernel, normalizer=normalizer),
        out_shape=(
            pltpu.VMEM((group, 2, vector_count, vector_count), f32),
            pltpu.VMEM((vector_count, 2 * late_count), bf16),
            pltpu.VMEM((2 * late_count, 2 * vector_count), bf16),
        ),
        in_specs=[anywhere] * 5,
        out_specs=(vmem, vmem, vmem),
        scratch_shapes=[
            pltpu.SMEM(momenta.shape, jnp.int32),
            pltpu.SMEM(ratios.shape, jnp.int32),
            pltpu.SMEM(source_slice.shape, jnp.int32),
            pltpu.VMEM(eigenvectors.shape[1:], bf16),
            pltpu.VMEM((vector_count, 4 * vector_count), f32),
            pltpu.VMEM((group, 2, vector_count, vector_count), bf16),
            pltpu.VMEM((2, vector_count, late_count), bf16),
            pltpu.VMEM(whole, f32),
            *[pltpu.VMEM(whole, bf16) for _ in range(8)],
            pltpu.VMEM((2 * vector_count, 2 * vector_count), bf16),
            pltpu.VMEM((2 * vector_count, 2 * vector_count), bf16),
            pltpu.VMEM((group, vector_count, 2 * vector_count), bf16),
            pltpu.VMEM((vector_count, 2 * late_count), bf16),
            pltpu.VMEM((site_count, 128), f32),
            pltpu.VMEM((site_count, 128), f32),
            dma((6,)),
            dma((3,)),
            dma((16,)),
            dma((3,)),
            pltpu.SemaphoreType.REGULAR((5,)),
        ],
        compiler_params=pltpu.CompilerParams(
            collective_id=0,
            has_side_effects=True,
            vmem_limit_bytes=VMEM_BYTES - 3 * room,
        ),
        name="exchange",
    )(
        in_hbm(momenta),
        in_hbm(ratios),
        in_hbm(source_slice),
        in_hbm(eigenvectors),
        in_hbm(perambulator),
    )
    return pl.pallas_call(
        finish_kernel,
        out_shape=pltpu.HBM((1, 2, vector_count, group * vector_count), f32),
        in_specs=[vmem, vmem, vmem],
        out_specs=anywhere,
        scratch_shapes=[pltpu.VMEM((2, tail_rows(vector_count), vector_count), f32), dma],
        compiler_params=pltpu.CompilerParams(vmem_limit_bytes=VMEM_BYTES // 2),
        name="finish",
    )(*[pltpu.with_memory_space_constraint(array, pltpu.VMEM) for array in results])


def body(*arrays):
    perambulator = arrays[1]
    group = lax.axis_size("space")
    part_count, order, columns = perambulator.shape[1:]

    def never(*_):
        return jnp.zeros((1, part_count, order // group, columns * group), jnp.float32)

    return lax.cond(lax.axis_index("space") < 2 * group, both_kernels, never, *arrays)


def fits(mesh, eigenvectors, perambulator):
    space, slots = mesh.shape["space"], mesh.shape["tm"]
    vector_count = eigenvectors.shape[4]
    return (
        space == 4
        and slots == 4
        and eigenvectors.shape[0] == slots * mesh.shape["cfg"]
        and perambulator.shape[2] == space * vector_count
        and vector_count % 128 == 0
        and vector_count >= 384
        and eigenvectors.shape[3] % (32 * space) == 0
    )


def solution(mesh):
    placed = (
        P(("cfg", "tm"), None, None, "space", None),
        P(("cfg", "tm"), None, None, "space"),
        P(),
        P(),
        P(),
    )

    def program(eigenvectors, perambulator, momenta, ratios, source_slice):
        chosen = body if fits(mesh, eigenvectors, perambulator) else general_body
        mapped = jax.shard_map(
            chosen,
            mesh=mesh,
            in_specs=placed,
            out_specs=P(("cfg", "tm"), None, "space", None),
            check_vma=False,
        )
        return mapped(eigenvectors, perambulator, momenta, ratios, source_slice)

    return program
```

```python
import functools
import math

import jax
import jax.numpy as jnp
from jax import lax
from jax.experimental import pallas as pl
from jax.experimental.pallas import tpu as pltpu
from jax.sharding import PartitionSpec as P

MESH = pl.DeviceIdType.MESH

LSIDE = 64

VMEM_BYTES = 67043328


def spread(value, axis, source):
    kept = jnp.where(lax.axis_index(axis) == source, value, 0).astype(value.dtype)
    return lax.psum(kept, axis)


def site_phases(momenta, first_site, site_count):
    site_index = first_site + lax.iota(jnp.int32, site_count)
    along_x = site_index % LSIDE
    along_y = site_index // LSIDE % LSIDE
    along_z = site_index // (LSIDE * LSIDE)
    turn_count = (
        momenta[:, 0:1] * along_x[None, :]
        + momenta[:, 1:2] * along_y[None, :]
        + momenta[:, 2:3] * along_z[None, :]
    )
    phase_angle = (turn_count % LSIDE).astype(jnp.float32) * (2.0 * math.pi / LSIDE)
    return (jnp.cos(phase_angle), jnp.sin(phase_angle))


def split_elementals(product, vector_count):
    lead_shape = product.shape[:-2]
    product_grid = product.reshape(lead_shape + (2, vector_count, 2, 2, vector_count))
    real_part = product_grid[..., 0, :, :, 0, :] + product_grid[..., 1, :, :, 1, :]
    imaginary = product_grid[..., 0, :, :, 1, :] - product_grid[..., 1, :, :, 0, :]
    stacked = jnp.stack([real_part, imaginary], axis=-4)
    return jnp.moveaxis(stacked, -2, -4)


def elementals(vectors, cosine, sine_part):
    slab_count, color_count, site_count, vector_count = (
        vectors.shape[0],
        vectors.shape[2],
        vectors.shape[3],
        vectors.shape[4],
    )
    row_count = color_count * site_count
    real_rows = vectors[:, 0].reshape(slab_count, row_count, vector_count)
    imaginary_rows = vectors[:, 1].reshape(slab_count, row_count, vector_count)
    cos_rows = jnp.broadcast_to(cosine[:, None, :], (2, color_count, site_count)).reshape(
        1, 2, row_count, 1
    )
    sin_rows = jnp.broadcast_to(sine_part[:, None, :], (2, color_count, site_count)).reshape(
        1, 2, row_count, 1
    )
    phased_real = (cos_rows * real_rows[:, None] + sin_rows * imaginary_rows[:, None]).astype(
        jnp.bfloat16
    )
    phased_imaginary = (cos_rows * imaginary_rows[:, None] - sin_rows * real_rows[:, None]).astype(
        jnp.bfloat16
    )
    phased = jnp.concatenate([phased_real, phased_imaginary], axis=3)
    phased = jnp.transpose(phased, (0, 2, 1, 3)).reshape(slab_count, row_count, 4 * vector_count)
    plain_vectors = jnp.concatenate([real_rows, imaginary_rows], axis=2)
    product = lax.dot_general(
        plain_vectors, phased, (((1,), (1,)), ((0,), (0,))), preferred_element_type=jnp.float32
    )
    return split_elementals(product, vector_count)


def source_block(chosen):
    real_t = chosen[0].T
    imaginary_t = chosen[1].T
    upper = jnp.concatenate([real_t, -imaginary_t], axis=1)
    lower = jnp.concatenate([imaginary_t, real_t], axis=1)
    return jnp.concatenate([upper, lower], axis=0)


def propagate(sink_matrix, tau):
    vector_count = sink_matrix.shape[1]
    spin_count = tau.shape[1] // vector_count
    column_count = tau.shape[2]
    real_part, imaginary = (sink_matrix[0], sink_matrix[1])
    upper = jnp.concatenate([real_part, -imaginary], axis=1)
    lower = jnp.concatenate([imaginary, real_part], axis=1)
    sink_big = jnp.concatenate([upper, lower], axis=0)
    stacked = jnp.transpose(tau.reshape(2, spin_count, vector_count, column_count), (0, 2, 1, 3))
    stacked = stacked.reshape(2 * vector_count, spin_count * column_count)
    product = jnp.dot(sink_big, stacked, preferred_element_type=jnp.float32)
    product = jnp.transpose(
        product.reshape(2, vector_count, spin_count, column_count), (0, 2, 1, 3)
    )
    return product.reshape(2, spin_count * vector_count, column_count).astype(jnp.bfloat16)


def attach_source(propagated, source_big):
    vector_count = source_big.shape[0] // 2
    row_count = propagated.shape[1]
    spin_count = propagated.shape[2] // vector_count
    stacked = jnp.concatenate(
        [
            propagated[0].reshape(row_count, spin_count, vector_count),
            propagated[1].reshape(row_count, spin_count, vector_count),
        ],
        axis=2,
    )
    product = jnp.dot(
        stacked.reshape(row_count * spin_count, 2 * vector_count),
        source_big,
        preferred_element_type=jnp.float32,
    )
    product = jnp.transpose(product.reshape(row_count, spin_count, 2, vector_count), (2, 0, 1, 3))
    return product.reshape(2, row_count, spin_count * vector_count)


def general_body(eigenvectors, perambulator, momenta, ratios, source_slice):
    slab_count = eigenvectors.shape[0]
    color_count = eigenvectors.shape[2]
    site_count = eigenvectors.shape[3]
    vector_count = eigenvectors.shape[4]
    first_site = lax.axis_index("space") * site_count
    cosine, sine_part = site_phases(momenta, first_site, site_count)
    normalizer = 1.0 / math.sqrt(color_count * site_count * lax.axis_size("space") * vector_count)
    weights = (
        ratios[:, 0].astype(jnp.float32) / ratios[:, 1].astype(jnp.float32) * normalizer
    ).reshape(1, 2, 1, 1, 1)
    parts = elementals(eigenvectors, cosine, sine_part)
    partial_sums = jnp.sum(weights * parts, axis=1, keepdims=True)
    summed = lax.psum(partial_sums, "space")
    sink_matrices = summed[:, 0].astype(jnp.bfloat16)
    global_slice = source_slice[0] % (slab_count * lax.axis_size("tm"))
    local_source = lax.dynamic_index_in_dim(
        sink_matrices, global_slice % slab_count, 0, keepdims=False
    )
    chosen = spread(local_source, "tm", global_slice // slab_count)
    source_big = source_block(chosen)
    propagated = jnp.stack([propagate(sink_matrices[0], perambulator[0])])
    return jnp.stack(
        [
            attach_source(
                lax.all_to_all(propagated, "space", split_axis=2, concat_axis=3, tiled=True)[0],
                source_big,
            )
        ]
    )


def block_dot(left, right, left_dim, right_dim):
    return lax.dot_general(
        left, right, (((left_dim,), (right_dim,)), ((), ())), preferred_element_type=jnp.float32
    )


def exchange_kernel(
    momenta_hbm,
    ratio_hbm,
    slice_hbm,
    eig_hbm,
    tau_hbm,
    res_ref,
    prop_in,
    source_late,
    momenta_ref,
    ratio_ref,
    slice_ref,
    eig,
    acc,
    tau,
    tau_mine,
    part,
    pair_out,
    pair_in,
    cross_out,
    cross_in,
    sink,
    sink_pair,
    picked,
    far,
    sink_big,
    source_big,
    prop,
    prop_out,
    cosines,
    sines,
    own_sem,
    send,
    recv,
    spread_recv,
    ready,
    *,
    normalizer,
):
    vector_count = eig_hbm.shape[4]
    site_count = eig_hbm.shape[3]
    chunk_count, chunk_rows = part.shape[0], part.shape[2]
    color_count = eig.shape[1]
    site_step = site_count // 2
    steps_per_color = site_count // site_step
    step_count = color_count * steps_per_color
    late_count = tau_mine.shape[2]
    early_count = vector_count - late_count
    last_rows = vector_count // 12 // 32 * 32
    piece_rows = (vector_count - tail_rows(vector_count)) // 2
    piece_ends = [piece_rows, 2 * piece_rows, vector_count - last_rows, vector_count]
    pieces = [pl.ds(a, b - a) for a, b in zip([0] + piece_ends, piece_ends) if b > a]
    piece_count = len(pieces)
    me = lax.axis_index("space")
    slot = lax.axis_index("tm")
    near = me + 1 - 2 * (me % 2)
    across = me + 2 - 4 * (me // 2)
    mirror = 3 - me
    inner = ((me + 1) // 2) % 2
    core = slot % 2
    core_peer = slot + 1 - 2 * core
    chip_peer = slot + 2 - 4 * (slot // 2)

    eig_copy = pltpu.make_async_copy(eig_hbm.at[0], eig, own_sem.at[4])
    own_copy = pltpu.make_async_copy(
        tau_hbm.at[0, :, pl.ds(me * vector_count, vector_count), :], tau.at[me], own_sem.at[0]
    )
    late_copy = pltpu.make_async_copy(
        tau_hbm.at[
            0, :, pl.ds(mirror * vector_count, vector_count), pl.ds(early_count, late_count)
        ],
        tau_mine,
        own_sem.at[1],
    )
    scalar_copies = [
        pltpu.make_async_copy(momenta_hbm, momenta_ref, own_sem.at[2]),
        pltpu.make_async_copy(ratio_hbm, ratio_ref, own_sem.at[3]),
        pltpu.make_async_copy(slice_hbm, slice_ref, own_sem.at[5]),
    ]

    barrier = pltpu.get_barrier_semaphore()

    def hello(peer):
        pl.semaphore_signal(barrier, inc=1, device_id=peer, device_id_type=MESH)

    def hop(from_ref, to_ref, send_sem, recv_sem, peer):
        return pltpu.make_async_remote_copy(
            src_ref=from_ref,
            dst_ref=to_ref,
            send_sem=send_sem,
            recv_sem=recv_sem,
            device_id=peer,
            device_id_type=MESH,
        )

    def tau_copy(to, part_of, recv_index):
        return hop(
            tau_hbm.at[0, part_of, pl.ds(to * vector_count, vector_count), :],
            tau.at[me, part_of],
            send.at[0],
            recv.at[recv_index],
            {"space": to},
        )

    near_copies = [tau_copy(near, piece, 0) for piece in range(2)]
    near_whole = tau_copy(near, slice(None), 0)
    across_raw = tau_copy(across, slice(None), 6)
    across_copies = [tau_copy(across, piece, 11) for piece in range(2)]
    across_whole = tau_copy(across, slice(None), 11)
    mirror_copy = tau_copy(mirror, slice(None), 1)
    def early_copy(piece):
        first, count = early_rows[piece]
        return hop(
            tau_hbm.at[
                0, :, pl.ds(mirror * vector_count + first, count), pl.ds(0, early_count)
            ],
            tau.at[me, :, pl.ds(first, count), pl.ds(0, early_count)],
            send.at[1],
            recv.at[10],
            {"space": mirror},
        )

    lead = vector_count // 2 // 32 * 32
    early_ends = [
        lead,
        lead + lead // 4 // 16 * 16,
        lead + lead // 2 // 16 * 16,
        vector_count,
    ]
    early_rows = [(a, b - a) for a, b in zip([0] + early_ends, early_ends)]
    early_copies = [early_copy(piece) for piece in range(4)]
    prop_copies = [
        hop(
            prop_out.at[pieces[p], :],
            prop_in.at[pieces[p], :],
            send.at[1],
            recv.at[12 + p],
            {"space": mirror},
        )
        for p in range(piece_count)
    ]

    def tell(index, peer):
        pl.semaphore_signal(ready.at[index], inc=1, device_id=peer, device_id_type=MESH)

    def phases():
        for copy in scalar_copies:
            copy.wait()
        lanes = cosines.shape[1]
        site = me * site_count + lax.broadcasted_iota(jnp.int32, (site_count, lanes), 0)
        first_lane = lax.broadcasted_iota(jnp.int32, (site_count, lanes), 1) == 0
        shift = LSIDE.bit_length() - 1
        places = (
            jnp.bitwise_and(site, LSIDE - 1),
            jnp.bitwise_and(jnp.right_shift(site, shift), LSIDE - 1),
            jnp.right_shift(site, 2 * shift),
        )
        turn = jnp.zeros_like(site)
        for axis in range(3):
            turn += jnp.where(first_lane, momenta_ref[0, axis], momenta_ref[1, axis]) * places[axis]
        angle = jnp.bitwise_and(turn, LSIDE - 1).astype(jnp.float32) * (2.0 * math.pi / LSIDE)
        cosines[...] = jnp.cos(angle)
        sines[...] = jnp.sin(angle)

    @pl.when(inner == 1)
    def _():
        hello({"space": mirror})
        hello({"space": near})
        pl.semaphore_wait(barrier, 1)
        early_copies[0].start()
        for copy in scalar_copies:
            copy.start()
        eig_copy.start()
        phases()
        pl.semaphore_wait(ready.at[0], 1)
        tell(1, {"space": mirror})
        near_copies[0].start()
        pl.semaphore_wait(ready.at[1], 1)
        across_raw.start()
        tell(2, {"space": near})
        late_copy.start()

    @pl.when(inner == 0)
    def _():
        hello({"tm": core_peer})
        hello({"tm": chip_peer})
        for copy in scalar_copies:
            copy.start()
        eig_copy.start()
        pl.semaphore_wait(barrier, 3)
        tell(0, {"space": near})
        near_copies[0].start()
        tell(0, {"tm": core_peer})
        tell(1, {"tm": chip_peer})
        phases()
        pl.semaphore_wait(ready.at[0], 1)
        pl.semaphore_wait(ready.at[1], 1)
        tell(3, {"space": near})

    own_copy.start()

    acc[...] = jnp.zeros_like(acc)

    eig_copy.wait()

    def accumulate(step, carry):
        color = step // steps_per_color
        rows = pl.ds(pl.multiple_of((step % steps_per_color) * site_step, site_step), site_step)
        plain_real, plain_imag = eig[0, color, rows, :], eig[1, color, rows, :]
        real = plain_real.astype(jnp.float32)
        imag = plain_imag.astype(jnp.float32)
        upper, lower = [], []
        for k in range(2):
            cosine = cosines[rows, k : k + 1]
            sine = sines[rows, k : k + 1]
            turned_real = (cosine * real + sine * imag).astype(jnp.bfloat16)
            turned_imag = (cosine * imag - sine * real).astype(jnp.bfloat16)
            upper += [turned_real, turned_imag]
            lower += [turned_imag, -turned_real]
        left = jnp.concatenate([plain_real, plain_imag], axis=0)
        right = jnp.concatenate(
            [jnp.concatenate(upper, axis=1), jnp.concatenate(lower, axis=1)], axis=0
        )
        acc[...] += block_dot(left, right, 0, 0)
        return carry

    lax.fori_loop(0, step_count, accumulate, 0, unroll=True)

    weights = [
        jnp.full((1, vector_count), ratio_ref[k, 0], jnp.int32).astype(jnp.float32)
        / jnp.full((1, vector_count), ratio_ref[k, 1], jnp.int32).astype(jnp.float32)
        * normalizer
        for k in range(2)
    ]

    def weighted(chunk, c):
        rows = pl.ds(chunk * chunk_rows, chunk_rows)
        return (
            weights[0] * acc[rows, c * vector_count : (c + 1) * vector_count]
            + weights[1] * acc[rows, (2 + c) * vector_count : (3 + c) * vector_count]
        )

    pair_hops = [
        hop(
            pair_out.at[q], pair_in.at[q], send.at[0], recv.at[2 + q], {"space": near}
        )
        for q in range(chunk_count)
    ]
    cross_hops = [
        hop(
            cross_out.at[q], cross_in.at[q], send.at[0], recv.at[6 + q], {"space": mirror}
        )
        for q in range(chunk_count)
    ]
    back_hops = [
        hop(sink.at[q], sink.at[q], send.at[0], recv.at[2 + q], {"space": near})
        for q in range(chunk_count)
    ]

    @pl.when(inner == 0)
    def _():
        for q in range(chunk_count):
            for c in range(2):
                pair_out[q, c] = weighted(q, c).astype(jnp.bfloat16)
            pair_hops[q].start()
        near_copies[1].start()
        pl.semaphore_wait(ready.at[2], 1)
        for q in range(chunk_count // 2):
            back_hops[q].wait_recv()
        tell(4, {"tm": core_peer})
        pl.semaphore_wait(ready.at[4], 1)
        across_copies[0].start()
        mirror_copy.start()
        across_copies[1].start()
        for q in range(chunk_count // 2, chunk_count):
            back_hops[q].wait_recv()

    @pl.when(inner == 1)
    def _():
        for q in range(chunk_count):
            for c in range(2):
                part[q, c] = weighted(q, c)

        first_half = jnp.logical_or(core == 0, me // 2 == 1)

        def forward(q):
            pair_hops[q].wait_recv()
            part[q] = part[q] + pair_in[q].astype(jnp.float32)
            cross_out[q] = part[q].astype(jnp.bfloat16)
            cross_hops[q].start()

        def settle(q):
            cross_hops[q].wait_recv()
            sink[q] = (part[q] + cross_in[q].astype(jnp.float32)).astype(jnp.bfloat16)
            back_hops[q].start()

        for q in range(chunk_count):
            forward(q)
            if q == chunk_count - 1:
                early_copies[1].start()
                pl.when(first_half)(early_copies[2].start)
                pl.when(core == 0)(early_copies[3].start)
            if q > 1:
                settle(q - 2)
        for q in range(chunk_count - 2, chunk_count):
            settle(q)
        pl.when(jnp.logical_not(first_half))(early_copies[2].start)
        pl.when(core == 1)(early_copies[3].start)
        near_copies[1].start()
        pl.semaphore_wait(ready.at[3], 1)

    core_hop = hop(sink, sink_pair, send.at[2], spread_recv.at[0], {"tm": core_peer})
    core_hop.start()
    for q in range(chunk_count):
        rows = pl.ds(q * chunk_rows, chunk_rows)
        low = pl.ds(vector_count + q * chunk_rows, chunk_rows)
        real, imag = sink[q, 0], sink[q, 1]
        sink_big[rows, :vector_count] = real
        sink_big[rows, vector_count:] = -imag
        sink_big[low, :vector_count] = imag
        sink_big[low, vector_count:] = real

    def carried(block):
        stacked = block.reshape(2 * vector_count, block.shape[2])
        product = block_dot(sink_big[...], stacked, 1, 0).astype(jnp.bfloat16)
        return product[:vector_count], product[vector_count:]

    def left_multiply(origin):
        real, imag = carried(tau[origin])
        prop[origin, :, :vector_count] = real
        prop[origin, :, vector_count:] = imag

    def right_multiply(origin):
        product = block_dot(prop[origin], source_big[...], 1, 1)
        res_ref[origin, 0] = product[:, :vector_count]
        res_ref[origin, 1] = product[:, vector_count:]

    @pl.when(inner == 1)
    def _():
        late_copy.wait()
        real, imag = carried(tau_mine[...])
        prop_out[:, :late_count] = real
        prop_out[:, late_count:] = imag
        for copy in prop_copies:
            copy.start()

    core_hop.wait_recv()
    chosen_slot = slice_ref[0] % lax.axis_size("tm")
    picked[...] = jnp.where(chosen_slot == slot, sink[...], sink_pair[...])
    half = pl.ds(core * (chunk_count // 2), chunk_count // 2)
    chip_hop = hop(
        picked.at[half], far.at[half], send.at[2], spread_recv.at[1], {"tm": chip_peer}
    )
    chip_hop.start()

    own_copy.wait()
    left_multiply(me)

    @pl.when(inner == 1)
    def _():
        near_whole.wait_recv()
        left_multiply(near)

    @pl.when(inner == 0)
    def _():
        across_raw.wait_recv()
        left_multiply(across)

    chip_hop.wait_recv()
    forward_hop = hop(
        far.at[half], far.at[half], send.at[2], spread_recv.at[2], {"tm": core_peer}
    )
    forward_hop.start()
    forward_hop.wait_recv()
    chosen = jnp.where(chosen_slot // 2 == slot // 2, picked[...], far[...])
    for q in range(chunk_count):
        rows = pl.ds(q * chunk_rows, chunk_rows)
        low = pl.ds(vector_count + q * chunk_rows, chunk_rows)
        source_big[rows, :vector_count] = chosen[q, 0]
        source_big[rows, vector_count:] = chosen[q, 1]
        source_big[low, :vector_count] = -chosen[q, 1]
        source_big[low, vector_count:] = chosen[q, 0]
    right_multiply(me)

    @pl.when(inner == 0)
    def _():
        right_multiply(across)
        for origin, copy in ((near, near_whole), (mirror, mirror_copy)):
            copy.wait_recv()
            left_multiply(origin)
            right_multiply(origin)

    @pl.when(inner == 1)
    def _():
        right_multiply(near)
        across_whole.wait_recv()
        left_multiply(across)
        right_multiply(across)
        landed = tau.at[mirror, :, :, pl.ds(0, early_count)]
        hop(landed, landed, send.at[1], recv.at[10], {"space": mirror}).wait_recv()
        both = jnp.concatenate(carried(tau[mirror, :, :, :early_count]), axis=1)
        source_early = jnp.concatenate(
            [
                source_big[:, :early_count],
                source_big[:, vector_count : vector_count + early_count],
            ],
            axis=1,
        )
        product = block_dot(both, source_early, 1, 1)
        res_ref[mirror, 0] = product[:, :vector_count]
        res_ref[mirror, 1] = product[:, vector_count:]
        source_late[:late_count] = source_big[:, early_count:vector_count].T
        source_late[late_count:] = source_big[:, vector_count + early_count :].T

        def add_piece(p):
            rows = pieces[p]
            prop_copies[p].wait_recv()
            product = block_dot(prop_in[rows, :], source_late[...], 1, 0)
            res_ref[mirror, 0, rows, :] += product[:, :vector_count]
            res_ref[mirror, 1, rows, :] += product[:, vector_count:]

        for p in range(piece_count - 2):
            add_piece(p)
        for copy in prop_copies[piece_count - 2 :]:
            copy.wait_recv()
        hop(sink, sink, send.at[1], recv.at[0], {"space": near}).wait_send()

    hop(tau, tau, send.at[0], recv.at[0], {"space": near}).wait_send()
    pair = pl.ds(0, 2)
    hop(tau.at[pair], tau.at[pair], send.at[2], recv.at[0], {"space": near}).wait_send()


def finish_kernel(res_ref, prop_ref, source_ref, out_hbm, last, sem):
    group, _, vector_count, _ = res_ref.shape
    last_rows = last.shape[1]
    body_rows = pl.ds(0, vector_count - last_rows)
    tail = pl.ds(vector_count - last_rows, last_rows)
    me = lax.axis_index("space")
    mirror = group - 1 - me
    inner = ((me + 1) // 2) % 2

    def put(source, origin, rows):
        columns = pl.ds(origin * vector_count, vector_count)
        pltpu.make_async_copy(source, out_hbm.at[0, :, rows, columns], sem).start()

    for origin in range(group):
        put(res_ref.at[origin, :, body_rows, :], origin, body_rows)

    for origin in range(group):
        kept = jnp.logical_or(inner == 0, mirror != origin)
        pl.when(kept)(functools.partial(put, res_ref.at[origin, :, tail, :], origin, tail))

    @pl.when(inner == 1)
    def _():
        product = block_dot(prop_ref[tail, :], source_ref[...], 1, 0)
        last[0] = res_ref[mirror, 0, tail, :] + product[:, :vector_count]
        last[1] = res_ref[mirror, 1, tail, :] + product[:, vector_count:]

    for origin in range(group):
        late = jnp.logical_and(inner == 1, mirror == origin)
        pl.when(late)(functools.partial(put, last, origin, tail))

    pltpu.make_async_copy(res_ref, res_ref, sem).wait()


def tail_rows(vector_count):
    last_rows = vector_count // 12 // 32 * 32
    return vector_count - (vector_count - last_rows) // 3 // 32 * 64


def in_hbm(array):
    return pltpu.with_memory_space_constraint(array, pltpu.HBM)


def both_kernels(eigenvectors, perambulator, momenta, ratios, source_slice):
    color_count, site_count, vector_count = eigenvectors.shape[2:]
    group = lax.axis_size("space")
    normalizer = 1.0 / math.sqrt(color_count * site_count * group * vector_count)
    chunk_count = 4
    late_count = 128
    whole = (chunk_count, 2, vector_count // chunk_count, vector_count)
    bf16, f32 = jnp.bfloat16, jnp.float32
    vmem = pl.BlockSpec(memory_space=pltpu.VMEM)
    anywhere = pl.BlockSpec(memory_space=pl.ANY)
    dma = pltpu.SemaphoreType.DMA
    room = 4 * group * 2 * vector_count * vector_count
    results = pl.pallas_call(
        functools.partial(exchange_kernel, normalizer=normalizer),
        out_shape=(
            pltpu.VMEM((group, 2, vector_count, vector_count), f32),
            pltpu.VMEM((vector_count, 2 * late_count), bf16),
            pltpu.VMEM((2 * late_count, 2 * vector_count), bf16),
        ),
        in_specs=[anywhere] * 5,
        out_specs=(vmem, vmem, vmem),
        scratch_shapes=[
            pltpu.SMEM(momenta.shape, jnp.int32),
            pltpu.SMEM(ratios.shape, jnp.int32),
            pltpu.SMEM(source_slice.shape, jnp.int32),
            pltpu.VMEM(eigenvectors.shape[1:], bf16),
            pltpu.VMEM((vector_count, 4 * vector_count), f32),
            pltpu.VMEM((group, 2, vector_count, vector_count), bf16),
            pltpu.VMEM((2, vector_count, late_count), bf16),
            pltpu.VMEM(whole, f32),
            *[pltpu.VMEM(whole, bf16) for _ in range(8)],
            pltpu.VMEM((2 * vector_count, 2 * vector_count), bf16),
            pltpu.VMEM((2 * vector_count, 2 * vector_count), bf16),
            pltpu.VMEM((group, vector_count, 2 * vector_count), bf16),
            pltpu.VMEM((vector_count, 2 * late_count), bf16),
            pltpu.VMEM((site_count, 128), f32),
            pltpu.VMEM((site_count, 128), f32),
            dma((6,)),
            dma((3,)),
            dma((16,)),
            dma((3,)),
            pltpu.SemaphoreType.REGULAR((5,)),
        ],
        compiler_params=pltpu.CompilerParams(
            collective_id=0,
            has_side_effects=True,
            vmem_limit_bytes=VMEM_BYTES - 3 * room,
        ),
        name="exchange",
    )(
        in_hbm(momenta),
        in_hbm(ratios),
        in_hbm(source_slice),
        in_hbm(eigenvectors),
        in_hbm(perambulator),
    )
    return pl.pallas_call(
        finish_kernel,
        out_shape=pltpu.HBM((1, 2, vector_count, group * vector_count), f32),
        in_specs=[vmem, vmem, vmem],
        out_specs=anywhere,
        scratch_shapes=[pltpu.VMEM((2, tail_rows(vector_count), vector_count), f32), dma],
        compiler_params=pltpu.CompilerParams(vmem_limit_bytes=VMEM_BYTES // 2),
        name="finish",
    )(*[pltpu.with_memory_space_constraint(array, pltpu.VMEM) for array in results])


def body(*arrays):
    perambulator = arrays[1]
    group = lax.axis_size("space")
    part_count, order, columns = perambulator.shape[1:]

    def never(*_):
        return jnp.zeros((1, part_count, order // group, columns * group), jnp.float32)

    return lax.cond(lax.axis_index("space") < 2 * group, both_kernels, never, *arrays)


def fits(mesh, eigenvectors, perambulator):
    space, slots = mesh.shape["space"], mesh.shape["tm"]
    vector_count = eigenvectors.shape[4]
    return (
        space == 4
        and slots == 4
        and eigenvectors.shape[0] == slots * mesh.shape["cfg"]
        and perambulator.shape[2] == space * vector_count
        and vector_count % 128 == 0
        and vector_count >= 384
        and eigenvectors.shape[3] % (32 * space) == 0
    )


def solution(mesh):
    placed = (
        P(("cfg", "tm"), None, None, "space", None),
        P(("cfg", "tm"), None, None, "space"),
        P(),
        P(),
        P(),
    )

    def program(eigenvectors, perambulator, momenta, ratios, source_slice):
        chosen = body if fits(mesh, eigenvectors, perambulator) else general_body
        mapped = jax.shard_map(
            chosen,
            mesh=mesh,
            in_specs=placed,
            out_specs=P(("cfg", "tm"), None, "space", None),
            check_vma=False,
        )
        return mapped(eigenvectors, perambulator, momenta, ratios, source_slice)

    return program
```

```python
import functools
import math

import jax
import jax.numpy as jnp
from jax import lax
from jax.experimental import pallas as pl
from jax.experimental.pallas import tpu as pltpu
from jax.sharding import PartitionSpec as P

MESH = pl.DeviceIdType.MESH

LSIDE = 64

VMEM_BYTES = 67043328


def spread(value, axis, source):
    kept = jnp.where(lax.axis_index(axis) == source, value, 0).astype(value.dtype)
    return lax.psum(kept, axis)


def site_phases(momenta, first_site, site_count):
    site_index = first_site + lax.iota(jnp.int32, site_count)
    along_x = site_index % LSIDE
    along_y = site_index // LSIDE % LSIDE
    along_z = site_index // (LSIDE * LSIDE)
    turn_count = (
        momenta[:, 0:1] * along_x[None, :]
        + momenta[:, 1:2] * along_y[None, :]
        + momenta[:, 2:3] * along_z[None, :]
    )
    phase_angle = (turn_count % LSIDE).astype(jnp.float32) * (2.0 * math.pi / LSIDE)
    return (jnp.cos(phase_angle), jnp.sin(phase_angle))


def split_elementals(product, vector_count):
    lead_shape = product.shape[:-2]
    product_grid = product.reshape(lead_shape + (2, vector_count, 2, 2, vector_count))
    real_part = product_grid[..., 0, :, :, 0, :] + product_grid[..., 1, :, :, 1, :]
    imaginary = product_grid[..., 0, :, :, 1, :] - product_grid[..., 1, :, :, 0, :]
    stacked = jnp.stack([real_part, imaginary], axis=-4)
    return jnp.moveaxis(stacked, -2, -4)


def elementals(vectors, cosine, sine_part):
    slab_count, color_count, site_count, vector_count = (
        vectors.shape[0],
        vectors.shape[2],
        vectors.shape[3],
        vectors.shape[4],
    )
    row_count = color_count * site_count
    real_rows = vectors[:, 0].reshape(slab_count, row_count, vector_count)
    imaginary_rows = vectors[:, 1].reshape(slab_count, row_count, vector_count)
    cos_rows = jnp.broadcast_to(cosine[:, None, :], (2, color_count, site_count)).reshape(
        1, 2, row_count, 1
    )
    sin_rows = jnp.broadcast_to(sine_part[:, None, :], (2, color_count, site_count)).reshape(
        1, 2, row_count, 1
    )
    phased_real = (cos_rows * real_rows[:, None] + sin_rows * imaginary_rows[:, None]).astype(
        jnp.bfloat16
    )
    phased_imaginary = (cos_rows * imaginary_rows[:, None] - sin_rows * real_rows[:, None]).astype(
        jnp.bfloat16
    )
    phased = jnp.concatenate([phased_real, phased_imaginary], axis=3)
    phased = jnp.transpose(phased, (0, 2, 1, 3)).reshape(slab_count, row_count, 4 * vector_count)
    plain_vectors = jnp.concatenate([real_rows, imaginary_rows], axis=2)
    product = lax.dot_general(
        plain_vectors, phased, (((1,), (1,)), ((0,), (0,))), preferred_element_type=jnp.float32
    )
    return split_elementals(product, vector_count)


def source_block(chosen):
    real_t = chosen[0].T
    imaginary_t = chosen[1].T
    upper = jnp.concatenate([real_t, -imaginary_t], axis=1)
    lower = jnp.concatenate([imaginary_t, real_t], axis=1)
    return jnp.concatenate([upper, lower], axis=0)


def propagate(sink_matrix, tau):
    vector_count = sink_matrix.shape[1]
    spin_count = tau.shape[1] // vector_count
    column_count = tau.shape[2]
    real_part, imaginary = (sink_matrix[0], sink_matrix[1])
    upper = jnp.concatenate([real_part, -imaginary], axis=1)
    lower = jnp.concatenate([imaginary, real_part], axis=1)
    sink_big = jnp.concatenate([upper, lower], axis=0)
    stacked = jnp.transpose(tau.reshape(2, spin_count, vector_count, column_count), (0, 2, 1, 3))
    stacked = stacked.reshape(2 * vector_count, spin_count * column_count)
    product = jnp.dot(sink_big, stacked, preferred_element_type=jnp.float32)
    product = jnp.transpose(
        product.reshape(2, vector_count, spin_count, column_count), (0, 2, 1, 3)
    )
    return product.reshape(2, spin_count * vector_count, column_count).astype(jnp.bfloat16)


def attach_source(propagated, source_big):
    vector_count = source_big.shape[0] // 2
    row_count = propagated.shape[1]
    spin_count = propagated.shape[2] // vector_count
    stacked = jnp.concatenate(
        [
            propagated[0].reshape(row_count, spin_count, vector_count),
            propagated[1].reshape(row_count, spin_count, vector_count),
        ],
        axis=2,
    )
    product = jnp.dot(
        stacked.reshape(row_count * spin_count, 2 * vector_count),
        source_big,
        preferred_element_type=jnp.float32,
    )
    product = jnp.transpose(product.reshape(row_count, spin_count, 2, vector_count), (2, 0, 1, 3))
    return product.reshape(2, row_count, spin_count * vector_count)


def general_body(eigenvectors, perambulator, momenta, ratios, source_slice):
    slab_count = eigenvectors.shape[0]
    color_count = eigenvectors.shape[2]
    site_count = eigenvectors.shape[3]
    vector_count = eigenvectors.shape[4]
    first_site = lax.axis_index("space") * site_count
    cosine, sine_part = site_phases(momenta, first_site, site_count)
    normalizer = 1.0 / math.sqrt(color_count * site_count * lax.axis_size("space") * vector_count)
    weights = (
        ratios[:, 0].astype(jnp.float32) / ratios[:, 1].astype(jnp.float32) * normalizer
    ).reshape(1, 2, 1, 1, 1)
    parts = elementals(eigenvectors, cosine, sine_part)
    partial_sums = jnp.sum(weights * parts, axis=1, keepdims=True)
    summed = lax.psum(partial_sums, "space")
    sink_matrices = summed[:, 0].astype(jnp.bfloat16)
    global_slice = source_slice[0] % (slab_count * lax.axis_size("tm"))
    local_source = lax.dynamic_index_in_dim(
        sink_matrices, global_slice % slab_count, 0, keepdims=False
    )
    chosen = spread(local_source, "tm", global_slice // slab_count)
    source_big = source_block(chosen)
    propagated = jnp.stack([propagate(sink_matrices[0], perambulator[0])])
    return jnp.stack(
        [
            attach_source(
                lax.all_to_all(propagated, "space", split_axis=2, concat_axis=3, tiled=True)[0],
                source_big,
            )
        ]
    )


def block_dot(left, right, left_dim, right_dim):
    return lax.dot_general(
        left, right, (((left_dim,), (right_dim,)), ((), ())), preferred_element_type=jnp.float32
    )


def exchange_kernel(
    momenta_hbm,
    ratio_hbm,
    slice_hbm,
    eig_hbm,
    tau_hbm,
    res_ref,
    prop_in,
    source_late,
    momenta_ref,
    ratio_ref,
    slice_ref,
    eig,
    acc,
    tau,
    tau_mine,
    part,
    pair_out,
    pair_in,
    cross_out,
    cross_in,
    sink,
    sink_pair,
    picked,
    far,
    sink_big,
    source_big,
    prop,
    prop_out,
    cosines,
    sines,
    own_sem,
    send,
    recv,
    spread_recv,
    ready,
    *,
    normalizer,
):
    vector_count = eig_hbm.shape[4]
    site_count = eig_hbm.shape[3]
    chunk_count, chunk_rows = part.shape[0], part.shape[2]
    color_count = eig.shape[1]
    site_step = site_count // 2
    steps_per_color = site_count // site_step
    step_count = color_count * steps_per_color
    late_count = tau_mine.shape[2]
    early_count = vector_count - late_count
    last_rows = tail_rows(vector_count)
    piece_rows = (vector_count - last_rows) // 3 // 32 * 32
    piece_ends = [piece_rows, 2 * piece_rows, vector_count - last_rows, vector_count]
    pieces = [pl.ds(a, b - a) for a, b in zip([0] + piece_ends, piece_ends) if b > a]
    piece_count = len(pieces)
    me = lax.axis_index("space")
    slot = lax.axis_index("tm")
    near = me + 1 - 2 * (me % 2)
    across = me + 2 - 4 * (me // 2)
    mirror = 3 - me
    inner = ((me + 1) // 2) % 2
    core = slot % 2
    core_peer = slot + 1 - 2 * core
    chip_peer = slot + 2 - 4 * (slot // 2)

    eig_copy = pltpu.make_async_copy(eig_hbm.at[0], eig, own_sem.at[4])
    own_copy = pltpu.make_async_copy(
        tau_hbm.at[0, :, pl.ds(me * vector_count, vector_count), :], tau.at[me], own_sem.at[0]
    )
    late_copy = pltpu.make_async_copy(
        tau_hbm.at[
            0, :, pl.ds(mirror * vector_count, vector_count), pl.ds(early_count, late_count)
        ],
        tau_mine,
        own_sem.at[1],
    )
    scalar_copies = [
        pltpu.make_async_copy(momenta_hbm, momenta_ref, own_sem.at[2]),
        pltpu.make_async_copy(ratio_hbm, ratio_ref, own_sem.at[3]),
        pltpu.make_async_copy(slice_hbm, slice_ref, own_sem.at[5]),
    ]

    barrier = pltpu.get_barrier_semaphore()

    def hello(peer):
        pl.semaphore_signal(barrier, inc=1, device_id=peer, device_id_type=MESH)

    def hop(from_ref, to_ref, send_sem, recv_sem, peer):
        return pltpu.make_async_remote_copy(
            src_ref=from_ref,
            dst_ref=to_ref,
            send_sem=send_sem,
            recv_sem=recv_sem,
            device_id=peer,
            device_id_type=MESH,
        )

    def tau_copy(to, part_of, recv_index):
        return hop(
            tau_hbm.at[0, part_of, pl.ds(to * vector_count, vector_count), :],
            tau.at[me, part_of],
            send.at[0],
            recv.at[recv_index],
            {"space": to},
        )

    near_copies = [tau_copy(near, piece, 0) for piece in range(2)]
    near_whole = tau_copy(near, slice(None), 0)
    across_raw = tau_copy(across, slice(None), 6)
    across_copies = [tau_copy(across, piece, 10) for piece in range(2)]
    across_whole = tau_copy(across, slice(None), 10)
    mirror_copy = tau_copy(mirror, slice(None), 1)
    def early_copy(piece):
        first, count = early_rows[piece]
        return hop(
            tau_hbm.at[
                0, :, pl.ds(mirror * vector_count + first, count), pl.ds(0, early_count)
            ],
            tau.at[me, :, pl.ds(first, count), pl.ds(0, early_count)],
            send.at[1],
            recv.at[1],
            {"space": mirror},
        )

    lead = vector_count // 2 // 32 * 32
    early_ends = [
        lead,
        lead + lead // 4 // 16 * 16,
        lead + lead // 2 // 16 * 16,
        vector_count,
    ]
    early_rows = [(a, b - a) for a, b in zip([0] + early_ends, early_ends)]
    early_copies = [early_copy(piece) for piece in range(4)]
    prop_copies = [
        hop(
            prop_out.at[pieces[p], :],
            prop_in.at[pieces[p], :],
            send.at[1],
            recv.at[11 + p],
            {"space": mirror},
        )
        for p in range(piece_count)
    ]

    def tell(index, peer):
        pl.semaphore_signal(ready.at[index], inc=1, device_id=peer, device_id_type=MESH)

    def phases():
        for copy in scalar_copies:
            copy.wait()
        lanes = cosines.shape[1]
        site = me * site_count + lax.broadcasted_iota(jnp.int32, (site_count, lanes), 0)
        first_lane = lax.broadcasted_iota(jnp.int32, (site_count, lanes), 1) == 0
        shift = LSIDE.bit_length() - 1
        places = (
            jnp.bitwise_and(site, LSIDE - 1),
            jnp.bitwise_and(jnp.right_shift(site, shift), LSIDE - 1),
            jnp.right_shift(site, 2 * shift),
        )
        turn = jnp.zeros_like(site)
        for axis in range(3):
            turn += jnp.where(first_lane, momenta_ref[0, axis], momenta_ref[1, axis]) * places[axis]
        angle = jnp.bitwise_and(turn, LSIDE - 1).astype(jnp.float32) * (2.0 * math.pi / LSIDE)
        cosines[...] = jnp.cos(angle)
        sines[...] = jnp.sin(angle)

    @pl.when(inner == 1)
    def _():
        hello({"space": mirror})
        hello({"space": near})
        pl.semaphore_wait(barrier, 1)
        early_copies[0].start()
        for copy in scalar_copies:
            copy.start()
        eig_copy.start()
        phases()
        pl.semaphore_wait(ready.at[0], 1)
        tell(1, {"space": mirror})
        near_copies[0].start()
        pl.semaphore_wait(ready.at[1], 1)
        across_raw.start()
        tell(2, {"space": near})
        late_copy.start()

    @pl.when(inner == 0)
    def _():
        hello({"tm": core_peer})
        hello({"tm": chip_peer})
        for copy in scalar_copies:
            copy.start()
        eig_copy.start()
        pl.semaphore_wait(barrier, 3)
        tell(0, {"space": near})
        near_copies[0].start()
        tell(0, {"tm": core_peer})
        tell(1, {"tm": chip_peer})
        phases()
        pl.semaphore_wait(ready.at[0], 1)
        pl.semaphore_wait(ready.at[1], 1)
        tell(2, {"space": near})

    own_copy.start()

    acc[...] = jnp.zeros_like(acc)

    eig_copy.wait()

    def accumulate(step, carry):
        color = step // steps_per_color
        rows = pl.ds(pl.multiple_of((step % steps_per_color) * site_step, site_step), site_step)
        plain_real, plain_imag = eig[0, color, rows, :], eig[1, color, rows, :]
        real = plain_real.astype(jnp.float32)
        imag = plain_imag.astype(jnp.float32)
        upper, lower = [], []
        for k in range(2):
            cosine = cosines[rows, k : k + 1]
            sine = sines[rows, k : k + 1]
            turned_real = (cosine * real + sine * imag).astype(jnp.bfloat16)
            turned_imag = (cosine * imag - sine * real).astype(jnp.bfloat16)
            upper += [turned_real, turned_imag]
            lower += [turned_imag, -turned_real]
        left = jnp.concatenate([plain_real, plain_imag], axis=0)
        right = jnp.concatenate(
            [jnp.concatenate(upper, axis=1), jnp.concatenate(lower, axis=1)], axis=0
        )
        acc[...] += block_dot(left, right, 0, 0)
        return carry

    lax.fori_loop(0, step_count, accumulate, 0, unroll=True)

    weights = [
        jnp.full((1, vector_count), ratio_ref[k, 0], jnp.int32).astype(jnp.float32)
        / jnp.full((1, vector_count), ratio_ref[k, 1], jnp.int32).astype(jnp.float32)
        * normalizer
        for k in range(2)
    ]

    def weighted(chunk, c):
        rows = pl.ds(chunk * chunk_rows, chunk_rows)
        return (
            weights[0] * acc[rows, c * vector_count : (c + 1) * vector_count]
            + weights[1] * acc[rows, (2 + c) * vector_count : (3 + c) * vector_count]
        )

    pair_hops = [
        hop(
            pair_out.at[q], pair_in.at[q], send.at[0], recv.at[2 + q], {"space": near}
        )
        for q in range(chunk_count)
    ]
    cross_hops = [
        hop(
            cross_out.at[q], cross_in.at[q], send.at[0], recv.at[6 + q], {"space": mirror}
        )
        for q in range(chunk_count)
    ]
    back_hops = [
        hop(sink.at[q], sink.at[q], send.at[0], recv.at[2 + q], {"space": near})
        for q in range(chunk_count)
    ]

    @pl.when(inner == 0)
    def _():
        for q in range(chunk_count):
            for c in range(2):
                pair_out[q, c] = weighted(q, c).astype(jnp.bfloat16)
            pair_hops[q].start()
        near_copies[1].start()
        pl.semaphore_wait(ready.at[2], 1)
        for q in range(chunk_count // 2):
            back_hops[q].wait_recv()
        tell(3, {"tm": core_peer})
        pl.semaphore_wait(ready.at[3], 1)
        across_copies[0].start()
        mirror_copy.start()
        across_copies[1].start()
        for q in range(chunk_count // 2, chunk_count):
            back_hops[q].wait_recv()

    @pl.when(inner == 1)
    def _():
        for q in range(chunk_count):
            for c in range(2):
                part[q, c] = weighted(q, c)

        first_half = jnp.logical_or(core == 0, me // 2 == 1)

        def forward(q):
            pair_hops[q].wait_recv()
            part[q] = part[q] + pair_in[q].astype(jnp.float32)
            cross_out[q] = part[q].astype(jnp.bfloat16)
            cross_hops[q].start()

        def settle(q):
            cross_hops[q].wait_recv()
            sink[q] = (part[q] + cross_in[q].astype(jnp.float32)).astype(jnp.bfloat16)
            back_hops[q].start()

        for q in range(chunk_count):
            forward(q)
            if q == chunk_count - 1:
                early_copies[1].start()
                pl.when(first_half)(early_copies[2].start)
                pl.when(core == 0)(early_copies[3].start)
            if q > 1:
                settle(q - 2)
        for q in range(chunk_count - 2, chunk_count):
            settle(q)
        pl.when(jnp.logical_not(first_half))(early_copies[2].start)
        pl.when(core == 1)(early_copies[3].start)
        near_copies[1].start()
        pl.semaphore_wait(ready.at[2], 1)

    core_hop = hop(sink, sink_pair, send.at[2], spread_recv.at[0], {"tm": core_peer})
    core_hop.start()
    for q in range(chunk_count):
        rows = pl.ds(q * chunk_rows, chunk_rows)
        low = pl.ds(vector_count + q * chunk_rows, chunk_rows)
        real, imag = sink[q, 0], sink[q, 1]
        sink_big[rows, :vector_count] = real
        sink_big[rows, vector_count:] = -imag
        sink_big[low, :vector_count] = imag
        sink_big[low, vector_count:] = real

    def carried(block):
        stacked = block.reshape(2 * vector_count, block.shape[2])
        product = block_dot(sink_big[...], stacked, 1, 0).astype(jnp.bfloat16)
        return product[:vector_count], product[vector_count:]

    def left_multiply(origin):
        real, imag = carried(tau[origin])
        prop[origin, :, :vector_count] = real
        prop[origin, :, vector_count:] = imag

    def right_multiply(origin):
        product = block_dot(prop[origin], source_big[...], 1, 1)
        res_ref[origin, 0] = product[:, :vector_count]
        res_ref[origin, 1] = product[:, vector_count:]

    @pl.when(inner == 1)
    def _():
        late_copy.wait()
        real, imag = carried(tau_mine[...])
        prop_out[:, :late_count] = real
        prop_out[:, late_count:] = imag
        for copy in prop_copies:
            copy.start()

    core_hop.wait_recv()
    chosen_slot = slice_ref[0] % lax.axis_size("tm")
    picked[...] = jnp.where(chosen_slot == slot, sink[...], sink_pair[...])
    half = pl.ds(core * (chunk_count // 2), chunk_count // 2)
    chip_hop = hop(
        picked.at[half], far.at[half], send.at[2], spread_recv.at[1], {"tm": chip_peer}
    )
    chip_hop.start()

    own_copy.wait()
    left_multiply(me)

    @pl.when(inner == 1)
    def _():
        near_whole.wait_recv()
        left_multiply(near)

    @pl.when(inner == 0)
    def _():
        across_raw.wait_recv()
        left_multiply(across)

    chip_hop.wait_recv()
    forward_hop = hop(
        far.at[half], far.at[half], send.at[2], spread_recv.at[2], {"tm": core_peer}
    )
    forward_hop.start()
    forward_hop.wait_recv()
    chosen = jnp.where(chosen_slot // 2 == slot // 2, picked[...], far[...])
    for q in range(chunk_count):
        rows = pl.ds(q * chunk_rows, chunk_rows)
        low = pl.ds(vector_count + q * chunk_rows, chunk_rows)
        source_big[rows, :vector_count] = chosen[q, 0]
        source_big[rows, vector_count:] = chosen[q, 1]
        source_big[low, :vector_count] = -chosen[q, 1]
        source_big[low, vector_count:] = chosen[q, 0]
    right_multiply(me)

    @pl.when(inner == 0)
    def _():
        right_multiply(across)
        for origin, copy in ((near, near_whole), (mirror, mirror_copy)):
            copy.wait_recv()
            left_multiply(origin)
            right_multiply(origin)

    @pl.when(inner == 1)
    def _():
        right_multiply(near)
        across_whole.wait_recv()
        left_multiply(across)
        right_multiply(across)
        landed = tau.at[mirror, :, :, pl.ds(0, early_count)]
        hop(landed, landed, send.at[1], recv.at[1], {"space": mirror}).wait_recv()
        both = jnp.concatenate(carried(tau[mirror, :, :, :early_count]), axis=1)
        source_early = jnp.concatenate(
            [
                source_big[:, :early_count],
                source_big[:, vector_count : vector_count + early_count],
            ],
            axis=1,
        )
        product = block_dot(both, source_early, 1, 1)
        res_ref[mirror, 0] = product[:, :vector_count]
        res_ref[mirror, 1] = product[:, vector_count:]
        source_late[:late_count] = source_big[:, early_count:vector_count].T
        source_late[late_count:] = source_big[:, vector_count + early_count :].T

        def add_piece(p):
            rows = pieces[p]
            prop_copies[p].wait_recv()
            product = block_dot(prop_in[rows, :], source_late[...], 1, 0)
            res_ref[mirror, 0, rows, :] += product[:, :vector_count]
            res_ref[mirror, 1, rows, :] += product[:, vector_count:]

        for p in range(piece_count - 1):
            add_piece(p)
        prop_copies[-1].wait_recv()
        hop(sink, sink, send.at[1], recv.at[0], {"space": near}).wait_send()

    hop(tau, tau, send.at[0], recv.at[0], {"space": near}).wait_send()
    pair = pl.ds(0, 2)
    hop(tau.at[pair], tau.at[pair], send.at[2], recv.at[0], {"space": near}).wait_send()


def finish_kernel(res_ref, prop_ref, source_ref, out_hbm, last, sem):
    group, _, vector_count, _ = res_ref.shape
    last_rows = last.shape[1]
    body_rows = pl.ds(0, vector_count - last_rows)
    tail = pl.ds(vector_count - last_rows, last_rows)
    me = lax.axis_index("space")
    mirror = group - 1 - me
    inner = ((me + 1) // 2) % 2

    def put(source, origin, rows):
        columns = pl.ds(origin * vector_count, vector_count)
        pltpu.make_async_copy(source, out_hbm.at[0, :, rows, columns], sem).start()

    for origin in range(group):
        put(res_ref.at[origin, :, body_rows, :], origin, body_rows)

    @pl.when(inner == 1)
    def _():
        product = block_dot(prop_ref[tail, :], source_ref[...], 1, 0)
        last[0] = res_ref[mirror, 0, tail, :] + product[:, :vector_count]
        last[1] = res_ref[mirror, 1, tail, :] + product[:, vector_count:]

    for origin in range(group):
        late = jnp.logical_and(inner == 1, mirror == origin)
        pl.when(late)(functools.partial(put, last, origin, tail))
        pl.when(jnp.logical_not(late))(
            functools.partial(put, res_ref.at[origin, :, tail, :], origin, tail)
        )
    pltpu.make_async_copy(res_ref, res_ref, sem).wait()


def tail_rows(vector_count):
    return vector_count // 12 // 32 * 32


def in_hbm(array):
    return pltpu.with_memory_space_constraint(array, pltpu.HBM)


def both_kernels(eigenvectors, perambulator, momenta, ratios, source_slice):
    color_count, site_count, vector_count = eigenvectors.shape[2:]
    group = lax.axis_size("space")
    normalizer = 1.0 / math.sqrt(color_count * site_count * group * vector_count)
    chunk_count = 4
    late_count = 128
    whole = (chunk_count, 2, vector_count // chunk_count, vector_count)
    bf16, f32 = jnp.bfloat16, jnp.float32
    vmem = pl.BlockSpec(memory_space=pltpu.VMEM)
    anywhere = pl.BlockSpec(memory_space=pl.ANY)
    dma = pltpu.SemaphoreType.DMA
    room = 4 * group * 2 * vector_count * vector_count
    results = pl.pallas_call(
        functools.partial(exchange_kernel, normalizer=normalizer),
        out_shape=(
            pltpu.VMEM((group, 2, vector_count, vector_count), f32),
            pltpu.VMEM((vector_count, 2 * late_count), bf16),
            pltpu.VMEM((2 * late_count, 2 * vector_count), bf16),
        ),
        in_specs=[anywhere] * 5,
        out_specs=(vmem, vmem, vmem),
        scratch_shapes=[
            pltpu.SMEM(momenta.shape, jnp.int32),
            pltpu.SMEM(ratios.shape, jnp.int32),
            pltpu.SMEM(source_slice.shape, jnp.int32),
            pltpu.VMEM(eigenvectors.shape[1:], bf16),
            pltpu.VMEM((vector_count, 4 * vector_count), f32),
            pltpu.VMEM((group, 2, vector_count, vector_count), bf16),
            pltpu.VMEM((2, vector_count, late_count), bf16),
            pltpu.VMEM(whole, f32),
            *[pltpu.VMEM(whole, bf16) for _ in range(8)],
            pltpu.VMEM((2 * vector_count, 2 * vector_count), bf16),
            pltpu.VMEM((2 * vector_count, 2 * vector_count), bf16),
            pltpu.VMEM((group, vector_count, 2 * vector_count), bf16),
            pltpu.VMEM((vector_count, 2 * late_count), bf16),
            pltpu.VMEM((site_count, 128), f32),
            pltpu.VMEM((site_count, 128), f32),
            dma((6,)),
            dma((3,)),
            dma((15,)),
            dma((3,)),
            pltpu.SemaphoreType.REGULAR((4,)),
        ],
        compiler_params=pltpu.CompilerParams(
            collective_id=0,
            has_side_effects=True,
            vmem_limit_bytes=VMEM_BYTES - 3 * room,
        ),
        name="exchange",
    )(
        in_hbm(momenta),
        in_hbm(ratios),
        in_hbm(source_slice),
        in_hbm(eigenvectors),
        in_hbm(perambulator),
    )
    return pl.pallas_call(
        finish_kernel,
        out_shape=pltpu.HBM((1, 2, vector_count, group * vector_count), f32),
        in_specs=[vmem, vmem, vmem],
        out_specs=anywhere,
        scratch_shapes=[pltpu.VMEM((2, tail_rows(vector_count), vector_count), f32), dma],
        compiler_params=pltpu.CompilerParams(vmem_limit_bytes=VMEM_BYTES // 2),
        name="finish",
    )(*[pltpu.with_memory_space_constraint(array, pltpu.VMEM) for array in results])


def body(*arrays):
    perambulator = arrays[1]
    group = lax.axis_size("space")
    part_count, order, columns = perambulator.shape[1:]

    def never(*_):
        return jnp.zeros((1, part_count, order // group, columns * group), jnp.float32)

    return lax.cond(lax.axis_index("space") < 2 * group, both_kernels, never, *arrays)


def fits(mesh, eigenvectors, perambulator):
    space, slots = mesh.shape["space"], mesh.shape["tm"]
    vector_count = eigenvectors.shape[4]
    return (
        space == 4
        and slots == 4
        and eigenvectors.shape[0] == slots * mesh.shape["cfg"]
        and perambulator.shape[2] == space * vector_count
        and vector_count % 128 == 0
        and vector_count >= 384
        and eigenvectors.shape[3] % (32 * space) == 0
    )


def solution(mesh):
    placed = (
        P(("cfg", "tm"), None, None, "space", None),
        P(("cfg", "tm"), None, None, "space"),
        P(),
        P(),
        P(),
    )

    def program(eigenvectors, perambulator, momenta, ratios, source_slice):
        chosen = body if fits(mesh, eigenvectors, perambulator) else general_body
        mapped = jax.shard_map(
            chosen,
            mesh=mesh,
            in_specs=placed,
            out_specs=P(("cfg", "tm"), None, "space", None),
            check_vma=False,
        )
        return mapped(eigenvectors, perambulator, momenta, ratios, source_slice)

    return program
```
